32 devices in a mesh: pairs: 8 (over z, y), win: 4 (over x, core).
Axes of the slice: x: 2, y: 2, z: 4, core: 2. Of those that a mesh axis runs over, the one named last changes fastest.
Arguments:
- traces: bfloat16 [128, 128, 4096], P('win', 'pairs'), may hold values from -16 to 16, as said below
- taps: float32 [129], replicated, may hold values from -0.5 to 0.5
- neighbours: int32 [128, 64], P('pairs'), may hold values from 0 to 127, as said below
- valid: int32 [128, 64], P('pairs'), may hold values 0 or 1
Outputs:
- stacks: float32 [128, 64, 1024], P('pairs', 'win')
The draws below stay inside these ranges and needn't reach their ends.
Inputs may be any that keep to these rules, and one draw needn't show every extreme that they name: `neighbours`: every listed neighbour of a station of tile t (stations t * 16 to (t + 1) * 16 - 1) lies in tile t - 1, t or t + 1. `traces`: Station-wise amplitudes differ between stations.
All inputs are finite; a program needn't handle non-finite values. No bound on the sum of `valid` on one device may be relied on, other than what follows from the above.
Results may differ from the reference program's by a relative error of at most 0.0014.
Values may be sent and summed in bfloat16 or wider, within the bound.
No kernel may reach another device: no remote copies, remote signals or barrier semaphores. Data moves between devices by JAX's collectives and lax.ppermute only.
A program may use at most 128 MiB of HBM per device.

```python
import math
import jax
import jax.numpy as jnp
from jax import lax

NODE_DEV = 16
SAMPLES = 4096
BINS = 512
BAND = 64
LOW_BIN = 64
LAGS = 1024
TAPS = 129
NBR = 64
NODES = 128
WINDOWS = 128


def draw_traces(key, part):
    key_scale, key_base = jax.random.split(key, 2)
    scaling = jnp.exp(jax.random.uniform(key_scale, (1, NODES, 1), jnp.float32, math.log(0.3), math.log(3.0)))
    values = scaling * jnp.clip(jax.random.normal(key_base, (WINDOWS, NODES, SAMPLES), jnp.float32), -4.0, 4.0)
    return values.astype(jnp.bfloat16)


def draw_neighbours(key, part):
    key_tile, key_member = jax.random.split(key, 2)
    tiles = jnp.arange(NODES, dtype=jnp.int32) // NODE_DEV
    shifts = jax.random.randint(key_tile, (NODES, NBR), -1, 2, dtype=jnp.int32)
    chosen = jnp.clip(tiles[:, None] + shifts, 0, NODES // NODE_DEV - 1)
    members = jax.random.randint(key_member, (NODES, NBR), 0, NODE_DEV, dtype=jnp.int32)
    node_ids = chosen * NODE_DEV + members
    node_ids = node_ids.at[0, 0].set(0).at[NODES - 1, 0].set(NODES - 1)
    return node_ids.astype(jnp.int32)


def plant(drawn, stream_key, least, high):
    dims = drawn.shape
    spot = [jax.random.randint(jax.random.fold_in(stream_key, axis), (), 0, dims[axis]) for axis in range(len(dims))]
    drawn = drawn.at[tuple(spot)].set(least)
    longest = dims.index(max(dims))
    spot[longest] = (spot[longest] + 1) % dims[longest]
    return drawn.at[tuple(spot)].set(high)


def gaussian(stream_key, dims, scale, bound, held_as=jnp.bfloat16):
    drawn = scale * jax.random.normal(stream_key, dims, jnp.float32)
    return jnp.clip(drawn, min=-bound, max=bound).astype(held_as)


def setup_inputs(seed: int = 0) -> dict:
    streams_of = jax.random.split(jax.random.key(seed), 5)
    return {
        "traces": draw_traces(jax.random.fold_in(streams_of[4], 71), 0),
        "taps": gaussian(streams_of[1], (TAPS,), TAPS ** -0.5, 0.5, jnp.float32),
        "neighbours": draw_neighbours(jax.random.fold_in(streams_of[4], 71), 0),
        "valid": plant((jax.random.randint(streams_of[3], (NODES, NBR), 0, 4) < 3).astype(jnp.int32), jax.random.fold_in(streams_of[3], 1), 0, 1),
    }


epsilon = 1e-06

def phase_angles(times, frequency, samples):
    phases = times[:, None] * frequency[None, :] % samples
    return phases.astype(jnp.float32) * (2.0 * math.pi / samples)

def whiten(raw_rows, resp_re, resp_im):
    bins = raw_rows.shape[1] // 2
    real_part = raw_rows[:, :bins].reshape(-1, bins // BAND, BAND)
    imag_part = raw_rows[:, bins:].reshape(-1, bins // BAND, BAND)
    scaling = lax.rsqrt(lax.optimization_barrier(jnp.mean(real_part * real_part + imag_part * imag_part, -1, keepdims=True)) + epsilon)
    real_white = (real_part * scaling).reshape(-1, bins)
    imag_white = (imag_part * scaling).reshape(-1, bins)
    out_real = real_white * resp_re - imag_white * resp_im
    out_imag = real_white * resp_im + imag_white * resp_re
    return jnp.concatenate([out_real, out_imag], 1).astype(jnp.bfloat16)

def cross_stack(own_node, partner, mask_row):
    bins = own_node.shape[-1] // 2
    a_real = own_node[:, None, :bins].astype(jnp.float32)
    a_imag = own_node[:, None, bins:].astype(jnp.float32)
    b_real = partner[:, :, :bins].astype(jnp.float32)
    b_imag = partner[:, :, bins:].astype(jnp.float32)
    real_part = lax.optimization_barrier(jnp.sum(a_real * b_real + a_imag * b_imag, 0))
    imag_part = lax.optimization_barrier(jnp.sum(a_imag * b_real - a_real * b_imag, 0))
    return jnp.concatenate([real_part, imag_part], 1) * mask_row.astype(jnp.float32)[:, None]

def inverse_lags(stack):
    bins = stack.shape[-1] // 2
    frequency = LOW_BIN + jnp.arange(bins, dtype=jnp.int32)
    lag_index = ((jnp.arange(LAGS, dtype=jnp.int32) - LAGS // 2) % SAMPLES).astype(jnp.int32)
    angles = phase_angles(frequency, lag_index, SAMPLES)
    flat_rows = stack.reshape(-1, 2 * bins)
    result = jnp.dot(flat_rows[:, :bins], jnp.cos(angles), precision=lax.Precision.HIGHEST)
    result = result - jnp.dot(flat_rows[:, bins:], jnp.sin(angles), precision=lax.Precision.HIGHEST)
    return result.reshape(stack.shape[:-1] + (LAGS,))

def reference(traces, taps, neighbours, valid):
    frequency = LOW_BIN + jnp.arange(BINS, dtype=jnp.int32)
    angles = phase_angles(jnp.arange(SAMPLES, dtype=jnp.int32), frequency, SAMPLES)
    forward = jnp.concatenate([jnp.cos(angles), -jnp.sin(angles)], 1).astype(jnp.bfloat16)
    forward = lax.optimization_barrier(forward).astype(jnp.float32)
    tap_angles = phase_angles(jnp.arange(TAPS, dtype=jnp.int32), frequency, SAMPLES)
    resp_re = jnp.dot(taps, jnp.cos(tap_angles), precision=lax.Precision.HIGHEST)
    resp_im = -jnp.dot(taps, jnp.sin(tap_angles), precision=lax.Precision.HIGHEST)

    def transform(window):
        raw_rows = jnp.dot(window.astype(jnp.float32), forward, precision=lax.Precision.HIGHEST)
        return whiten(raw_rows, resp_re, resp_im)
    spectra = lax.map(transform, traces)

    def pair_stack(items):
        own_node, node_ids, mask_row = items
        partner = jnp.take(spectra, node_ids, axis=1)
        return cross_stack(own_node, partner, mask_row)
    stack = lax.map(pair_stack, (jnp.moveaxis(spectra, 1, 0), neighbours, valid))
    return inverse_lags(stack) * (1.0 / math.sqrt(BINS * WINDOWS))
```

```python
import functools
import math

import jax
import jax.numpy as jnp
import numpy as np
from jax import lax
from jax.experimental import pallas as pl
from jax.experimental.pallas import tpu as pltpu
from jax.sharding import PartitionSpec as P

SAMPLES = 4096
BINS = 512
BAND = 64
LOW_BIN = 64
LAGS = 1024
TAPS = 129
LANES = 2 * BAND
EPSILON = 1e-06
STEP = 64
CHUNK = 512
VMEM_LIMIT = 60 * 1024 * 1024


def unit_circle(products):
    angles = (products % SAMPLES).astype(np.float64) * (2.0 * math.pi / SAMPLES)
    return np.cos(angles).astype(np.float32), (-np.sin(angles)).astype(np.float32)


def banded(first, second):
    rows = first.shape[0]
    parts = [a.reshape(rows, BINS // BAND, 1, BAND) for a in (first, second)]
    return np.concatenate(parts, 2).reshape(rows, 2 * BINS)


def forward_tables():
    bins = LOW_BIN + np.arange(BINS, dtype=np.int64)
    cos, msin = unit_circle(np.arange(TAPS, dtype=np.int64)[:, None] * bins[None, :])
    fine = banded(cos, msin)
    starts = np.arange(0, SAMPLES, STEP, dtype=np.int64)
    cos, msin = unit_circle(starts[:, None] * bins[None, :])
    return fine, banded(cos, cos), banded(-msin, msin)


def lag_tables(parts):
    lags = np.arange(LAGS, dtype=np.int64) - LAGS // 2
    cos, msin = unit_circle(np.arange(BAND, dtype=np.int64)[:, None] * lags[None, :])
    first = LOW_BIN + BAND * np.arange(parts, dtype=np.int64)
    cos0, msin0 = unit_circle(first[:, None] * lags[None, :])
    return cos, msin, cos0, msin0


def spectra_kernel(x_ref, taps_ref, fine_ref, turn_c_ref, turn_s_ref, out_ref, total, swapped, table):
    step = pl.program_id(0)

    @pl.when(step == 0)
    def _():
        for band in range(BINS // BAND):
            cols = pl.ds(band * LANES, LANES)
            swapped[:, cols] = pltpu.roll(fine_ref[0:STEP, cols], BAND, 1)

    for block in range(CHUNK // STEP):
        row = pl.ds(step * (CHUNK // STEP) + block, 1)
        turned = fine_ref[0:STEP, :] * turn_c_ref[row, :] + swapped[...] * turn_s_ref[row, :]
        table[block * STEP : (block + 1) * STEP, :] = turned.astype(jnp.bfloat16)
    product = jnp.dot(x_ref[...], table[...], preferred_element_type=jnp.float32)

    @pl.when(step == 0)
    def _():
        total[...] = product

    @pl.when(step > 0)
    def _():
        total[...] += product

    @pl.when(step == pl.num_programs(0) - 1)
    def _():
        response = jnp.dot(
            taps_ref[:, 0:128],
            fine_ref[0:128, :],
            precision=lax.Precision.HIGHEST,
            preferred_element_type=jnp.float32,
        )
        response = response + taps_ref[:, 128:129] * fine_ref[128:129, :]
        low = lax.broadcasted_iota(jnp.int32, (1, LANES), 1) < BAND
        for band in range(BINS // BAND):
            here = response[:, band * LANES : (band + 1) * LANES]
            other = pltpu.roll(jnp.broadcast_to(here, (8, LANES)), BAND, 1)[0:1, :]
            same = jnp.where(low, here, other)
            cross = jnp.where(low, -other, here)
            raw = total[:, band * LANES : (band + 1) * LANES]
            power = jnp.sum(raw * raw, 1, keepdims=True) * (1.0 / BAND)
            white = raw * lax.rsqrt(power + EPSILON)
            turned = white * same + pltpu.roll(white, BAND, 1) * cross
            out_ref[band] = turned.astype(jnp.bfloat16)


def own_spectra(rows, taps):
    fine, turn_c, turn_s = (jnp.asarray(t) for t in forward_tables())
    count = rows.shape[0]
    bands = BINS // BAND
    fixed = lambda shape: pl.BlockSpec(shape, lambda i: (0,) * len(shape))
    return pl.pallas_call(
        spectra_kernel,
        grid=(SAMPLES // CHUNK,),
        in_specs=[
            pl.BlockSpec((count, CHUNK), lambda i: (0, i)),
            fixed(taps.shape),
            fixed(fine.shape),
            fixed(turn_c.shape),
            fixed(turn_s.shape),
        ],
        out_specs=fixed((bands, count, LANES)),
        out_shape=jax.ShapeDtypeStruct((bands, count, LANES), jnp.bfloat16),
        scratch_shapes=[
            pltpu.VMEM((count, 2 * BINS), jnp.float32),
            pltpu.VMEM((STEP, 2 * BINS), jnp.float32),
            pltpu.VMEM((CHUNK, 2 * BINS), jnp.bfloat16),
        ],
        compiler_params=pltpu.CompilerParams(vmem_limit_bytes=VMEM_LIMIT),
        name="own_spectra",
    )(rows, taps, fine, turn_c, turn_s)


def lag_table_kernel(cos_ref, msin_ref, cos0_ref, msin0_ref, high_ref, low_ref, *, factor):
    part = pl.program_id(0)
    c0 = cos0_ref[pl.ds(part, 1), :] * factor
    s0 = msin0_ref[pl.ds(part, 1), :] * factor
    cos, msin = cos_ref[...], msin_ref[...]
    for half, values in ((0, cos * c0 - msin * s0), (1, cos * s0 + msin * c0)):
        high = values.astype(jnp.bfloat16)
        rows = pl.ds(half * BAND, BAND)
        high_ref[0, rows, :] = high
        low_ref[0, rows, :] = (values - high.astype(jnp.float32)).astype(jnp.bfloat16)


def make_lag_tables(parts, factor):
    tables = [jnp.asarray(t) for t in lag_tables(parts)]
    shape = jax.ShapeDtypeStruct((parts, LANES, LAGS), jnp.bfloat16)
    block = pl.BlockSpec((1, LANES, LAGS), lambda i: (i, 0, 0))
    return pl.pallas_call(
        functools.partial(lag_table_kernel, factor=factor),
        grid=(parts,),
        in_specs=[pl.BlockSpec(t.shape, lambda i: (0, 0)) for t in tables],
        out_specs=[block, block],
        out_shape=[shape, shape],
        name="lag_tables",
    )(*tables)


def widen(src_ref, dst_ref, dst_tile, nodes, swap_ref):
    groups, rows = src_ref.shape[0], src_ref.shape[1]
    for group in range(groups):
        values = src_ref[group].astype(jnp.float32)
        dst_ref[dst_tile, pl.ds(group * rows, rows), :] = values
        if swap_ref is not None:
            swap_ref[dst_tile, pl.ds(group * rows, rows), :] = pltpu.roll(values, BAND, 1)


def correlate(a_ref, a_tile, b_ref, s_ref, b_tile, nodes, windows, store):
    group = 4
    eights = nodes // 8

    def nodes_block(index, _):
        first = index * group

        def window(w, totals):
            row = w * nodes
            b = [b_ref[b_tile, pl.ds(pl.multiple_of(row + 8 * v, 8), 8), :] for v in range(eights)]
            s = [s_ref[b_tile, pl.ds(pl.multiple_of(row + 8 * v, 8), 8), :] for v in range(eights)]
            out = []
            for i in range(group):
                a = a_ref[a_tile, pl.ds(row + first + i, 8, stride=0), :]
                for v in range(eights):
                    direct, crossed = totals[i * eights + v]
                    out.append((direct + a * b[v], crossed + a * s[v]))
            return tuple(out)

        zero = jnp.zeros((8, LANES), jnp.float32)
        totals = lax.fori_loop(0, windows, window, ((zero, zero),) * (group * eights), unroll=4)
        low = lax.broadcasted_iota(jnp.int32, (8, LANES), 1) < BAND
        for i in range(group):
            for v in range(eights):
                direct, crossed = totals[i * eights + v]
                real = direct + pltpu.roll(direct, BAND, 1)
                imag = crossed - pltpu.roll(crossed, BAND, 1)
                store(first + i, v, jnp.where(low, real, imag))
        return 0

    lax.fori_loop(0, nodes // group, nodes_block, 0)


def own_cross_kernel(x_ref, out_ref, wide, swap, *, nodes, windows):
    groups = x_ref.shape[0] // 2
    for tile in range(2):
        widen(x_ref.at[pl.ds(tile * groups, groups)], wide, tile, nodes, swap)
    for a_tile, b_tile in ((0, 0), (0, 1), (1, 1)):
        def store(node, v, values, a_tile=a_tile, b_tile=b_tile):
            row = ((a_tile * nodes + node) * 2 + b_tile) * nodes + 8 * v
            out_ref[pl.ds(pl.multiple_of(row, 8), 8), :] = values

        correlate(wide, a_tile, wide, swap, b_tile, nodes, windows, store)
    sign = jnp.where(lax.broadcasted_iota(jnp.int32, (1, LANES), 1) < BAND, 1.0, -1.0)
    for node in range(nodes):
        mirrored = out_ref[pl.ds(nodes + node, nodes, stride=2 * nodes), :]
        out_ref[pl.ds((nodes + node) * 2 * nodes, nodes), :] = mirrored * sign


def own_cross(received, nodes, windows):
    rows = windows * nodes
    return pl.pallas_call(
        functools.partial(own_cross_kernel, nodes=nodes, windows=windows),
        out_shape=jax.ShapeDtypeStruct((4 * nodes * nodes, LANES), jnp.float32),
        in_specs=[pl.BlockSpec(memory_space=pltpu.VMEM)],
        out_specs=pl.BlockSpec(memory_space=pltpu.VMEM),
        scratch_shapes=[pltpu.VMEM((2, rows, LANES), jnp.float32)] * 2,
        compiler_params=pltpu.CompilerParams(vmem_limit_bytes=VMEM_LIMIT),
        cost_estimate=pl.CostEstimate(
            flops=2 * 8 * nodes * nodes * windows * BAND, bytes_accessed=8 * rows * LANES, transcendentals=0
        ),
        name="own_cross",
    )(received)


def edge_select_kernel(odd_ref, x_ref, even_ref, odd_halo_ref, own_ref, select_ref, out_ref, wide, halo, swap, edge, *, nodes, windows):
    groups = x_ref.shape[0] // 2
    for tile in range(2):
        widen(x_ref.at[pl.ds(tile * groups, groups)], wide, tile, nodes, None)
    widen(even_ref, halo, 0, nodes, swap)
    widen(odd_halo_ref, halo, 1, nodes, swap)
    odd = odd_ref[0]
    for which in range(2):
        tile = (1 - odd) if which == 0 else odd

        def store(node, v, values, tile=tile):
            row = (tile * nodes + node) * nodes + 8 * v
            edge[pl.ds(pl.multiple_of(row, 8), 8), :] = values

        correlate(wide, tile, halo, swap, which, nodes, windows, store)
    slots = out_ref.shape[2]
    destinations = out_ref.shape[0] // 2

    def one(index, _):
        own = own_ref[pl.ds(pl.multiple_of(index * 2 * nodes, 8), 2 * nodes), :]
        far = edge[pl.ds(pl.multiple_of(index * nodes, 8), nodes), :]
        values = jnp.concatenate([own, far], 0)
        high = values.astype(jnp.bfloat16)
        low = (values - high.astype(jnp.float32)).astype(jnp.bfloat16)
        picked = jnp.dot(
            select_ref[index], jnp.concatenate([high, low], 0), preferred_element_type=jnp.float32
        )
        tile, node = index // nodes, index % nodes
        for d in range(destinations):
            out_ref[tile * destinations + d, node] = picked[d * slots : (d + 1) * slots, :]
        return 0

    lax.fori_loop(0, 2 * nodes, one, 0)


def edge_select(odd, received, halo_a, halo_b, own, select, nodes, windows, parts):
    rows = windows * nodes
    slots = select.shape[1] // (parts // 2)
    vmem = pl.BlockSpec(memory_space=pltpu.VMEM)
    return pl.pallas_call(
        functools.partial(edge_select_kernel, nodes=nodes, windows=windows),
        out_shape=jax.ShapeDtypeStruct((parts, nodes, slots, LANES), jnp.float32),
        in_specs=[pl.BlockSpec(memory_space=pltpu.SMEM)] + [vmem] * 5,
        out_specs=vmem,
        scratch_shapes=[
            pltpu.VMEM((2, rows, LANES), jnp.float32),
            pltpu.VMEM((2, rows, LANES), jnp.float32),
            pltpu.VMEM((2, rows, LANES), jnp.float32),
            pltpu.VMEM((2 * nodes * nodes, LANES), jnp.float32),
        ],
        compiler_params=pltpu.CompilerParams(vmem_limit_bytes=VMEM_LIMIT),
        name="edge_select",
    )(odd, received, halo_a, halo_b, own, select)


def inverse_kernel(x_ref, high_ref, low_ref, out_ref):
    parts, nodes, slots = x_ref.shape[0], x_ref.shape[1], x_ref.shape[2]
    total = None
    for part in range(parts):
        values = x_ref[part].reshape(nodes * slots, LANES)
        high = values.astype(jnp.bfloat16)
        low = (values - high.astype(jnp.float32)).astype(jnp.bfloat16)
        dot = functools.partial(jnp.dot, preferred_element_type=jnp.float32)
        term = dot(high, high_ref[part]) + (dot(low, high_ref[part]) + dot(high, low_ref[part]))
        total = term if total is None else total + term
    out_ref[...] = total.reshape(out_ref.shape)


def inverse(stack, high, low):
    parts, nodes, slots, _ = stack.shape
    block = 256
    table = pl.BlockSpec((parts, LANES, block), lambda i: (0, 0, i))
    return pl.pallas_call(
        inverse_kernel,
        grid=(LAGS // block,),
        in_specs=[pl.BlockSpec(stack.shape, lambda i: (0, 0, 0, 0)), table, table],
        out_specs=pl.BlockSpec((nodes, slots, block), lambda i: (0, 0, i)),
        out_shape=jax.ShapeDtypeStruct((nodes, slots, LAGS), jnp.float32),
        compiler_params=pltpu.CompilerParams(vmem_limit_bytes=VMEM_LIMIT),
        name="inverse",
    )(stack, high, low)


def per_device(traces, taps, neighbours, valid, *, pairs, wins):
    windows, nodes, samples = traces.shape
    parts = 2 * wins
    place = lax.axis_index("pairs")
    parity = place % 2
    both = ("pairs", "win")
    groups = [[p * wins + w for p in (k, k + 1) for w in range(wins)] for k in range(0, pairs, 2)]
    exchange = functools.partial(
        lax.all_to_all, axis_name=both, split_axis=0, concat_axis=0, tiled=True, axis_index_groups=groups
    )

    local = neighbours - (place - 1) * nodes
    local = jnp.where(parity == 0, (local + 2 * nodes) % (3 * nodes), local)
    code = jnp.where(valid != 0, local, -1)
    other = lax.ppermute(code, "pairs", [(i, i ^ 1) for i in range(pairs)])
    codes = jnp.where(parity == 0, jnp.concatenate([code, other], 0), jnp.concatenate([other, code], 0))
    columns = jnp.arange(6 * nodes, dtype=jnp.int32) % (3 * nodes)
    select = (codes[:, :, None] == columns[None, None, :]).astype(jnp.bfloat16)

    factor = 1.0 / math.sqrt(BINS * windows * wins)
    high, low = make_lag_tables(parts, factor)

    spectra = own_spectra(traces.reshape(windows * nodes, samples), taps.reshape(1, TAPS))
    received = exchange(spectra)

    odd = (place // 2) % 2
    swap_a = [(i, i ^ 2) for i in range(pairs) if (i ^ 2) < pairs]
    swap_b = [(i, j) for i in range(pairs) for j in [((i - 2) ^ 2) + 2] if 2 <= i and j < pairs]
    send_a = lax.dynamic_slice_in_dim(received, (1 - odd) * wins, wins, 0)
    send_b = lax.dynamic_slice_in_dim(received, odd * wins, wins, 0)
    halo_a = lax.ppermute(send_a, "pairs", swap_a)
    halo_b = lax.ppermute(send_b, "pairs", swap_b)

    own = own_cross(received, nodes, windows * wins)
    stack = edge_select(odd.reshape(1), received, halo_a, halo_b, own, select, nodes, windows * wins, parts)
    return inverse(exchange(stack), high, low)


def solution(mesh):
    placed = (P("win", "pairs", None), P(), P("pairs", None), P("pairs", None))
    body = functools.partial(per_device, pairs=mesh.shape["pairs"], wins=mesh.shape["win"])
    return jax.shard_map(
        body, mesh=mesh, in_specs=placed, out_specs=P("pairs", "win", None), check_vma=False
    )
```

```python
import functools
import math

import jax
import jax.numpy as jnp
import numpy as np
from jax import lax
from jax.experimental import pallas as pl
from jax.experimental.pallas import tpu as pltpu
from jax.sharding import PartitionSpec as P

SAMPLES = 4096
BINS = 512
BAND = 64
LOW_BIN = 64
LAGS = 1024
TAPS = 129
LANES = 2 * BAND
EPSILON = 1e-06
STEP = 64
CHUNK = 512
MIB = 1024 * 1024


def unit_circle(products):
    angles = (products % SAMPLES).astype(np.float64) * (2.0 * math.pi / SAMPLES)
    return np.cos(angles).astype(np.float32), (-np.sin(angles)).astype(np.float32)


def banded(first, second):
    rows = first.shape[0]
    parts = [a.reshape(rows, BINS // BAND, 1, BAND) for a in (first, second)]
    return np.concatenate(parts, 2).reshape(rows, 2 * BINS)


def forward_tables():
    bins = LOW_BIN + np.arange(BINS, dtype=np.int64)
    cos, msin = unit_circle(np.arange(TAPS, dtype=np.int64)[:, None] * bins[None, :])
    fine = banded(cos, msin)
    starts = np.arange(0, SAMPLES, STEP, dtype=np.int64)
    cos, msin = unit_circle(starts[:, None] * bins[None, :])
    return fine, banded(cos, cos), banded(-msin, msin)


def lag_tables(parts):
    lags = np.arange(LAGS, dtype=np.int64) - LAGS // 2
    cos, msin = unit_circle(np.arange(BAND, dtype=np.int64)[:, None] * lags[None, :])
    first = LOW_BIN + BAND * np.arange(parts, dtype=np.int64)
    cos0, msin0 = unit_circle(first[:, None] * lags[None, :])
    return cos, msin, cos0, msin0


def spectra_kernel(x_ref, taps_ref, fine_ref, turn_c_ref, turn_s_ref, out_ref, total, swapped, table):
    step = pl.program_id(0)
    nodes = out_ref.shape[1]

    @pl.when(step == 0)
    def _():
        for band in range(BINS // BAND):
            cols = pl.ds(band * LANES, LANES)
            swapped[:, cols] = pltpu.roll(fine_ref[0:STEP, cols], BAND, 1)

    for block in range(CHUNK // STEP):
        row = pl.ds(step * (CHUNK // STEP) + block, 1)
        turned = fine_ref[0:STEP, :] * turn_c_ref[row, :] + swapped[...] * turn_s_ref[row, :]
        table[block * STEP : (block + 1) * STEP, :] = turned.astype(jnp.bfloat16)
    product = jnp.dot(x_ref[...], table[...], preferred_element_type=jnp.float32)

    for band in range(BINS // BAND):
        here = product[:, band * LANES : (band + 1) * LANES]

        @pl.when(step == 0)
        def _(band=band, here=here):
            total[band] = here

        @pl.when(step > 0)
        def _(band=band, here=here):
            total[band] += here

    @pl.when(step == pl.num_programs(0) - 1)
    def _():
        response = jnp.dot(
            taps_ref[:, 0:128],
            fine_ref[0:128, :],
            precision=lax.Precision.HIGHEST,
            preferred_element_type=jnp.float32,
        )
        response = response + taps_ref[:, 128:129] * fine_ref[128:129, :]
        low = lax.broadcasted_iota(jnp.int32, (1, LANES), 1) < BAND
        for band in range(BINS // BAND):
            here = response[:, band * LANES : (band + 1) * LANES]
            other = pltpu.roll(jnp.broadcast_to(here, (8, LANES)), BAND, 1)[0:1, :]
            same = jnp.where(low, here, other)
            cross = jnp.where(low, -other, here)
            for node in range(nodes):
                rows = pl.ds(node, out_ref.shape[2], stride=nodes)
                raw = total[band, rows, :]
                power = jnp.sum(raw * raw, 1, keepdims=True) * (1.0 / BAND)
                white = raw * lax.rsqrt(power + EPSILON)
                turned = white * same + pltpu.roll(white, BAND, 1) * cross
                out_ref[band, node] = turned.astype(jnp.bfloat16)


def own_spectra(rows, taps, nodes):
    fine, turn_c, turn_s = (jnp.asarray(t) for t in forward_tables())
    count = rows.shape[0]
    bands = BINS // BAND
    fixed = lambda shape: pl.BlockSpec(shape, lambda i: (0,) * len(shape))
    return pl.pallas_call(
        spectra_kernel,
        grid=(SAMPLES // CHUNK,),
        in_specs=[
            pl.BlockSpec((count, CHUNK), lambda i: (0, i)),
            fixed(taps.shape),
            fixed(fine.shape),
            fixed(turn_c.shape),
            fixed(turn_s.shape),
        ],
        out_specs=fixed((bands, nodes, count // nodes, LANES)),
        out_shape=jax.ShapeDtypeStruct((bands, nodes, count // nodes, LANES), jnp.bfloat16),
        scratch_shapes=[
            pltpu.VMEM((bands, count, LANES), jnp.float32),
            pltpu.VMEM((STEP, 2 * BINS), jnp.float32),
            pltpu.VMEM((CHUNK, 2 * BINS), jnp.bfloat16),
        ],
        compiler_params=pltpu.CompilerParams(vmem_limit_bytes=60 * MIB),
        name="own_spectra",
    )(rows, taps, fine, turn_c, turn_s)


def lag_table_kernel(cos_ref, msin_ref, cos0_ref, msin0_ref, high_ref, low_ref, *, factor):
    part = pl.program_id(0)
    c0 = cos0_ref[pl.ds(part, 1), :] * factor
    s0 = msin0_ref[pl.ds(part, 1), :] * factor
    cos, msin = cos_ref[...], msin_ref[...]
    for half, values in ((0, cos * c0 - msin * s0), (1, cos * s0 + msin * c0)):
        high = values.astype(jnp.bfloat16)
        rows = pl.ds(half * BAND, BAND)
        high_ref[0, rows, :] = high
        low_ref[0, rows, :] = (values - high.astype(jnp.float32)).astype(jnp.bfloat16)


def make_lag_tables(parts, factor):
    tables = [jnp.asarray(t) for t in lag_tables(parts)]
    shape = jax.ShapeDtypeStruct((parts, LANES, LAGS), jnp.bfloat16)
    block = pl.BlockSpec((1, LANES, LAGS), lambda i: (i, 0, 0))
    return pl.pallas_call(
        functools.partial(lag_table_kernel, factor=factor),
        grid=(parts,),
        in_specs=[pl.BlockSpec(t.shape, lambda i: (0, 0)) for t in tables],
        out_specs=[block, block],
        out_shape=[shape, shape],
        compiler_params=pltpu.CompilerParams(vmem_limit_bytes=6 * MIB),
        name="lag_tables",
    )(*tables)


def by_bin_kernel(odd_ref, x_ref, first_ref, second_ref, turned, *, groups, nodes):
    windows = x_ref.shape[2]
    row = lax.broadcasted_iota(jnp.int32, (LANES, LANES), 0)
    unit = (row == lax.broadcasted_iota(jnp.int32, (LANES, LANES), 1)).astype(jnp.bfloat16)

    def turn(index, _):
        tile, node = index // nodes, index % nodes
        parts = [x_ref[tile * groups + g, node] for g in range(groups)]
        values = lax.dot_general(
            unit, jnp.concatenate(parts, 0), (((1,), (1,)), ((), ())), preferred_element_type=jnp.float32
        )
        turned[pl.ds(pl.multiple_of(index * LANES, LANES), LANES), :] = values
        return 0

    lax.fori_loop(0, 2 * nodes, turn, 0, unroll=4)
    odd = odd_ref[0]
    for out_ref, tile in ((first_ref, 1 - odd), (second_ref, odd)):
        start = tile * (nodes * LANES)

        def one(f, _, out_ref=out_ref, start=start):
            real = turned[pl.ds(start + f, nodes, stride=LANES), :]
            imag = turned[pl.ds(start + BAND + f, nodes, stride=LANES), :]
            out_ref[f] = jnp.concatenate([real, imag], 1).astype(jnp.bfloat16)
            return 0

        lax.fori_loop(0, BAND, one, 0, unroll=4)


def by_bin(odd, received, nodes):
    parts, _, windows, _ = received.shape
    groups = parts // 2
    shape = jax.ShapeDtypeStruct((BAND, nodes, 2 * groups * windows), jnp.bfloat16)
    vmem = pl.BlockSpec(memory_space=pltpu.VMEM)
    return pl.pallas_call(
        functools.partial(by_bin_kernel, groups=groups, nodes=nodes),
        out_shape=[shape, shape],
        in_specs=[pl.BlockSpec(memory_space=pltpu.SMEM), vmem],
        out_specs=[vmem, vmem],
        scratch_shapes=[pltpu.VMEM((2 * nodes * LANES, groups * windows), jnp.float32)],
        compiler_params=pltpu.CompilerParams(vmem_limit_bytes=8 * MIB),
        name="by_bin",
    )(odd, received)


def cross_select_kernel(odd_ref, a_ref, b_ref, ha_ref, hb_ref, select_ref, out_ref, cross):
    nodes, width = a_ref.shape[1], a_ref.shape[2]
    stations, count = 2 * nodes, 4 * nodes
    contract = (((1,), (1,)), ((), ()))

    def one_bin(f, _):
        own = jnp.concatenate([a_ref[f], b_ref[f]], 0)
        partners = jnp.concatenate([own, ha_ref[f], hb_ref[f]], 0)
        turned = jnp.concatenate([own[:, width // 2 :], -own[:, : width // 2]], 1)
        both = jnp.concatenate([own, turned], 0)
        partners = jnp.concatenate([partners, partners], 0)
        cross[pl.ds(pl.multiple_of(f * count, count), count), :] = lax.dot_general(
            both, partners, contract, preferred_element_type=jnp.float32
        )
        return 0

    lax.fori_loop(0, BAND, one_bin, 0, unroll=4)
    slots = out_ref.shape[2]
    destinations = out_ref.shape[0] // 2
    odd = odd_ref[0]
    left = lax.broadcasted_iota(jnp.int32, (2 * BAND, 2 * count), 1) < count

    def one_node(index, _):
        real = cross[pl.ds(index, BAND, stride=count), :]
        imag = cross[pl.ds(stations + index, BAND, stride=count), :]
        values = jnp.concatenate([real, imag], 0)
        high = values.astype(jnp.bfloat16).astype(jnp.float32)
        split = jnp.where(left, high, values - high).astype(jnp.bfloat16)
        picked = lax.dot_general(select_ref[index], split, contract, preferred_element_type=jnp.float32)
        which, node = index // nodes, index % nodes
        tile = jnp.where(which == 0, 1 - odd, odd)
        for d in range(destinations):
            out_ref[tile * destinations + d, node] = picked[d * slots : (d + 1) * slots, :]
        return 0

    lax.fori_loop(0, stations, one_node, 0, unroll=2)


def cross_select(odd, a, b, halo_a, halo_b, select, parts):
    nodes = a.shape[1]
    slots = select.shape[1] // (parts // 2)
    vmem = pl.BlockSpec(memory_space=pltpu.VMEM)
    return pl.pallas_call(
        cross_select_kernel,
        out_shape=jax.ShapeDtypeStruct((parts, nodes, slots, LANES), jnp.float32),
        in_specs=[pl.BlockSpec(memory_space=pltpu.SMEM)] + [vmem] * 5,
        out_specs=vmem,
        scratch_shapes=[pltpu.VMEM((BAND * 4 * nodes, 8 * nodes), jnp.float32)],
        compiler_params=pltpu.CompilerParams(vmem_limit_bytes=12 * MIB),
        name="cross_select",
    )(odd, a, b, halo_a, halo_b, select)


def inverse_kernel(x_ref, high_ref, low_ref, out_ref):
    parts, nodes, slots = x_ref.shape[0], x_ref.shape[1], x_ref.shape[2]
    total = None
    for part in range(parts):
        values = x_ref[part].reshape(nodes * slots, LANES)
        high = values.astype(jnp.bfloat16)
        low = (values - high.astype(jnp.float32)).astype(jnp.bfloat16)
        dot = functools.partial(jnp.dot, preferred_element_type=jnp.float32)
        term = dot(high, high_ref[part]) + (dot(low, high_ref[part]) + dot(high, low_ref[part]))
        total = term if total is None else total + term
    out_ref[...] = total.reshape(out_ref.shape)


def inverse(stack, high, low):
    parts, nodes, slots, _ = stack.shape
    block = 256
    table = pl.BlockSpec((parts, LANES, block), lambda i: (0, 0, i))
    return pl.pallas_call(
        inverse_kernel,
        grid=(LAGS // block,),
        in_specs=[pl.BlockSpec(stack.shape, lambda i: (0, 0, 0, 0)), table, table],
        out_specs=pl.BlockSpec((nodes, slots, block), lambda i: (0, 0, i)),
        out_shape=jax.ShapeDtypeStruct((nodes, slots, LAGS), jnp.float32),
        compiler_params=pltpu.CompilerParams(vmem_limit_bytes=10 * MIB),
        name="inverse",
    )(stack, high, low)


def per_device(traces, taps, neighbours, valid, *, pairs, wins):
    windows, nodes, samples = traces.shape
    parts = 2 * wins
    place = lax.axis_index("pairs")
    parity = place % 2
    both = ("pairs", "win")
    groups = [[p * wins + w for p in (k, k + 1) for w in range(wins)] for k in range(0, pairs, 2)]
    exchange = functools.partial(
        lax.all_to_all, axis_name=both, split_axis=0, concat_axis=0, tiled=True, axis_index_groups=groups
    )

    odd = (place // 2) % 2
    first = 1 - odd
    is_first = parity == first
    tile, member = neighbours // nodes, neighbours % nodes
    inside = tile // 2 == place // 2
    block = jnp.where(inside, jnp.where(tile % 2 == first, 0, 1), jnp.where(is_first, 2, 3))
    code = jnp.where(valid != 0, block * nodes + member, -1)
    other = lax.ppermute(code, "pairs", [(i, i ^ 1) for i in range(pairs)])
    codes = jnp.where(is_first, jnp.concatenate([code, other], 0), jnp.concatenate([other, code], 0))
    columns = jnp.arange(8 * nodes, dtype=jnp.int32) % (4 * nodes)
    select = (codes[:, :, None] == columns[None, None, :]).astype(jnp.bfloat16)

    factor = 1.0 / math.sqrt(BINS * windows * wins)
    high, low = make_lag_tables(parts, factor)

    spectra = own_spectra(traces.reshape(windows * nodes, samples), taps.reshape(1, TAPS), nodes)
    odd = odd.reshape(1)
    a, b = by_bin(odd, exchange(spectra), nodes)
    swap_a = [(i, i ^ 2) for i in range(pairs) if (i ^ 2) < pairs]
    swap_b = [(i, j) for i in range(2, pairs) for j in [((i - 2) ^ 2) + 2] if j < pairs]
    halo_a = lax.ppermute(a, "pairs", swap_a)
    halo_b = lax.ppermute(b, "pairs", swap_b)
    stack = cross_select(odd, a, b, halo_a, halo_b, select, parts)
    return inverse(exchange(stack), high, low)


def solution(mesh):
    placed = (P("win", "pairs", None), P(), P("pairs", None), P("pairs", None))
    body = functools.partial(per_device, pairs=mesh.shape["pairs"], wins=mesh.shape["win"])
    return jax.shard_map(
        body, mesh=mesh, in_specs=placed, out_specs=P("pairs", "win", None), check_vma=False
    )
```

```python
import functools
import math

import jax
import jax.numpy as jnp
import numpy as np
from jax import lax
from jax.experimental import pallas as pl
from jax.experimental.pallas import tpu as pltpu
from jax.sharding import PartitionSpec as P

SAMPLES = 4096
BINS = 512
BAND = 64
LOW_BIN = 64
LAGS = 1024
TAPS = 129
LANES = 2 * BAND
EPSILON = 1e-06
STEP = 64
CHUNK = 512
MIB = 1024 * 1024
CONTRACT_LAST = (((1,), (1,)), ((), ()))


def unit_circle(products):
    angles = (products % SAMPLES).astype(np.float64) * (2.0 * math.pi / SAMPLES)
    return np.cos(angles).astype(np.float32), (-np.sin(angles)).astype(np.float32)


def banded(first, second):
    rows = first.shape[0]
    parts = [a.reshape(rows, BINS // BAND, 1, BAND) for a in (first, second)]
    return np.concatenate(parts, 2).reshape(rows, 2 * BINS)


def forward_tables():
    bins = LOW_BIN + np.arange(BINS, dtype=np.int64)
    cos, msin = unit_circle(np.arange(TAPS, dtype=np.int64)[:, None] * bins[None, :])
    fine = banded(cos, msin)
    starts = np.arange(0, SAMPLES, STEP, dtype=np.int64)
    cos, msin = unit_circle(starts[:, None] * bins[None, :])
    return fine, banded(cos, cos), banded(-msin, msin)


def lag_tables(parts):
    lags = np.arange(LAGS, dtype=np.int64) - LAGS // 2
    cos, msin = unit_circle(np.arange(BAND, dtype=np.int64)[:, None] * lags[None, :])
    first = LOW_BIN + BAND * np.arange(parts, dtype=np.int64)
    cos0, msin0 = unit_circle(first[:, None] * lags[None, :])
    return cos, msin, cos0, msin0


def spectra_kernel(me_ref, x_hbm, taps_ref, fine_hbm, turn_c_hbm, turn_s_hbm, *refs, steps):
    outs, refs = refs[: 2 * len(steps)], refs[2 * len(steps) :]
    x_ref, fine_ref, turn_c_ref, turn_s_ref, table, total, stage, sems = refs
    count = x_ref.shape[0]
    nodes, windows = outs[0].shape[0], outs[0].shape[1]
    width, halves = 2 * LANES, 2
    rows = count // halves
    me = me_ref[0]
    copies = [
        pltpu.make_async_copy(source, target, sems.at[i])
        for i, (source, target) in enumerate(
            ((fine_hbm, fine_ref), (turn_c_hbm, turn_c_ref), (turn_s_hbm, turn_s_ref))
        )
    ]
    chunks = [
        pltpu.make_async_copy(x_hbm.at[pl.ds(i * rows, rows), :], x_ref.at[pl.ds(i * rows, rows), :], sems.at[3 + i])
        for i in range(halves)
    ]
    for copy in copies + chunks:
        copy.start()

    def start_of(step):
        return pl.multiple_of(((me // 2) ^ step) * width, width)

    def generate(i):
        columns = pl.ds(start_of(steps[i]), width)
        base = fine_ref[0:STEP, columns]
        swapped = jnp.concatenate(
            [pltpu.roll(base[:, c : c + LANES], BAND, 1) for c in range(0, width, LANES)], 1
        )
        for j in range(SAMPLES // STEP):
            row = pl.ds(j, 1)
            turned = base * turn_c_ref[row, columns] + swapped * turn_s_ref[row, columns]
            table[i % 2, j * STEP : (j + 1) * STEP, :] = turned.astype(jnp.bfloat16)

    low = lax.broadcasted_iota(jnp.int32, (1, LANES), 1) < BAND

    def whiten(i):
        columns = pl.ds(start_of(steps[i]), width)
        response = jnp.dot(
            taps_ref[:, 0:128],
            fine_ref[0:128, columns],
            precision=lax.Precision.HIGHEST,
            preferred_element_type=jnp.float32,
        )
        response = response + taps_ref[:, 128:129] * fine_ref[128:129, columns]
        for c in range(2):
            here = response[:, c * LANES : (c + 1) * LANES]
            other = pltpu.roll(jnp.broadcast_to(here, (8, LANES)), BAND, 1)[0:1, :]
            same = jnp.where(low, here, other)
            cross = jnp.where(low, -other, here)
            raw = total[i % 2, c]
            power = jnp.sum(raw * raw, 1, keepdims=True) * (1.0 / BAND)
            white = raw * lax.rsqrt(power + EPSILON)
            stage[c ^ (me % 2)] = white * same + pltpu.roll(white, BAND, 1) * cross
        for c in range(2):
            for node in range(nodes):
                outs[2 * i + c][node] = stage[c, pl.ds(node, windows, stride=nodes), :].astype(jnp.bfloat16)

    for copy in copies:
        copy.wait()
    for i in range(len(steps)):
        if i == 0:
            generate(0)
        for part in range(halves if i == 0 else 1):
            if i == 0:
                chunks[part].wait()
                here = pl.ds(part * rows, rows)
            else:
                here = pl.ds(0, count)
            product = jnp.dot(x_ref[here, :], table[i % 2], preferred_element_type=jnp.float32)
            for c in range(2):
                total[i % 2, c, here, :] = product[:, c * LANES : (c + 1) * LANES]
        if i + 1 < len(steps):
            generate(i + 1)
        if i > 0:
            whiten(i - 1)
    whiten(len(steps) - 1)


def own_spectra(me, rows, taps, nodes, steps):
    tables = [jnp.asarray(t) for t in forward_tables()]
    count = rows.shape[0]
    hbm = pl.BlockSpec(memory_space=pltpu.HBM)
    vmem = pl.BlockSpec(memory_space=pltpu.VMEM)
    shape = jax.ShapeDtypeStruct((nodes, count // nodes, LANES), jnp.bfloat16)
    return pl.pallas_call(
        functools.partial(spectra_kernel, steps=steps),
        in_specs=[pl.BlockSpec(memory_space=pltpu.SMEM), hbm, vmem, hbm, hbm, hbm],
        out_specs=[vmem] * (2 * len(steps)),
        out_shape=[shape] * (2 * len(steps)),
        scratch_shapes=[
            pltpu.VMEM(rows.shape, jnp.bfloat16),
            *[pltpu.VMEM(t.shape, jnp.float32) for t in tables],
            pltpu.VMEM((2, SAMPLES, 2 * LANES), jnp.bfloat16),
            pltpu.VMEM((2, 2, count, LANES), jnp.float32),
            pltpu.VMEM((2, count, LANES), jnp.float32),
            pltpu.SemaphoreType.DMA((5,)),
        ],
        compiler_params=pltpu.CompilerParams(vmem_limit_bytes=60 * MIB),
        cost_estimate=pl.CostEstimate(
            flops=4 * len(steps) * count * SAMPLES * LANES, bytes_accessed=2 * count * SAMPLES, transcendentals=0
        ),
        name="own_spectra",
    )(me, rows, taps, *tables)


def lag_table_kernel(cos_ref, msin_ref, cos0_ref, msin0_ref, high_ref, low_ref, *, factor):
    part = pl.program_id(0)
    c0 = cos0_ref[pl.ds(part, 1), :] * factor
    s0 = msin0_ref[pl.ds(part, 1), :] * factor
    cos, msin = cos_ref[...], msin_ref[...]
    for half, values in ((0, cos * c0 - msin * s0), (1, cos * s0 + msin * c0)):
        high = values.astype(jnp.bfloat16)
        rows = pl.ds(half * BAND, BAND)
        high_ref[0, rows, :] = high
        low_ref[0, rows, :] = (values - high.astype(jnp.float32)).astype(jnp.bfloat16)


def make_lag_tables(parts, factor):
    tables = [jnp.asarray(t) for t in lag_tables(parts)]
    shape = jax.ShapeDtypeStruct((parts, LANES, LAGS), jnp.bfloat16)
    block = pl.BlockSpec((1, LANES, LAGS), lambda i: (i, 0, 0))
    return pl.pallas_call(
        functools.partial(lag_table_kernel, factor=factor),
        grid=(parts,),
        in_specs=[pl.BlockSpec(t.shape, lambda i: (0, 0)) for t in tables],
        out_specs=[block, block],
        out_shape=[shape, shape],
        compiler_params=pltpu.CompilerParams(vmem_limit_bytes=6 * MIB),
        name="lag_tables",
    )(*tables)


def by_bin_kernel(place_ref, *refs):
    blocks, (first_ref, second_ref, turned) = refs[:-3], refs[-3:]
    groups = len(blocks) // 2
    nodes = blocks[0].shape[0]
    row = lax.broadcasted_iota(jnp.int32, (LANES, LANES), 0)
    unit = (row == lax.broadcasted_iota(jnp.int32, (LANES, LANES), 1)).astype(jnp.bfloat16)
    for tile in range(2):
        here = blocks[tile * groups : (tile + 1) * groups]

        def turn(node, _, here=here, tile=tile):
            values = jnp.concatenate([block[node] for block in here], 0)
            values = lax.dot_general(unit, values, CONTRACT_LAST, preferred_element_type=jnp.float32)
            turned[pl.ds(pl.multiple_of((tile * nodes + node) * LANES, LANES), LANES), :] = values
            return 0

        lax.fori_loop(0, nodes, turn, 0, unroll=4)
    own_at = place_ref[1]
    for out_ref, tile in ((first_ref, own_at), (second_ref, 1 - own_at)):
        start = tile * (nodes * LANES)

        def one(f, _, out_ref=out_ref, start=start):
            real = turned[pl.ds(start + f, nodes, stride=LANES), :]
            imag = turned[pl.ds(start + BAND + f, nodes, stride=LANES), :]
            out_ref[f] = jnp.concatenate([real, imag], 1).astype(jnp.bfloat16)
            return 0

        lax.fori_loop(0, BAND, one, 0, unroll=4)


def by_bin(place, blocks):
    nodes, windows, _ = blocks[0].shape
    windows = windows * len(blocks) // 2
    shape = jax.ShapeDtypeStruct((BAND, nodes, 2 * windows), jnp.bfloat16)
    vmem = pl.BlockSpec(memory_space=pltpu.VMEM)
    return pl.pallas_call(
        by_bin_kernel,
        out_shape=[shape, shape],
        in_specs=[pl.BlockSpec(memory_space=pltpu.SMEM)] + [vmem] * len(blocks),
        out_specs=[vmem, vmem],
        scratch_shapes=[pltpu.VMEM((2 * nodes * LANES, windows), jnp.float32)],
        compiler_params=pltpu.CompilerParams(vmem_limit_bytes=8 * MIB),
        name="by_bin",
    )(place, *blocks)


def pick_slots(cross_ref, select_ref, outs, where, nodes):
    stations, count = 2 * nodes, 4 * nodes
    slots = outs[0].shape[1]
    left = lax.broadcasted_iota(jnp.int32, (2 * BAND, 2 * count), 1) < count

    def one_node(node, _):
        index = where * nodes + node
        real = cross_ref[pl.ds(index, BAND, stride=count), :]
        imag = cross_ref[pl.ds(stations + index, BAND, stride=count), :]
        values = jnp.concatenate([real, imag], 0)
        high = values.astype(jnp.bfloat16).astype(jnp.float32)
        split = jnp.where(left, high, values - high).astype(jnp.bfloat16)
        picked = lax.dot_general(select_ref[index], split, CONTRACT_LAST, preferred_element_type=jnp.float32)
        for d, out_ref in enumerate(outs):
            out_ref[node] = picked[d * slots : (d + 1) * slots, :]
        return 0

    lax.fori_loop(0, nodes, one_node, 0, unroll=4)


def cross_kernel(place_ref, a_ref, b_ref, ha_ref, hb_ref, select_ref, cross, *outs):
    nodes, width = a_ref.shape[1], a_ref.shape[2]
    count = 4 * nodes

    def one_bin(f, _):
        own = jnp.concatenate([a_ref[f], b_ref[f]], 0)
        partners = jnp.concatenate([own, ha_ref[f], hb_ref[f]], 0)
        turned = jnp.concatenate([own[:, width // 2 :], -own[:, : width // 2]], 1)
        both = jnp.concatenate([own, turned], 0)
        partners = jnp.concatenate([partners, partners], 0)
        cross[pl.ds(pl.multiple_of(f * count, count), count), :] = lax.dot_general(
            both, partners, CONTRACT_LAST, preferred_element_type=jnp.float32
        )
        return 0

    lax.fori_loop(0, BAND, one_bin, 0, unroll=8)
    pick_slots(cross, select_ref, outs, 1 - place_ref[1], nodes)


def own_slots_kernel(place_ref, cross_ref, select_ref, *outs):
    pick_slots(cross_ref, select_ref, outs, place_ref[1], outs[0].shape[0])


def cross_products(place, a, b, halo_a, halo_b, select, wins):
    nodes = a.shape[1]
    block = jax.ShapeDtypeStruct((nodes, select.shape[1] // wins, LANES), jnp.float32)
    vmem = pl.BlockSpec(memory_space=pltpu.VMEM)
    cross, *others = pl.pallas_call(
        cross_kernel,
        out_shape=[jax.ShapeDtypeStruct((BAND * 4 * nodes, 8 * nodes), jnp.float32)] + [block] * wins,
        in_specs=[pl.BlockSpec(memory_space=pltpu.SMEM)] + [vmem] * 5,
        out_specs=[vmem] * (1 + wins),
        compiler_params=pltpu.CompilerParams(vmem_limit_bytes=12 * MIB),
        name="cross_products",
    )(place, a, b, halo_a, halo_b, select)
    own = pl.pallas_call(
        own_slots_kernel,
        out_shape=[block] * wins,
        in_specs=[pl.BlockSpec(memory_space=pltpu.SMEM)] + [vmem] * 2,
        out_specs=[vmem] * wins,
        compiler_params=pltpu.CompilerParams(vmem_limit_bytes=8 * MIB),
        cost_estimate=pl.CostEstimate(flops=1 << 32, bytes_accessed=1 << 24, transcendentals=0),
        name="own_slots",
    )(place, cross, select)
    return own, others


def inverse_kernel(me_ref, high_ref, low_ref, *refs):
    blocks, out_ref = refs[:-1], refs[-1]
    nodes, slots, _ = blocks[0].shape
    me = me_ref[0]
    dot = functools.partial(jnp.dot, preferred_element_type=jnp.float32)
    total = None
    for d, block in enumerate(blocks):
        part = me ^ d
        values = block[...].reshape(nodes * slots, LANES)
        high = values.astype(jnp.bfloat16)
        low = (values - high.astype(jnp.float32)).astype(jnp.bfloat16)
        term = dot(high, high_ref[part]) + (dot(low, high_ref[part]) + dot(high, low_ref[part]))
        total = term if total is None else total + term
    out_ref[...] = total.reshape(out_ref.shape)


def inverse(me, blocks, high, low):
    nodes, slots, _ = blocks[0].shape
    width = 256
    table = pl.BlockSpec((high.shape[0], LANES, width), lambda i: (0, 0, i))
    return pl.pallas_call(
        inverse_kernel,
        grid=(LAGS // width,),
        in_specs=[pl.BlockSpec(memory_space=pltpu.SMEM), table, table]
        + [pl.BlockSpec(blocks[0].shape, lambda i: (0, 0, 0))] * len(blocks),
        out_specs=pl.BlockSpec((nodes, slots, width), lambda i: (0, 0, i)),
        out_shape=jax.ShapeDtypeStruct((nodes, slots, LAGS), jnp.float32),
        compiler_params=pltpu.CompilerParams(vmem_limit_bytes=10 * MIB),
        name="inverse",
    )(me, high, low, *blocks)


def per_device(traces, taps, neighbours, valid, *, pairs, wins):
    windows, nodes, samples = traces.shape
    parts = 2 * wins
    place = lax.axis_index("pairs")
    win = lax.axis_index("win")
    parity = place % 2
    me = parity * wins + win

    def exchange(blocks):
        moved = list(blocks)
        for d in range(parts - 1, 0, -1):
            hop = [(i, (((i // wins) ^ (d // wins)) * wins) + ((i % wins) ^ (d % wins))) for i in range(pairs * wins)]
            moved[d] = lax.ppermute(blocks[d], ("pairs", "win"), hop)
        return moved

    odd = (place // 2) % 2
    first = 1 - odd
    is_first = parity == first
    tile, member = neighbours // nodes, neighbours % nodes
    inside = tile // 2 == place // 2
    block = jnp.where(inside, jnp.where(tile % 2 == first, 0, 1), jnp.where(is_first, 2, 3))
    code = jnp.where(valid != 0, block * nodes + member, -1)
    other = lax.ppermute(code, "pairs", [(i, i ^ 1) for i in range(pairs)])
    codes = jnp.where(is_first, jnp.concatenate([code, other], 0), jnp.concatenate([other, code], 0))
    codes = codes.reshape(2 * nodes, wins, -1)
    for bit in (1 << k for k in range((wins - 1).bit_length())):
        split = codes.reshape(2 * nodes, wins // (2 * bit), 2, -1)
        codes = jnp.where(win & bit != 0, split[:, :, ::-1], split)
    codes = codes.reshape(2 * nodes, -1)
    columns = jnp.arange(8 * nodes, dtype=jnp.int32) % (4 * nodes)
    select = (codes[:, :, None] == columns[None, None, :]).astype(jnp.bfloat16)

    factor = 1.0 / math.sqrt(BINS * windows * wins)
    high, low = make_lag_tables(parts, factor)

    where = jnp.stack([me, jnp.where(is_first, 0, 1)]).astype(jnp.int32)
    rows, taps = traces.reshape(windows * nodes, samples), taps.reshape(1, TAPS)
    spectra = [None] * parts
    for steps in ((3, 1), (2, 0)):
        found = own_spectra(where, rows, taps, nodes, steps)
        for i, step in enumerate(steps):
            spectra[2 * step], spectra[2 * step + 1] = found[2 * i], found[2 * i + 1]
    a, b = by_bin(where, exchange(spectra))
    swap_a = [(i, i ^ 2) for i in range(pairs) if (i ^ 2) < pairs]
    swap_b = [(i, j) for i in range(2, pairs) for j in [((i - 2) ^ 2) + 2] if j < pairs]
    halo_a = lax.ppermute(a, "pairs", swap_a)
    halo_b = lax.ppermute(b, "pairs", swap_b)
    own, others = cross_products(where, a, b, halo_a, halo_b, select, wins)
    return inverse(where, exchange([*own, *others]), high, low)


def solution(mesh):
    placed = (P("win", "pairs", None), P(), P("pairs", None), P("pairs", None))
    body = functools.partial(per_device, pairs=mesh.shape["pairs"], wins=mesh.shape["win"])
    return jax.shard_map(
        body, mesh=mesh, in_specs=placed, out_specs=P("pairs", "win", None), check_vma=False
    )
```

```python
import functools
import math

import jax
import jax.numpy as jnp
import numpy as np
from jax import lax
from jax.experimental import pallas as pl
from jax.experimental.pallas import tpu as pltpu
from jax.sharding import PartitionSpec as P

SAMPLES = 4096
BINS = 512
BAND = 64
LOW_BIN = 64
LAGS = 1024
TAPS = 129
LANES = 2 * BAND
EPSILON = 1e-06
STEP = 64
CHUNK = 512
MIB = 1024 * 1024
CONTRACT_LAST = (((1,), (1,)), ((), ()))


def unit_circle(products):
    angles = (products % SAMPLES).astype(np.float64) * (2.0 * math.pi / SAMPLES)
    return np.cos(angles).astype(np.float32), (-np.sin(angles)).astype(np.float32)


def banded(first, second):
    rows = first.shape[0]
    parts = [a.reshape(rows, BINS // BAND, 1, BAND) for a in (first, second)]
    return np.concatenate(parts, 2).reshape(rows, 2 * BINS)


def forward_tables():
    bins = LOW_BIN + np.arange(BINS, dtype=np.int64)
    cos, msin = unit_circle(np.arange(TAPS, dtype=np.int64)[:, None] * bins[None, :])
    fine = banded(cos, msin)
    starts = np.arange(0, SAMPLES, STEP, dtype=np.int64)
    cos, msin = unit_circle(starts[:, None] * bins[None, :])
    return fine, banded(cos, cos), banded(-msin, msin)


def lag_tables(parts):
    lags = np.arange(LAGS, dtype=np.int64) - LAGS // 2
    cos, msin = unit_circle(np.arange(BAND, dtype=np.int64)[:, None] * lags[None, :])
    first = LOW_BIN + BAND * np.arange(parts, dtype=np.int64)
    cos0, msin0 = unit_circle(first[:, None] * lags[None, :])
    return cos, msin, cos0, msin0


def position(wins):
    place = lax.axis_index("pairs")
    me = (place % 2) * wins + lax.axis_index("win")
    return me, place % 2 != (place // 2) % 2


def spectra_kernel(x_hbm, taps_ref, fine_hbm, turn_c_hbm, turn_s_hbm, *refs, steps, wins):
    outs, refs = refs[: 2 * len(steps)], refs[2 * len(steps) :]
    x_ref, fine_ref, turn_c_ref, turn_s_ref, *refs, sems = refs
    tables, totals, stages = refs[0:2], refs[2:4], refs[4:6]
    count = x_ref.shape[0]
    nodes, windows = outs[0].shape[0], outs[0].shape[1]
    width = 2 * LANES
    pieces = SAMPLES // CHUNK
    me, _ = position(wins)
    copies = [
        pltpu.make_async_copy(source, target, sems.at[pieces + i])
        for i, (source, target) in enumerate(
            ((fine_hbm, fine_ref), (turn_c_hbm, turn_c_ref), (turn_s_hbm, turn_s_ref))
        )
    ]
    chunks = [
        pltpu.make_async_copy(
            x_hbm.at[:, pl.ds(i * CHUNK, CHUNK)], x_ref.at[:, pl.ds(i * CHUNK, CHUNK)], sems.at[i]
        )
        for i in range(pieces)
    ]
    for copy in copies + chunks:
        copy.start()

    def columns_of(i):
        return pl.ds(pl.multiple_of(((me // 2) ^ steps[i]) * width, width), width)

    def generate(i, piece):
        columns = columns_of(i)
        base = fine_ref[0:STEP, columns]
        swapped = jnp.concatenate(
            [pltpu.roll(base[:, c : c + LANES], BAND, 1) for c in range(0, width, LANES)], 1
        )
        for j in range(piece * (CHUNK // STEP), (piece + 1) * (CHUNK // STEP)):
            row = pl.ds(j, 1)
            turned = base * turn_c_ref[row, columns] + swapped * turn_s_ref[row, columns]
            tables[i % 2][j * STEP : (j + 1) * STEP, :] = turned.astype(jnp.bfloat16)

    low = lax.broadcasted_iota(jnp.int32, (1, LANES), 1) < BAND
    responses = {}

    def respond(i):
        columns = columns_of(i)
        response = jnp.dot(
            taps_ref[:, 0:128],
            fine_ref[0:128, columns],
            precision=lax.Precision.HIGHEST,
            preferred_element_type=jnp.float32,
        )
        response = response + taps_ref[:, 128:129] * fine_ref[128:129, columns]
        responses[i] = []
        for c in range(2):
            here = response[:, c * LANES : (c + 1) * LANES]
            other = pltpu.roll(jnp.broadcast_to(here, (8, LANES)), BAND, 1)[0:1, :]
            responses[i].append((jnp.where(low, here, other), jnp.where(low, -other, here)))

    def whiten(i, piece):
        rows = pl.ds(piece * (count // pieces), count // pieces)
        for c in range(2):
            same, cross = responses[i][c]
            raw = totals[i % 2][c, rows, :]
            power = jnp.sum(raw * raw, 1, keepdims=True) * (1.0 / BAND)
            white = raw * lax.rsqrt(power + EPSILON)
            stages[i % 2][c ^ (me % 2), rows, :] = white * same + pltpu.roll(white, BAND, 1) * cross

    def give(i, piece):
        for c in range(2):
            for node in range(piece * nodes // pieces, (piece + 1) * nodes // pieces):
                values = stages[i % 2][c, pl.ds(node, windows, stride=nodes), :]
                outs[2 * i + c][node] = values.astype(jnp.bfloat16)

    for copy in copies:
        copy.wait()
    for piece in range(pieces):
        generate(0, piece)
    last = len(steps) - 1
    for i in range(len(steps)):
        respond(i)
        for piece in range(pieces):
            part = pl.ds(piece * CHUNK, CHUNK)
            if i == 0:
                chunks[piece].wait()
            product = jnp.dot(x_ref[:, part], tables[i % 2][part, :], preferred_element_type=jnp.float32)
            for c in range(2):
                here = product[:, c * LANES : (c + 1) * LANES]
                totals[i % 2][c] = here if piece == 0 else totals[i % 2][c] + here
            if i < last:
                generate(i + 1, piece)
            if i > 0:
                whiten(i - 1, piece)
            if i > 1:
                give(i - 2, piece)
    for piece in range(pieces):
        whiten(last, piece)
        if last > 0:
            give(last - 1, piece)
    for piece in range(pieces):
        give(last, piece)


def own_spectra(rows, taps, nodes, steps):
    tables = [jnp.asarray(t) for t in forward_tables()]
    count = rows.shape[0]
    hbm = pl.BlockSpec(memory_space=pltpu.HBM)
    vmem = pl.BlockSpec(memory_space=pltpu.VMEM)
    shape = jax.ShapeDtypeStruct((nodes, count // nodes, LANES), jnp.bfloat16)
    return pl.pallas_call(
        functools.partial(spectra_kernel, steps=steps, wins=len(steps)),
        in_specs=[hbm, vmem, hbm, hbm, hbm],
        out_specs=[vmem] * (2 * len(steps)),
        out_shape=[shape] * (2 * len(steps)),
        scratch_shapes=[
            pltpu.VMEM(rows.shape, jnp.bfloat16),
            *[pltpu.VMEM(t.shape, jnp.float32) for t in tables],
            *[pltpu.VMEM((SAMPLES, 2 * LANES), jnp.bfloat16)] * 2,
            *[pltpu.VMEM((2, count, LANES), jnp.float32)] * 4,
            pltpu.SemaphoreType.DMA((SAMPLES // CHUNK + 3,)),
        ],
        compiler_params=pltpu.CompilerParams(vmem_limit_bytes=60 * MIB),
        cost_estimate=pl.CostEstimate(
            flops=4 * len(steps) * count * SAMPLES * LANES, bytes_accessed=2 * count * SAMPLES, transcendentals=0
        ),
        name="own_spectra",
    )(rows, taps, *tables)


def lag_table_kernel(cos_ref, msin_ref, cos0_ref, msin0_ref, high_ref, low_ref, *, factor):
    part = pl.program_id(0)
    c0 = cos0_ref[pl.ds(part, 1), :] * factor
    s0 = msin0_ref[pl.ds(part, 1), :] * factor
    cos, msin = cos_ref[...], msin_ref[...]
    for half, values in ((0, cos * c0 - msin * s0), (1, cos * s0 + msin * c0)):
        high = values.astype(jnp.bfloat16)
        rows = pl.ds(half * BAND, BAND)
        high_ref[0, rows, :] = high
        low_ref[0, rows, :] = (values - high.astype(jnp.float32)).astype(jnp.bfloat16)


def make_lag_tables(parts, factor):
    tables = [jnp.asarray(t) for t in lag_tables(parts)]
    shape = jax.ShapeDtypeStruct((parts, LANES, LAGS), jnp.bfloat16)
    block = pl.BlockSpec((1, LANES, LAGS), lambda i: (i, 0, 0))
    return pl.pallas_call(
        functools.partial(lag_table_kernel, factor=factor),
        grid=(parts,),
        in_specs=[pl.BlockSpec(t.shape, lambda i: (0, 0)) for t in tables],
        out_specs=[block, block],
        out_shape=[shape, shape],
        compiler_params=pltpu.CompilerParams(vmem_limit_bytes=6 * MIB),
        name="lag_tables",
    )(*tables)


def by_bin_kernel(*refs):
    blocks, (first_ref, second_ref, turned) = refs[:-3], refs[-3:]
    groups = len(blocks) // 2
    nodes = blocks[0].shape[0]
    _, is_first = position(groups)
    own_at = jnp.where(is_first, 0, 1)
    row = lax.broadcasted_iota(jnp.int32, (LANES, LANES), 0)
    unit = (row == lax.broadcasted_iota(jnp.int32, (LANES, LANES), 1)).astype(jnp.bfloat16)
    for tile in range(2):
        here = blocks[tile * groups : (tile + 1) * groups]

        def turn(node, _, here=here, tile=tile):
            values = jnp.concatenate([block[node] for block in here], 0)
            values = lax.dot_general(unit, values, CONTRACT_LAST, preferred_element_type=jnp.float32)
            turned[pl.ds(pl.multiple_of((tile * nodes + node) * LANES, LANES), LANES), :] = values
            return 0

        lax.fori_loop(0, nodes, turn, 0, unroll=8)
    for out_ref, tile in ((first_ref, own_at), (second_ref, 1 - own_at)):
        start = tile * (nodes * LANES)

        def one(f, _, out_ref=out_ref, start=start):
            real = turned[pl.ds(start + f, nodes, stride=LANES), :]
            imag = turned[pl.ds(start + BAND + f, nodes, stride=LANES), :]
            out_ref[f] = jnp.concatenate([real, imag], 1).astype(jnp.bfloat16)
            return 0

        lax.fori_loop(0, BAND, one, 0, unroll=8)


def by_bin(blocks):
    nodes, windows, _ = blocks[0].shape
    windows = windows * len(blocks) // 2
    shape = jax.ShapeDtypeStruct((BAND, nodes, 2 * windows), jnp.bfloat16)
    vmem = pl.BlockSpec(memory_space=pltpu.VMEM)
    return pl.pallas_call(
        by_bin_kernel,
        out_shape=[shape, shape],
        in_specs=[vmem] * len(blocks),
        out_specs=[vmem, vmem],
        scratch_shapes=[pltpu.VMEM((2 * nodes * LANES, windows), jnp.float32)],
        compiler_params=pltpu.CompilerParams(vmem_limit_bytes=8 * MIB),
        name="by_bin",
    )(*blocks)


def pick_slots(cross_ref, select_ref, outs, where, nodes):
    stations, count = 2 * nodes, 4 * nodes
    slots = outs[0].shape[1]
    left = lax.broadcasted_iota(jnp.int32, (2 * BAND, 2 * count), 1) < count

    def one_node(node, _):
        index = where * nodes + node
        real = cross_ref[pl.ds(index, BAND, stride=count), :]
        imag = cross_ref[pl.ds(stations + index, BAND, stride=count), :]
        values = jnp.concatenate([real, imag], 0)
        high = values.astype(jnp.bfloat16).astype(jnp.float32)
        split = jnp.where(left, high, values - high).astype(jnp.bfloat16)
        picked = lax.dot_general(select_ref[index], split, CONTRACT_LAST, preferred_element_type=jnp.float32)
        for d, out_ref in enumerate(outs):
            out_ref[node] = picked[d * slots : (d + 1) * slots, :]
        return 0

    lax.fori_loop(0, nodes, one_node, 0, unroll=4)


def cross_kernel(a_ref, b_ref, ha_ref, hb_ref, select_ref, cross, *outs):
    nodes, width = a_ref.shape[1], a_ref.shape[2]
    count = 4 * nodes

    def one_bin(f, _):
        own = jnp.concatenate([a_ref[f], b_ref[f]], 0)
        partners = jnp.concatenate([own, ha_ref[f], hb_ref[f]], 0)
        turned = jnp.concatenate([own[:, width // 2 :], -own[:, : width // 2]], 1)
        both = jnp.concatenate([own, turned], 0)
        partners = jnp.concatenate([partners, partners], 0)
        cross[pl.ds(pl.multiple_of(f * count, count), count), :] = lax.dot_general(
            both, partners, CONTRACT_LAST, preferred_element_type=jnp.float32
        )
        return 0

    lax.fori_loop(0, BAND, one_bin, 0, unroll=8)
    _, is_first = position(len(outs))
    pick_slots(cross, select_ref, outs, jnp.where(is_first, 1, 0), nodes)


def own_slots_kernel(cross_ref, select_ref, *outs):
    _, is_first = position(len(outs))
    pick_slots(cross_ref, select_ref, outs, jnp.where(is_first, 0, 1), outs[0].shape[0])


def cross_products(a, b, halo_a, halo_b, select, wins):
    nodes = a.shape[1]
    block = jax.ShapeDtypeStruct((nodes, select.shape[1] // wins, LANES), jnp.float32)
    vmem = pl.BlockSpec(memory_space=pltpu.VMEM)
    cross, *others = pl.pallas_call(
        cross_kernel,
        out_shape=[jax.ShapeDtypeStruct((BAND * 4 * nodes, 8 * nodes), jnp.float32)] + [block] * wins,
        in_specs=[vmem] * 5,
        out_specs=[vmem] * (1 + wins),
        compiler_params=pltpu.CompilerParams(vmem_limit_bytes=12 * MIB),
        name="cross_products",
    )(a, b, halo_a, halo_b, select)
    own = pl.pallas_call(
        own_slots_kernel,
        out_shape=[block] * wins,
        in_specs=[vmem] * 2,
        out_specs=[vmem] * wins,
        compiler_params=pltpu.CompilerParams(vmem_limit_bytes=8 * MIB),
        cost_estimate=pl.CostEstimate(flops=1 << 32, bytes_accessed=1 << 24, transcendentals=0),
        name="own_slots",
    )(cross, select)
    return own, others


def inverse_kernel(high_ref, low_ref, *refs):
    blocks, (out_ref, both) = refs[:-2], refs[-2:]
    nodes, slots, _ = blocks[0].shape
    rows = nodes * slots

    @pl.when(pl.program_id(0) == 0)
    def _():
        me, _ = position(len(blocks) // 2)
        for d, block in enumerate(blocks):
            columns = pl.ds(pl.multiple_of((me ^ d) * LANES, LANES), LANES)
            values = block[...].reshape(rows, LANES)
            high = values.astype(jnp.bfloat16)
            both[0:rows, columns] = high
            both[rows : 2 * rows, columns] = (values - high.astype(jnp.float32)).astype(jnp.bfloat16)

    first = jnp.dot(both[...], high_ref[...], preferred_element_type=jnp.float32)
    second = jnp.dot(both[0:rows, :], low_ref[...], preferred_element_type=jnp.float32)
    out_ref[...] = (first[0:rows, :] + (first[rows : 2 * rows, :] + second)).reshape(out_ref.shape)


def inverse(blocks, high, low):
    nodes, slots, _ = blocks[0].shape
    depth = high.shape[0] * LANES
    width = 256
    table = pl.BlockSpec((depth, width), lambda i: (0, i))
    return pl.pallas_call(
        inverse_kernel,
        grid=(LAGS // width,),
        in_specs=[table, table] + [pl.BlockSpec(blocks[0].shape, lambda i: (0, 0, 0))] * len(blocks),
        out_specs=pl.BlockSpec((nodes, slots, width), lambda i: (0, 0, i)),
        out_shape=jax.ShapeDtypeStruct((nodes, slots, LAGS), jnp.float32),
        scratch_shapes=[pltpu.VMEM((2 * nodes * slots, depth), jnp.bfloat16)],
        compiler_params=pltpu.CompilerParams(vmem_limit_bytes=12 * MIB),
        name="inverse",
    )(high.reshape(depth, LAGS), low.reshape(depth, LAGS), *blocks)


def per_device(traces, taps, neighbours, valid, *, pairs, wins):
    windows, nodes, samples = traces.shape
    parts = 2 * wins
    place = lax.axis_index("pairs")
    win = lax.axis_index("win")

    def exchange(blocks):
        moved = list(blocks)
        for d in range(parts - 1, 0, -1):
            hop = [(i, (((i // wins) ^ (d // wins)) * wins) + ((i % wins) ^ (d % wins))) for i in range(pairs * wins)]
            moved[d] = lax.ppermute(blocks[d], ("pairs", "win"), hop)
        return moved

    rows, taps = traces.reshape(windows * nodes, samples), taps.reshape(1, TAPS)
    steps = tuple(range(wins))[::-1]
    found = own_spectra(rows, taps, nodes, steps)
    found, neighbours, valid = lax.optimization_barrier((found, neighbours, valid))
    spectra = [found[2 * steps.index(d // 2) + d % 2] for d in range(parts)]

    _, is_first = position(wins)
    tile, member = neighbours // nodes, neighbours % nodes
    inside = tile // 2 == place // 2
    leading = 1 - (place // 2) % 2
    block = jnp.where(inside, jnp.where(tile % 2 == leading, 0, 1), jnp.where(is_first, 2, 3))
    code = jnp.where(valid != 0, block * nodes + member, -1)
    other = lax.ppermute(code, "pairs", [(i, i ^ 1) for i in range(pairs)])
    codes = jnp.where(is_first, jnp.concatenate([code, other], 0), jnp.concatenate([other, code], 0))
    for bit in (1 << k for k in range((wins - 1).bit_length())):
        split = codes.reshape(2 * nodes, wins // (2 * bit), 2, -1)
        codes = jnp.where(win & bit != 0, split[:, :, ::-1], split)
    codes = codes.reshape(2 * nodes, -1)
    columns = jnp.arange(8 * nodes, dtype=jnp.int32) % (4 * nodes)
    select = (codes[:, :, None] == columns[None, None, :]).astype(jnp.bfloat16)

    factor = 1.0 / math.sqrt(BINS * windows * wins)
    high, low = make_lag_tables(parts, factor)

    a, b = by_bin(exchange(spectra))
    swap_a = [(i, i ^ 2) for i in range(pairs) if (i ^ 2) < pairs]
    swap_b = [(i, j) for i in range(2, pairs) for j in [((i - 2) ^ 2) + 2] if j < pairs]
    halo_a = lax.ppermute(a, "pairs", swap_a)
    halo_b = lax.ppermute(b, "pairs", swap_b)
    own, others = cross_products(a, b, halo_a, halo_b, select, wins)
    return inverse(exchange([*own, *others]), high, low)


def solution(mesh):
    placed = (P("win", "pairs", None), P(), P("pairs", None), P("pairs", None))
    body = functools.partial(per_device, pairs=mesh.shape["pairs"], wins=mesh.shape["win"])
    return jax.shard_map(
        body, mesh=mesh, in_specs=placed, out_specs=P("pairs", "win", None), check_vma=False
    )
```

```python
import functools
import math

import jax
import jax.numpy as jnp
import numpy as np
from jax import lax
from jax.experimental import pallas as pl
from jax.experimental.pallas import tpu as pltpu
from jax.sharding import PartitionSpec as P

SAMPLES = 4096
BINS = 512
BAND = 64
LOW_BIN = 64
LAGS = 1024
TAPS = 129
LANES = 2 * BAND
EPSILON = 1e-06
STEP = 64
CHUNK = 512
HALVES = 2
MIB = 1024 * 1024
CONTRACT_LAST = (((1,), (1,)), ((), ()))


def unit_circle(products):
    angles = (products % SAMPLES).astype(np.float64) * (2.0 * math.pi / SAMPLES)
    return np.cos(angles).astype(np.float32), (-np.sin(angles)).astype(np.float32)


def banded(first, second):
    rows = first.shape[0]
    parts = [a.reshape(rows, BINS // BAND, 1, BAND) for a in (first, second)]
    return np.concatenate(parts, 2).reshape(rows, 2 * BINS)


def forward_tables():
    bins = LOW_BIN + np.arange(BINS, dtype=np.int64)
    cos, msin = unit_circle(np.arange(TAPS, dtype=np.int64)[:, None] * bins[None, :])
    fine = banded(cos, msin)
    starts = np.arange(0, SAMPLES, STEP, dtype=np.int64)
    cos, msin = unit_circle(starts[:, None] * bins[None, :])
    return fine, banded(cos, cos), banded(-msin, msin)


def lag_tables(parts):
    lags = np.arange(LAGS, dtype=np.int64) - LAGS // 2
    cos, msin = unit_circle(np.arange(BAND, dtype=np.int64)[:, None] * lags[None, :])
    first = LOW_BIN + BAND * np.arange(parts, dtype=np.int64)
    cos0, msin0 = unit_circle(first[:, None] * lags[None, :])
    return cos, msin, cos0, msin0


def position(wins):
    place = lax.axis_index("pairs")
    me = (place % 2) * wins + lax.axis_index("win")
    return me, place % 2 != (place // 2) % 2


def spectra_kernel(x_hbm, taps_ref, fine_hbm, turn_c_hbm, turn_s_hbm, *refs, steps, wins):
    outs, refs = refs[: HALVES * len(steps)], refs[HALVES * len(steps) :]
    x_ref, fine_ref, turn_c_ref, turn_s_ref, *refs, sems = refs
    tables, totals, stages = refs[0:2], refs[2:4], refs[4:6]
    count = x_ref.shape[0]
    nodes, windows = outs[0].shape[1], outs[0].shape[2]
    width = 2 * LANES
    pieces = SAMPLES // CHUNK
    me, _ = position(wins)
    copies = [
        pltpu.make_async_copy(source, target, sems.at[pieces + i])
        for i, (source, target) in enumerate(
            ((fine_hbm, fine_ref), (turn_c_hbm, turn_c_ref), (turn_s_hbm, turn_s_ref))
        )
    ]
    chunks = [
        pltpu.make_async_copy(
            x_hbm.at[:, pl.ds(i * CHUNK, CHUNK)], x_ref.at[:, pl.ds(i * CHUNK, CHUNK)], sems.at[i]
        )
        for i in range(pieces)
    ]
    for copy in copies + chunks:
        copy.start()

    def columns_of(i):
        return pl.ds(pl.multiple_of(((me // 2) ^ steps[i]) * width, width), width)

    def generate(i):
        columns = columns_of(i)
        base = fine_ref[0:STEP, columns]
        swapped = jnp.concatenate(
            [pltpu.roll(base[:, c : c + LANES], BAND, 1) for c in range(0, width, LANES)], 1
        )
        for j in range(SAMPLES // STEP):
            row = pl.ds(j, 1)
            turned = base * turn_c_ref[row, columns] + swapped * turn_s_ref[row, columns]
            tables[i % 2][j * STEP : (j + 1) * STEP, :] = turned.astype(jnp.bfloat16)

    low = lax.broadcasted_iota(jnp.int32, (1, LANES), 1) < BAND
    responses = {}

    def respond(i):
        columns = columns_of(i)
        response = jnp.dot(
            taps_ref[:, 0:128],
            fine_ref[0:128, columns],
            precision=lax.Precision.HIGHEST,
            preferred_element_type=jnp.float32,
        )
        response = response + taps_ref[:, 128:129] * fine_ref[128:129, columns]
        responses[i] = []
        for c in range(2):
            here = response[:, c * LANES : (c + 1) * LANES]
            other = pltpu.roll(jnp.broadcast_to(here, (8, LANES)), BAND, 1)[0:1, :]
            responses[i].append((jnp.where(low, here, other), jnp.where(low, -other, here)))

    row = lax.broadcasted_iota(jnp.int32, (width, width), 0)
    same_band = (row // LANES) == (lax.broadcasted_iota(jnp.int32, (width, width), 1) // LANES)
    summing = same_band.astype(jnp.bfloat16)

    def whiten(i):
        raw = jnp.concatenate([totals[i % 2][c] for c in range(2)], 1)
        square = raw * raw
        high = square.astype(jnp.bfloat16)
        rest = (square - high.astype(jnp.float32)).astype(jnp.bfloat16)
        sums = jnp.dot(jnp.concatenate([high, rest], 0), summing, preferred_element_type=jnp.float32)
        white = raw * lax.rsqrt((sums[0:count, :] + sums[count:, :]) * (1.0 / BAND) + EPSILON)
        for c, (same, cross) in enumerate(responses[i]):
            part = white[:, c * LANES : (c + 1) * LANES]
            stages[i % 2][c ^ (me % 2)] = part * same + pltpu.roll(part, BAND, 1) * cross

    def give(i):
        for half in range(HALVES):
            first = half * windows * nodes
            for c in range(2):
                for node in range(nodes):
                    values = stages[i % 2][c, pl.ds(first + node, windows, stride=nodes), :]
                    outs[half * len(steps) + i][c, node] = values.astype(jnp.bfloat16)

    for copy in copies:
        copy.wait()
    generate(0)
    last = len(steps) - 1
    for copy in chunks:
        copy.wait()
    for i in range(len(steps)):
        respond(i)
        product = jnp.dot(x_ref[...], tables[i % 2][...], preferred_element_type=jnp.float32)
        for c in range(2):
            totals[i % 2][c] = product[:, c * LANES : (c + 1) * LANES]
        if i < last:
            generate(i + 1)
        if i > 0:
            whiten(i - 1)
        if i > 1:
            give(i - 2)
    if last > 0:
        give(last - 1)
    whiten(last)
    give(last)


def own_spectra(rows, taps, nodes, steps):
    tables = [jnp.asarray(t) for t in forward_tables()]
    count = rows.shape[0]
    hbm = pl.BlockSpec(memory_space=pltpu.HBM)
    vmem = pl.BlockSpec(memory_space=pltpu.VMEM)
    shape = jax.ShapeDtypeStruct((2, nodes, count // nodes // HALVES, LANES), jnp.bfloat16)
    return pl.pallas_call(
        functools.partial(spectra_kernel, steps=steps, wins=len(steps)),
        in_specs=[hbm, vmem, hbm, hbm, hbm],
        out_specs=[vmem] * (HALVES * len(steps)),
        out_shape=[shape] * (HALVES * len(steps)),
        scratch_shapes=[
            pltpu.VMEM(rows.shape, jnp.bfloat16),
            *[pltpu.VMEM(t.shape, jnp.float32) for t in tables],
            *[pltpu.VMEM((SAMPLES, 2 * LANES), jnp.bfloat16)] * 2,
            *[pltpu.VMEM((2, count, LANES), jnp.float32)] * 4,
            pltpu.SemaphoreType.DMA((SAMPLES // CHUNK + 3,)),
        ],
        compiler_params=pltpu.CompilerParams(vmem_limit_bytes=60 * MIB),
        cost_estimate=pl.CostEstimate(
            flops=4 * len(steps) * count * SAMPLES * LANES, bytes_accessed=2 * count * SAMPLES, transcendentals=0
        ),
        name="own_spectra",
    )(rows, taps, *tables)


def lag_table_kernel(cos_ref, msin_ref, cos0_ref, msin0_ref, high_ref, low_ref, *, factor):
    part = pl.program_id(0)
    c0 = cos0_ref[pl.ds(part, 1), :] * factor
    s0 = msin0_ref[pl.ds(part, 1), :] * factor
    cos, msin = cos_ref[...], msin_ref[...]
    for half, values in ((0, cos * c0 - msin * s0), (1, cos * s0 + msin * c0)):
        high = values.astype(jnp.bfloat16)
        rows = pl.ds(half * BAND, BAND)
        high_ref[0, rows, :] = high
        low_ref[0, rows, :] = (values - high.astype(jnp.float32)).astype(jnp.bfloat16)


def make_lag_tables(parts, factor):
    tables = [jnp.asarray(t) for t in lag_tables(parts)]
    shape = jax.ShapeDtypeStruct((parts, LANES, LAGS), jnp.bfloat16)
    block = pl.BlockSpec((1, LANES, LAGS), lambda i: (i, 0, 0))
    return pl.pallas_call(
        functools.partial(lag_table_kernel, factor=factor),
        grid=(parts,),
        in_specs=[pl.BlockSpec(t.shape, lambda i: (0, 0)) for t in tables],
        out_specs=[block, block],
        out_shape=[shape, shape],
        compiler_params=pltpu.CompilerParams(vmem_limit_bytes=6 * MIB),
        name="lag_tables",
    )(*tables)


def by_bin_kernel(*refs, steps):
    blocks, refs = refs[: 2 * steps], refs[2 * steps :]
    first_ref, second_ref, turned_ref, turned, near, sem = refs
    nodes, windows = near.shape[0], near.shape[1]
    _, is_first = position(steps)
    own_at = jnp.where(is_first, 0, 1)
    copy = pltpu.make_async_copy(blocks[0].at[0], near, sem)
    copy.start()
    row = lax.broadcasted_iota(jnp.int32, (LANES, LANES), 0)
    unit = (row == lax.broadcasted_iota(jnp.int32, (LANES, LANES), 1)).astype(jnp.bfloat16)
    for tile in (1, 0):
        here = []
        for step in range(tile * steps // 2, (tile + 1) * steps // 2):
            here.append(near if step == 0 else blocks[2 * step].at[0])
            here.append(blocks[2 * step + 1].at[1])
        if tile == 0:
            copy.wait()

        def turn(node, _, here=here, tile=tile):
            values = jnp.concatenate([block[node] for block in here] * 2, 0)
            values = lax.dot_general(unit, values, CONTRACT_LAST, preferred_element_type=jnp.float32)
            turned[pl.ds(pl.multiple_of((tile * nodes + node) * LANES, LANES), LANES), :] = values
            return 0

        lax.fori_loop(0, nodes, turn, 0, unroll=8)
    left = lax.broadcasted_iota(jnp.int32, (nodes, LANES), 1) < LANES // 2
    for which, (out_ref, tile) in enumerate(((first_ref, own_at), (second_ref, 1 - own_at))):
        start = tile * (nodes * LANES)

        def one(f, _, out_ref=out_ref, start=start, which=which):
            real = turned[pl.ds(start + f, nodes, stride=LANES), :]
            imag = turned[pl.ds(start + BAND + f, nodes, stride=LANES), :]
            out_ref[f] = jnp.where(left, real, imag).astype(jnp.bfloat16)
            turned_ref[f, which * nodes : (which + 1) * nodes, :] = jnp.where(left, imag, -real).astype(jnp.bfloat16)
            return 0

        lax.fori_loop(0, BAND, one, 0, unroll=8)


def by_bin(blocks):
    _, nodes, windows, _ = blocks[0].shape
    steps = len(blocks) // 2
    shape = jax.ShapeDtypeStruct((BAND, nodes, LANES), jnp.bfloat16)
    vmem = pl.BlockSpec(memory_space=pltpu.VMEM)
    return pl.pallas_call(
        functools.partial(by_bin_kernel, steps=steps),
        out_shape=[shape, shape, jax.ShapeDtypeStruct((BAND, 2 * nodes, LANES), jnp.bfloat16)],
        in_specs=[pl.BlockSpec(memory_space=pl.ANY)] + [vmem] * (len(blocks) - 1),
        out_specs=[vmem] * 3,
        scratch_shapes=[
            pltpu.VMEM((2 * nodes * LANES, LANES), jnp.float32),
            pltpu.VMEM((nodes, windows, LANES), jnp.bfloat16),
            pltpu.SemaphoreType.DMA,
        ],
        compiler_params=pltpu.CompilerParams(vmem_limit_bytes=8 * MIB),
        cost_estimate=pl.CostEstimate(flops=1 << 31, bytes_accessed=1 << 22, transcendentals=0),
        name="by_bin",
    )(*blocks)


def pick_slots(cross_ref, select_ref, outs, where, nodes):
    stations, count = 2 * nodes, 4 * nodes
    slots = outs[0].shape[2]
    left = lax.broadcasted_iota(jnp.int32, (2 * BAND, 2 * count), 1) < count

    def one_node(node, _):
        index = where * nodes + node
        real = cross_ref[pl.ds(index, BAND, stride=count), :]
        imag = cross_ref[pl.ds(stations + index, BAND, stride=count), :]
        values = jnp.concatenate([real, imag], 0)
        high = values.astype(jnp.bfloat16).astype(jnp.float32)
        split = jnp.where(left, high, values - high).astype(jnp.bfloat16)
        picked = lax.dot_general(select_ref[index], split, CONTRACT_LAST, preferred_element_type=jnp.float32)
        for d in range(2 * len(outs)):
            outs[d // 2][d % 2, node] = picked[d * slots : (d + 1) * slots, :]
        return 0

    lax.fori_loop(0, nodes, one_node, 0, unroll=4)


def cross_kernel(*refs):
    halves = [refs[5 * h : 5 * h + 5] for h in range(HALVES)]
    select_ref, cross, *outs = refs[5 * HALVES :]
    nodes = halves[0][0].shape[1]
    count = 4 * nodes

    def one_bin(f, _):
        wide = lambda k: jnp.concatenate([half[k][f] for half in halves], 1)
        own = jnp.concatenate([wide(0), wide(1)], 0)
        both = jnp.concatenate([own, wide(2)], 0)
        partners = jnp.concatenate([own, wide(3), wide(4)] * 2, 0)
        cross[pl.ds(pl.multiple_of(f * count, count), count), :] = lax.dot_general(
            both, partners, CONTRACT_LAST, preferred_element_type=jnp.float32
        )
        return 0

    lax.fori_loop(0, BAND, one_bin, 0, unroll=8)
    _, is_first = position(2 * len(outs))
    pick_slots(cross, select_ref, outs, jnp.where(is_first, 1, 0), nodes)


def own_slots_kernel(cross_ref, select_ref, *outs):
    _, is_first = position(2 * len(outs))
    pick_slots(cross_ref, select_ref, outs, jnp.where(is_first, 0, 1), outs[0].shape[1])


def cross_products(halves, select, wins):
    nodes = halves[0][0].shape[1]
    block = jax.ShapeDtypeStruct((2, nodes, select.shape[1] // wins, LANES), jnp.float32)
    vmem = pl.BlockSpec(memory_space=pltpu.VMEM)
    operands = [x for half in halves for x in half]
    cross, *others = pl.pallas_call(
        cross_kernel,
        out_shape=[jax.ShapeDtypeStruct((BAND * 4 * nodes, 8 * nodes), jnp.float32)] + [block] * (wins // 2),
        in_specs=[vmem] * (len(operands) + 1),
        out_specs=[vmem] * (1 + wins // 2),
        compiler_params=pltpu.CompilerParams(vmem_limit_bytes=12 * MIB),
        name="cross_products",
    )(*operands, select)
    own = pl.pallas_call(
        own_slots_kernel,
        out_shape=[block] * (wins // 2),
        in_specs=[vmem] * 2,
        out_specs=[vmem] * (wins // 2),
        compiler_params=pltpu.CompilerParams(vmem_limit_bytes=8 * MIB),
        cost_estimate=pl.CostEstimate(flops=1 << 32, bytes_accessed=1 << 24, transcendentals=0),
        name="own_slots",
    )(cross, select)
    return [*own, *others]


def inverse_kernel(high_ref, low_ref, *refs):
    blocks, (out_ref, both) = refs[:-2], refs[-2:]
    _, nodes, slots, _ = blocks[0].shape
    rows = nodes * slots

    @pl.when(pl.program_id(0) == 0)
    def _():
        me, _ = position(len(blocks) // 2)
        for d, block in enumerate(blocks):
            columns = pl.ds(pl.multiple_of((me ^ d) * LANES, LANES), LANES)
            values = block[0].reshape(rows, LANES)
            high = values.astype(jnp.bfloat16)
            both[0:rows, columns] = high
            both[rows : 2 * rows, columns] = (values - high.astype(jnp.float32)).astype(jnp.bfloat16)

    first = jnp.dot(both[...], high_ref[...], preferred_element_type=jnp.float32)
    second = jnp.dot(both[0:rows, :], low_ref[...], preferred_element_type=jnp.float32)
    out_ref[...] = (first[0:rows, :] + (first[rows : 2 * rows, :] + second)).reshape(out_ref.shape)


def inverse(blocks, high, low):
    _, nodes, slots, _ = blocks[0].shape
    depth = high.shape[0] * LANES
    width = 256
    table = pl.BlockSpec((depth, width), lambda i: (0, i))
    return pl.pallas_call(
        inverse_kernel,
        grid=(LAGS // width,),
        in_specs=[table, table]
        + [pl.BlockSpec((1, nodes, slots, LANES), lambda i, j=d % 2: (j, 0, 0, 0)) for d in range(len(blocks))],
        out_specs=pl.BlockSpec((nodes, slots, width), lambda i: (0, 0, i)),
        out_shape=jax.ShapeDtypeStruct((nodes, slots, LAGS), jnp.float32),
        scratch_shapes=[pltpu.VMEM((2 * nodes * slots, depth), jnp.bfloat16)],
        compiler_params=pltpu.CompilerParams(vmem_limit_bytes=12 * MIB),
        name="inverse",
    )(high.reshape(depth, LAGS), low.reshape(depth, LAGS), *blocks)


def per_device(traces, taps, neighbours, valid, *, pairs, wins):
    windows, nodes, samples = traces.shape
    parts = 2 * wins
    place = lax.axis_index("pairs")
    win = lax.axis_index("win")

    def hop(array, d):
        pairing = [
            (i, ((i // wins) ^ (d // wins)) * wins + ((i % wins) ^ (d % wins))) for i in range(pairs * wins)
        ]
        return lax.ppermute(array, ("pairs", "win"), pairing)

    def between_chips(blocks):
        return [hop(block, 2 * s) if s else block for s, block in enumerate(blocks)]

    def within_chip(moved):
        return [x for block in moved for x in (block, hop(block, 1))]

    rows, taps = traces.reshape(windows * nodes, samples), taps.reshape(1, TAPS)
    steps = tuple(range(wins))[::-1]
    found = own_spectra(rows, taps, nodes, steps)
    found, neighbours, valid = lax.optimization_barrier((found, neighbours, valid))

    _, is_first = position(wins)
    tile, member = neighbours // nodes, neighbours % nodes
    inside = tile // 2 == place // 2
    leading = 1 - (place // 2) % 2
    block = jnp.where(inside, jnp.where(tile % 2 == leading, 0, 1), jnp.where(is_first, 2, 3))
    code = jnp.where(valid != 0, block * nodes + member, -1)
    other = lax.ppermute(code, "pairs", [(i, i ^ 1) for i in range(pairs)])
    codes = jnp.where(is_first, jnp.concatenate([code, other], 0), jnp.concatenate([other, code], 0))
    for bit in (1 << k for k in range((wins - 1).bit_length())):
        split = codes.reshape(2 * nodes, wins // (2 * bit), 2, -1)
        codes = jnp.where(win & bit != 0, split[:, :, ::-1], split)
    codes = codes.reshape(2 * nodes, -1)
    columns = jnp.arange(8 * nodes, dtype=jnp.int32) % (4 * nodes)
    select = (codes[:, :, None] == columns[None, None, :]).astype(jnp.bfloat16)

    factor = 1.0 / math.sqrt(BINS * windows * wins)
    high, low = make_lag_tables(parts, factor)

    swap_a = [(i, i ^ 2) for i in range(pairs) if (i ^ 2) < pairs]
    swap_b = [(i, j) for i in range(2, pairs) for j in [((i - 2) ^ 2) + 2] if j < pairs]
    halves, moved = [], []

    def finish(moved):
        a, b, turned = by_bin(within_chip(moved))
        halves.append((a, b, turned, lax.ppermute(a, "pairs", swap_a), lax.ppermute(b, "pairs", swap_b)))

    for half in range(HALVES):
        blocks = [found[half * wins + steps.index(s)] for s in range(wins)]
        if half:
            blocks, moved[1] = lax.optimization_barrier((blocks, moved[1]))
            finish(moved)
        moved = between_chips(blocks)
    finish(moved)
    stack = cross_products(halves, select, wins)
    return inverse(within_chip(between_chips(stack)), high, low)


def solution(mesh):
    placed = (P("win", "pairs", None), P(), P("pairs", None), P("pairs", None))
    body = functools.partial(per_device, pairs=mesh.shape["pairs"], wins=mesh.shape["win"])
    return jax.shard_map(
        body, mesh=mesh, in_specs=placed, out_specs=P("pairs", "win", None), check_vma=False
    )
```

```python
import functools
import math

import jax
import jax.numpy as jnp
import numpy as np
from jax import lax
from jax.experimental import pallas as pl
from jax.experimental.pallas import tpu as pltpu
from jax.sharding import PartitionSpec as P

SAMPLES = 4096
BINS = 512
BAND = 64
LOW_BIN = 64
LAGS = 1024
TAPS = 129
LANES = 2 * BAND
EPSILON = 1e-06
STEP = 64
CHUNK = 512
HALVES = 2
MIB = 1024 * 1024
CONTRACT_LAST = (((1,), (1,)), ((), ()))


def unit_circle(products):
    angles = (products % SAMPLES).astype(np.float64) * (2.0 * math.pi / SAMPLES)
    return np.cos(angles).astype(np.float32), (-np.sin(angles)).astype(np.float32)


def banded(first, second):
    rows = first.shape[0]
    parts = [a.reshape(rows, BINS // BAND, 1, BAND) for a in (first, second)]
    return np.concatenate(parts, 2).reshape(rows, 2 * BINS)


def forward_tables():
    bins = LOW_BIN + np.arange(BINS, dtype=np.int64)
    cos, msin = unit_circle(np.arange(TAPS, dtype=np.int64)[:, None] * bins[None, :])
    fine = banded(cos, msin)
    starts = np.arange(0, SAMPLES, STEP, dtype=np.int64)
    cos, msin = unit_circle(starts[:, None] * bins[None, :])
    return fine, banded(cos, cos), banded(-msin, msin)


def lag_tables(parts):
    lags = np.arange(LAGS, dtype=np.int64) - LAGS // 2
    cos, msin = unit_circle(np.arange(BAND, dtype=np.int64)[:, None] * lags[None, :])
    first = LOW_BIN + BAND * np.arange(parts, dtype=np.int64)
    cos0, msin0 = unit_circle(first[:, None] * lags[None, :])
    return cos, msin, cos0, msin0


def position(wins):
    place = lax.axis_index("pairs")
    me = (place % 2) * wins + lax.axis_index("win")
    return me, place % 2 != (place // 2) % 2


def spectra_kernel(x_hbm, taps_ref, fine_hbm, turn_c_hbm, turn_s_hbm, *refs, steps, wins):
    outs, refs = refs[: len(steps)], refs[len(steps) :]
    x_ref, fine_ref, turn_c_ref, turn_s_ref, *refs, sems = refs
    tables, totals, stages = refs[0:2], refs[2:4], refs[4:6]
    count = x_ref.shape[0]
    nodes, windows = outs[0].shape[0], outs[0].shape[1]
    width = 2 * LANES
    pieces = SAMPLES // CHUNK
    me, _ = position(wins)
    copies = [
        pltpu.make_async_copy(source, target, sems.at[pieces + i])
        for i, (source, target) in enumerate(
            ((fine_hbm, fine_ref), (turn_c_hbm, turn_c_ref), (turn_s_hbm, turn_s_ref))
        )
    ]
    chunks = [
        pltpu.make_async_copy(
            x_hbm.at[:, pl.ds(i * CHUNK, CHUNK)], x_ref.at[:, pl.ds(i * CHUNK, CHUNK)], sems.at[i]
        )
        for i in range(pieces)
    ]
    for copy in copies + chunks:
        copy.start()

    def columns_of(i):
        return [pl.ds(pl.multiple_of((me ^ (2 * step)) * LANES, LANES), LANES) for step in steps[2 * i : 2 * i + 2]]

    def generate(i):
        for c, columns in enumerate(columns_of(i)):
            base = fine_ref[0:STEP, columns]
            swapped = pltpu.roll(base, BAND, 1)
            for j in range(SAMPLES // STEP):
                row = pl.ds(j, 1)
                turned = base * turn_c_ref[row, columns] + swapped * turn_s_ref[row, columns]
                tables[i % 2][j * STEP : (j + 1) * STEP, c * LANES : (c + 1) * LANES] = turned.astype(jnp.bfloat16)

    low = lax.broadcasted_iota(jnp.int32, (1, LANES), 1) < BAND
    responses = {}

    def respond(i):
        responses[i] = []
        for columns in columns_of(i):
            here = jnp.dot(
                taps_ref[:, 0:128],
                fine_ref[0:128, columns],
                precision=lax.Precision.HIGHEST,
                preferred_element_type=jnp.float32,
            )
            here = here + taps_ref[:, 128:129] * fine_ref[128:129, columns]
            other = pltpu.roll(jnp.broadcast_to(here, (8, LANES)), BAND, 1)[0:1, :]
            responses[i].append((jnp.where(low, here, other), jnp.where(low, -other, here)))

    row = lax.broadcasted_iota(jnp.int32, (width, width), 0)
    same_band = (row // LANES) == (lax.broadcasted_iota(jnp.int32, (width, width), 1) // LANES)
    summing = same_band.astype(jnp.bfloat16)

    def whiten(i):
        raw = jnp.concatenate([totals[i % 2][c] for c in range(2)], 1)
        square = raw * raw
        high = square.astype(jnp.bfloat16)
        rest = (square - high.astype(jnp.float32)).astype(jnp.bfloat16)
        sums = jnp.dot(jnp.concatenate([high, rest], 0), summing, preferred_element_type=jnp.float32)
        white = raw * lax.rsqrt((sums[0:count, :] + sums[count:, :]) * (1.0 / BAND) + EPSILON)
        for c, (same, cross) in enumerate(responses[i]):
            part = white[:, c * LANES : (c + 1) * LANES]
            stages[i % 2][c] = part * same + pltpu.roll(part, BAND, 1) * cross

    def give(i):
        for c in range(2):
            for node in range(nodes):
                values = stages[i % 2][c, pl.ds(node, windows, stride=nodes), :]
                outs[2 * i + c][node] = values.astype(jnp.bfloat16)

    for copy in copies:
        copy.wait()
    generate(0)
    last = len(steps) // 2 - 1
    for copy in chunks:
        copy.wait()
    for i in range(len(steps) // 2):
        respond(i)
        product = jnp.dot(x_ref[...], tables[i % 2][...], preferred_element_type=jnp.float32)
        for c in range(2):
            totals[i % 2][c] = product[:, c * LANES : (c + 1) * LANES]
        if i < last:
            generate(i + 1)
        if i > 0:
            whiten(i - 1)
        if i > 1:
            give(i - 2)
    if last > 0:
        give(last - 1)
    whiten(last)
    give(last)


def own_spectra(rows, taps, nodes, steps):
    tables = [jnp.asarray(t) for t in forward_tables()]
    count = rows.shape[0]
    hbm = pl.BlockSpec(memory_space=pltpu.HBM)
    vmem = pl.BlockSpec(memory_space=pltpu.VMEM)
    shape = jax.ShapeDtypeStruct((nodes, count // nodes, LANES), jnp.bfloat16)
    return pl.pallas_call(
        functools.partial(spectra_kernel, steps=steps, wins=len(steps)),
        in_specs=[hbm, vmem, hbm, hbm, hbm],
        out_specs=[vmem] * len(steps),
        out_shape=[shape] * len(steps),
        scratch_shapes=[
            pltpu.VMEM(rows.shape, jnp.bfloat16),
            *[pltpu.VMEM(t.shape, jnp.float32) for t in tables],
            *[pltpu.VMEM((SAMPLES, 2 * LANES), jnp.bfloat16)] * 2,
            *[pltpu.VMEM((2, count, LANES), jnp.float32)] * 4,
            pltpu.SemaphoreType.DMA((SAMPLES // CHUNK + 3,)),
        ],
        compiler_params=pltpu.CompilerParams(vmem_limit_bytes=60 * MIB),
        cost_estimate=pl.CostEstimate(
            flops=2 * len(steps) * count * SAMPLES * LANES, bytes_accessed=2 * count * SAMPLES, transcendentals=0
        ),
        name="own_spectra",
    )(rows, taps, *tables)


def lag_table_kernel(cos_ref, msin_ref, cos0_ref, msin0_ref, high_ref, low_ref, *, factor):
    part = pl.program_id(0)
    c0 = cos0_ref[pl.ds(part, 1), :] * factor
    s0 = msin0_ref[pl.ds(part, 1), :] * factor
    cos, msin = cos_ref[...], msin_ref[...]
    for half, values in ((0, cos * c0 - msin * s0), (1, cos * s0 + msin * c0)):
        high = values.astype(jnp.bfloat16)
        rows = pl.ds(half * BAND, BAND)
        high_ref[0, rows, :] = high
        low_ref[0, rows, :] = (values - high.astype(jnp.float32)).astype(jnp.bfloat16)


def make_lag_tables(parts, factor):
    tables = [jnp.asarray(t) for t in lag_tables(parts)]
    shape = jax.ShapeDtypeStruct((parts, LANES, LAGS), jnp.bfloat16)
    block = pl.BlockSpec((1, LANES, LAGS), lambda i: (i, 0, 0))
    return pl.pallas_call(
        functools.partial(lag_table_kernel, factor=factor),
        grid=(parts,),
        in_specs=[pl.BlockSpec(t.shape, lambda i: (0, 0)) for t in tables],
        out_specs=[block, block],
        out_shape=[shape, shape],
        compiler_params=pltpu.CompilerParams(vmem_limit_bytes=6 * MIB),
        name="lag_tables",
    )(*tables)


def by_bin_kernel(*refs, steps):
    blocks, refs = refs[:steps], refs[steps:]
    first_ref, second_ref, turned_ref, turned, near, sem = refs
    nodes, windows = near.shape[0], near.shape[1]
    _, is_first = position(steps)
    own_at = jnp.where(is_first, 0, 1)
    copy = pltpu.make_async_copy(blocks[0], near, sem)
    copy.start()
    row = lax.broadcasted_iota(jnp.int32, (LANES, LANES), 0)
    unit = (row == lax.broadcasted_iota(jnp.int32, (LANES, LANES), 1)).astype(jnp.bfloat16)
    for tile in (1, 0):
        here = [near if s == 0 else blocks[s] for s in range(tile * steps // 2, (tile + 1) * steps // 2)]
        if tile == 0:
            copy.wait()

        def turn(node, _, here=here, tile=tile):
            values = jnp.concatenate([block[node] for block in here] * 2, 0)
            values = lax.dot_general(unit, values, CONTRACT_LAST, preferred_element_type=jnp.float32)
            turned[pl.ds(pl.multiple_of((tile * nodes + node) * LANES, LANES), LANES), :] = values
            return 0

        lax.fori_loop(0, nodes, turn, 0, unroll=8)
    left = lax.broadcasted_iota(jnp.int32, (nodes, LANES), 1) < LANES // 2
    for which, (out_ref, tile) in enumerate(((first_ref, own_at), (second_ref, 1 - own_at))):
        start = tile * (nodes * LANES)

        def one(f, _, out_ref=out_ref, start=start, which=which):
            real = turned[pl.ds(start + f, nodes, stride=LANES), :]
            imag = turned[pl.ds(start + BAND + f, nodes, stride=LANES), :]
            out_ref[f] = jnp.where(left, real, imag).astype(jnp.bfloat16)
            turned_ref[f, which * nodes : (which + 1) * nodes, :] = jnp.where(left, imag, -real).astype(jnp.bfloat16)
            return 0

        lax.fori_loop(0, BAND, one, 0, unroll=8)


def by_bin(blocks):
    nodes, windows, _ = blocks[0].shape
    steps = len(blocks)
    shape = jax.ShapeDtypeStruct((BAND, nodes, LANES), jnp.bfloat16)
    vmem = pl.BlockSpec(memory_space=pltpu.VMEM)
    return pl.pallas_call(
        functools.partial(by_bin_kernel, steps=steps),
        out_shape=[shape, shape, jax.ShapeDtypeStruct((BAND, 2 * nodes, LANES), jnp.bfloat16)],
        in_specs=[pl.BlockSpec(memory_space=pl.ANY)] + [vmem] * (len(blocks) - 1),
        out_specs=[vmem] * 3,
        scratch_shapes=[
            pltpu.VMEM((2 * nodes * LANES, LANES), jnp.float32),
            pltpu.VMEM((nodes, windows, LANES), jnp.bfloat16),
            pltpu.SemaphoreType.DMA,
        ],
        compiler_params=pltpu.CompilerParams(vmem_limit_bytes=8 * MIB),
        cost_estimate=pl.CostEstimate(flops=1 << 31, bytes_accessed=1 << 22, transcendentals=0),
        name="by_bin",
    )(*blocks)


def pick_slots(cross_ref, select_ref, outs, where, nodes):
    stations, count = 2 * nodes, 4 * nodes
    slots = outs[0].shape[2]
    left = lax.broadcasted_iota(jnp.int32, (2 * BAND, 2 * count), 1) < count

    def one_node(node, _):
        index = where * nodes + node
        real = cross_ref[pl.ds(index, BAND, stride=count), :]
        imag = cross_ref[pl.ds(stations + index, BAND, stride=count), :]
        values = jnp.concatenate([real, imag], 0)
        high = values.astype(jnp.bfloat16).astype(jnp.float32)
        split = jnp.where(left, high, values - high).astype(jnp.bfloat16)
        picked = lax.dot_general(select_ref[index], split, CONTRACT_LAST, preferred_element_type=jnp.float32)
        for d in range(2 * len(outs)):
            outs[d // 2][d % 2, node] = picked[d * slots : (d + 1) * slots, :]
        return 0

    lax.fori_loop(0, nodes, one_node, 0, unroll=4)


def cross_kernel(*refs):
    halves = [refs[5 * h : 5 * h + 5] for h in range(HALVES)]
    select_ref, cross, *outs = refs[5 * HALVES :]
    nodes = halves[0][0].shape[1]
    count = 4 * nodes

    def one_bin(f, _):
        wide = lambda k: jnp.concatenate([half[k][f] for half in halves], 1)
        own = jnp.concatenate([wide(0), wide(1)], 0)
        both = jnp.concatenate([own, wide(2)], 0)
        partners = jnp.concatenate([own, wide(3), wide(4)] * 2, 0)
        cross[pl.ds(pl.multiple_of(f * count, count), count), :] = lax.dot_general(
            both, partners, CONTRACT_LAST, preferred_element_type=jnp.float32
        )
        return 0

    lax.fori_loop(0, BAND, one_bin, 0, unroll=8)
    _, is_first = position(2 * len(outs))
    pick_slots(cross, select_ref, outs, jnp.where(is_first, 1, 0), nodes)


def own_slots_kernel(cross_ref, select_ref, *outs):
    _, is_first = position(2 * len(outs))
    pick_slots(cross_ref, select_ref, outs, jnp.where(is_first, 0, 1), outs[0].shape[1])


def cross_products(halves, select, wins):
    nodes = halves[0][0].shape[1]
    block = jax.ShapeDtypeStruct((2, nodes, select.shape[1] // wins, LANES), jnp.float32)
    vmem = pl.BlockSpec(memory_space=pltpu.VMEM)
    operands = [x for half in halves for x in half]
    cross, *others = pl.pallas_call(
        cross_kernel,
        out_shape=[jax.ShapeDtypeStruct((BAND * 4 * nodes, 8 * nodes), jnp.float32)] + [block] * (wins // 2),
        in_specs=[vmem] * (len(operands) + 1),
        out_specs=[vmem] * (1 + wins // 2),
        compiler_params=pltpu.CompilerParams(vmem_limit_bytes=12 * MIB),
        name="cross_products",
    )(*operands, select)
    own = pl.pallas_call(
        own_slots_kernel,
        out_shape=[block] * (wins // 2),
        in_specs=[vmem] * 2,
        out_specs=[vmem] * (wins // 2),
        compiler_params=pltpu.CompilerParams(vmem_limit_bytes=8 * MIB),
        cost_estimate=pl.CostEstimate(flops=1 << 32, bytes_accessed=1 << 24, transcendentals=0),
        name="own_slots",
    )(cross, select)
    return [*own, *others]


def inverse_kernel(high_ref, low_ref, *refs):
    blocks, (out_ref, both) = refs[:-2], refs[-2:]
    _, nodes, slots, _ = blocks[0].shape
    rows = nodes * slots

    @pl.when(pl.program_id(0) == 0)
    def _():
        me, _ = position(len(blocks) // 2)
        for d, block in enumerate(blocks):
            columns = pl.ds(pl.multiple_of((me ^ d) * LANES, LANES), LANES)
            values = block[0].reshape(rows, LANES)
            high = values.astype(jnp.bfloat16)
            both[0:rows, columns] = high
            both[rows : 2 * rows, columns] = (values - high.astype(jnp.float32)).astype(jnp.bfloat16)

    first = jnp.dot(both[...], high_ref[...], preferred_element_type=jnp.float32)
    second = jnp.dot(both[0:rows, :], low_ref[...], preferred_element_type=jnp.float32)
    out_ref[...] = (first[0:rows, :] + (first[rows : 2 * rows, :] + second)).reshape(out_ref.shape)


def inverse(blocks, high, low):
    _, nodes, slots, _ = blocks[0].shape
    depth = high.shape[0] * LANES
    width = 256
    table = pl.BlockSpec((depth, width), lambda i: (0, i))
    return pl.pallas_call(
        inverse_kernel,
        grid=(LAGS // width,),
        in_specs=[table, table]
        + [pl.BlockSpec((1, nodes, slots, LANES), lambda i, j=d % 2: (j, 0, 0, 0)) for d in range(len(blocks))],
        out_specs=pl.BlockSpec((nodes, slots, width), lambda i: (0, 0, i)),
        out_shape=jax.ShapeDtypeStruct((nodes, slots, LAGS), jnp.float32),
        scratch_shapes=[pltpu.VMEM((2 * nodes * slots, depth), jnp.bfloat16)],
        compiler_params=pltpu.CompilerParams(vmem_limit_bytes=12 * MIB),
        name="inverse",
    )(high.reshape(depth, LAGS), low.reshape(depth, LAGS), *blocks)


def per_device(traces, taps, neighbours, valid, *, pairs, wins):
    windows, nodes, samples = traces.shape
    parts = 2 * wins
    place = lax.axis_index("pairs")
    win = lax.axis_index("win")

    def hop(array, d):
        pairing = [
            (i, ((i // wins) ^ (d // wins)) * wins + ((i % wins) ^ (d % wins))) for i in range(pairs * wins)
        ]
        return lax.ppermute(array, ("pairs", "win"), pairing)

    def between_chips(blocks):
        return [hop(block, 2 * s) if s else block for s, block in enumerate(blocks)]

    def within_chip(moved):
        return [x for block in moved for x in (block, hop(block, 1))]

    rows, taps = traces.reshape(windows * nodes, samples), taps.reshape(1, TAPS)
    steps = tuple(range(wins))[::-1]
    partner_rows = hop(rows, 1)
    found = own_spectra(rows, taps, nodes, steps)
    found, neighbours, valid = lax.optimization_barrier((found, neighbours, valid))

    _, is_first = position(wins)
    tile, member = neighbours // nodes, neighbours % nodes
    inside = tile // 2 == place // 2
    leading = 1 - (place // 2) % 2
    block = jnp.where(inside, jnp.where(tile % 2 == leading, 0, 1), jnp.where(is_first, 2, 3))
    code = jnp.where(valid != 0, block * nodes + member, -1)
    other = lax.ppermute(code, "pairs", [(i, i ^ 1) for i in range(pairs)])
    codes = jnp.where(is_first, jnp.concatenate([code, other], 0), jnp.concatenate([other, code], 0))
    for bit in (1 << k for k in range((wins - 1).bit_length())):
        split = codes.reshape(2 * nodes, wins // (2 * bit), 2, -1)
        codes = jnp.where(win & bit != 0, split[:, :, ::-1], split)
    codes = codes.reshape(2 * nodes, -1)
    columns = jnp.arange(8 * nodes, dtype=jnp.int32) % (4 * nodes)
    select = (codes[:, :, None] == columns[None, None, :]).astype(jnp.bfloat16)

    factor = 1.0 / math.sqrt(BINS * windows * wins)
    high, low = make_lag_tables(parts, factor)

    swap_a = [(i, i ^ 2) for i in range(pairs) if (i ^ 2) < pairs]
    swap_b = [(i, j) for i in range(2, pairs) for j in [((i - 2) ^ 2) + 2] if j < pairs]
    halves = []
    for half in range(HALVES):
        if half:
            found = own_spectra(partner_rows, taps, nodes, steps)
        a, b, turned = by_bin(between_chips([found[steps.index(s)] for s in range(wins)]))
        halves.append((a, b, turned, lax.ppermute(a, "pairs", swap_a), lax.ppermute(b, "pairs", swap_b)))
    stack = cross_products(halves, select, wins)
    return inverse(within_chip(between_chips(stack)), high, low)


def solution(mesh):
    placed = (P("win", "pairs", None), P(), P("pairs", None), P("pairs", None))
    body = functools.partial(per_device, pairs=mesh.shape["pairs"], wins=mesh.shape["win"])
    return jax.shard_map(
        body, mesh=mesh, in_specs=placed, out_specs=P("pairs", "win", None), check_vma=False
    )
```

```python
import functools
import math

import jax
import jax.numpy as jnp
import numpy as np
from jax import lax
from jax.experimental import pallas as pl
from jax.experimental.pallas import tpu as pltpu
from jax.sharding import PartitionSpec as P

SAMPLES = 4096
BINS = 512
BAND = 64
LOW_BIN = 64
LAGS = 1024
TAPS = 129
LANES = 2 * BAND
EPSILON = 1e-06
STEP = 64
CHUNK = 512
HALVES = 2
PITCH = LANES + 8
MIB = 1024 * 1024
CONTRACT_LAST = (((1,), (1,)), ((), ()))


def unit_circle(products):
    angles = (products % SAMPLES).astype(np.float64) * (2.0 * math.pi / SAMPLES)
    return np.cos(angles).astype(np.float32), (-np.sin(angles)).astype(np.float32)


def banded(first, second):
    rows = first.shape[0]
    parts = [a.reshape(rows, BINS // BAND, 1, BAND) for a in (first, second)]
    return np.concatenate(parts, 2).reshape(rows, 2 * BINS)


def forward_tables():
    bins = LOW_BIN + np.arange(BINS, dtype=np.int64)
    cos, msin = unit_circle(np.arange(TAPS, dtype=np.int64)[:, None] * bins[None, :])
    fine = banded(cos, msin)
    starts = np.arange(0, SAMPLES, STEP, dtype=np.int64)
    cos, msin = unit_circle(starts[:, None] * bins[None, :])
    return fine, banded(cos, cos), banded(-msin, msin)


def lag_tables(parts):
    lags = np.arange(LAGS, dtype=np.int64) - LAGS // 2
    cos, msin = unit_circle(np.arange(BAND, dtype=np.int64)[:, None] * lags[None, :])
    first = LOW_BIN + BAND * np.arange(parts, dtype=np.int64)
    cos0, msin0 = unit_circle(first[:, None] * lags[None, :])
    return cos, msin, cos0, msin0


def position(wins):
    place = lax.axis_index("pairs")
    me = (place % 2) * wins + lax.axis_index("win")
    return me, place % 2 != (place // 2) % 2


def spectra_kernel(x_hbm, taps_ref, fine_hbm, turn_c_hbm, turn_s_hbm, *refs, steps, wins):
    outs, refs = refs[: len(steps)], refs[len(steps) :]
    x_ref, fine_ref, turn_c_ref, turn_s_ref, *refs, sems = refs
    tables, totals, stages = refs[0:2], refs[2:4], refs[4:6]
    count = x_ref.shape[0]
    nodes, windows = outs[0].shape[0], outs[0].shape[1]
    width = 2 * LANES
    pitch = stages[0].shape[1] // windows
    pieces = SAMPLES // CHUNK
    me, _ = position(wins)
    copies = [
        pltpu.make_async_copy(source, target, sems.at[pieces + i])
        for i, (source, target) in enumerate(
            ((fine_hbm, fine_ref), (turn_c_hbm, turn_c_ref), (turn_s_hbm, turn_s_ref))
        )
    ]
    chunks = [
        pltpu.make_async_copy(
            x_hbm.at[:, pl.ds(i * CHUNK, CHUNK)], x_ref.at[:, pl.ds(i * CHUNK, CHUNK)], sems.at[i]
        )
        for i in range(pieces)
    ]
    for copy in copies + chunks:
        copy.start()

    def columns_of(i):
        return [pl.ds(pl.multiple_of((me ^ (2 * step)) * LANES, LANES), LANES) for step in steps[2 * i : 2 * i + 2]]

    def generate(i):
        for c, columns in enumerate(columns_of(i)):
            base = fine_ref[0:STEP, columns]
            swapped = pltpu.roll(base, BAND, 1)
            for j in range(SAMPLES // STEP):
                row = pl.ds(j, 1)
                turned = base * turn_c_ref[row, columns] + swapped * turn_s_ref[row, columns]
                tables[i % 2][j * STEP : (j + 1) * STEP, c * LANES : (c + 1) * LANES] = turned.astype(jnp.bfloat16)

    low = lax.broadcasted_iota(jnp.int32, (1, LANES), 1) < BAND
    responses = {}

    def respond(i):
        responses[i] = []
        for columns in columns_of(i):
            here = jnp.dot(
                taps_ref[:, 0:128],
                fine_ref[0:128, columns],
                precision=lax.Precision.HIGHEST,
                preferred_element_type=jnp.float32,
            )
            here = here + taps_ref[:, 128:129] * fine_ref[128:129, columns]
            other = pltpu.roll(jnp.broadcast_to(here, (8, LANES)), BAND, 1)[0:1, :]
            responses[i].append((jnp.where(low, here, other), jnp.where(low, -other, here)))

    row = lax.broadcasted_iota(jnp.int32, (width, width), 0)
    same_band = (row // LANES) == (lax.broadcasted_iota(jnp.int32, (width, width), 1) // LANES)
    summing = same_band.astype(jnp.bfloat16)

    def whiten(i):
        raw = jnp.concatenate([totals[i % 2][c] for c in range(2)], 1)
        square = raw * raw
        high = square.astype(jnp.bfloat16)
        rest = (square - high.astype(jnp.float32)).astype(jnp.bfloat16)
        sums = jnp.dot(jnp.concatenate([high, rest], 0), summing, preferred_element_type=jnp.float32)
        white = raw * lax.rsqrt((sums[0:count, :] + sums[count:, :]) * (1.0 / BAND) + EPSILON)
        for c, (same, cross) in enumerate(responses[i]):
            part = white[:, c * LANES : (c + 1) * LANES]
            turned = part * same + pltpu.roll(part, BAND, 1) * cross
            for window in range(windows):
                stages[i % 2][c, window * pitch : window * pitch + nodes, :] = turned[window * nodes : (window + 1) * nodes]

    def give(i):
        for c in range(2):
            for node in range(nodes):
                values = stages[i % 2][c, pl.ds(node, windows, stride=pitch), :]
                outs[2 * i + c][node] = values.astype(jnp.bfloat16)

    for copy in copies:
        copy.wait()
    generate(0)
    last = len(steps) // 2 - 1
    for copy in chunks:
        copy.wait()
    for i in range(len(steps) // 2):
        respond(i)
        product = jnp.dot(x_ref[...], tables[i % 2][...], preferred_element_type=jnp.float32)
        for c in range(2):
            totals[i % 2][c] = product[:, c * LANES : (c + 1) * LANES]
        if i < last:
            generate(i + 1)
        if i > 0:
            whiten(i - 1)
        if i > 1:
            give(i - 2)
    if last > 0:
        give(last - 1)
    whiten(last)
    give(last)


def own_spectra(rows, taps, nodes, steps):
    tables = [jnp.asarray(t) for t in forward_tables()]
    count = rows.shape[0]
    hbm = pl.BlockSpec(memory_space=pltpu.HBM)
    vmem = pl.BlockSpec(memory_space=pltpu.VMEM)
    shape = jax.ShapeDtypeStruct((nodes, count // nodes, LANES), jnp.bfloat16)
    return pl.pallas_call(
        functools.partial(spectra_kernel, steps=steps, wins=len(steps)),
        in_specs=[hbm, vmem, hbm, hbm, hbm],
        out_specs=[vmem] * len(steps),
        out_shape=[shape] * len(steps),
        scratch_shapes=[
            pltpu.VMEM(rows.shape, jnp.bfloat16),
            *[pltpu.VMEM(t.shape, jnp.float32) for t in tables],
            *[pltpu.VMEM((SAMPLES, 2 * LANES), jnp.bfloat16)] * 2,
            *[pltpu.VMEM((2, count, LANES), jnp.float32)] * 2,
            *[pltpu.VMEM((2, (nodes + 8) * (count // nodes), LANES), jnp.float32)] * 2,
            pltpu.SemaphoreType.DMA((SAMPLES // CHUNK + 3,)),
        ],
        compiler_params=pltpu.CompilerParams(vmem_limit_bytes=60 * MIB),
        cost_estimate=pl.CostEstimate(
            flops=2 * len(steps) * count * SAMPLES * LANES, bytes_accessed=2 * count * SAMPLES, transcendentals=0
        ),
        name="own_spectra",
    )(rows, taps, *tables)


def lag_table_kernel(cos_ref, msin_ref, cos0_ref, msin0_ref, high_ref, low_ref, *, factor):
    part = pl.program_id(0)
    c0 = cos0_ref[pl.ds(part, 1), :] * factor
    s0 = msin0_ref[pl.ds(part, 1), :] * factor
    cos, msin = cos_ref[...], msin_ref[...]
    for half, values in ((0, cos * c0 - msin * s0), (1, cos * s0 + msin * c0)):
        high = values.astype(jnp.bfloat16)
        rows = pl.ds(half * BAND, BAND)
        high_ref[0, rows, :] = high
        low_ref[0, rows, :] = (values - high.astype(jnp.float32)).astype(jnp.bfloat16)


def make_lag_tables(parts, factor):
    tables = [jnp.asarray(t) for t in lag_tables(parts)]
    shape = jax.ShapeDtypeStruct((parts, LANES, LAGS), jnp.bfloat16)
    block = pl.BlockSpec((1, LANES, LAGS), lambda i: (i, 0, 0))
    return pl.pallas_call(
        functools.partial(lag_table_kernel, factor=factor),
        grid=(parts,),
        in_specs=[pl.BlockSpec(t.shape, lambda i: (0, 0)) for t in tables],
        out_specs=[block, block],
        out_shape=[shape, shape],
        compiler_params=pltpu.CompilerParams(vmem_limit_bytes=6 * MIB),
        name="lag_tables",
    )(*tables)


def by_bin_kernel(*refs, steps):
    blocks, refs = refs[:steps], refs[steps:]
    first_ref, second_ref, turned_ref, turned, near, sem = refs
    nodes, windows = near.shape[0], near.shape[1]
    _, is_first = position(steps)
    own_at = jnp.where(is_first, 0, 1)
    copy = pltpu.make_async_copy(blocks[0], near, sem)
    copy.start()
    row = lax.broadcasted_iota(jnp.int32, (LANES, LANES), 0)
    unit = (row == lax.broadcasted_iota(jnp.int32, (LANES, LANES), 1)).astype(jnp.bfloat16)
    for tile in (1, 0):
        here = [near if s == 0 else blocks[s] for s in range(tile * steps // 2, (tile + 1) * steps // 2)]
        if tile == 0:
            copy.wait()

        def turn(node, _, here=here, tile=tile):
            values = jnp.concatenate([block[node] for block in here] * 2, 0)
            values = lax.dot_general(unit, values, CONTRACT_LAST, preferred_element_type=jnp.float32)
            turned[pl.ds(pl.multiple_of((tile * nodes + node) * PITCH, 8), LANES), :] = values
            return 0

        lax.fori_loop(0, nodes, turn, 0, unroll=16)
    left = lax.broadcasted_iota(jnp.int32, (nodes, LANES), 1) < LANES // 2
    for which, (out_ref, tile) in enumerate(((first_ref, own_at), (second_ref, 1 - own_at))):
        start = tile * (nodes * PITCH)

        def one(f, _, out_ref=out_ref, start=start, which=which):
            real = turned[pl.ds(start + f, nodes, stride=PITCH), :]
            imag = turned[pl.ds(start + BAND + f, nodes, stride=PITCH), :]
            out_ref[f] = jnp.where(left, real, imag).astype(jnp.bfloat16)
            turned_ref[f, which * nodes : (which + 1) * nodes, :] = jnp.where(left, imag, -real).astype(jnp.bfloat16)
            return 0

        lax.fori_loop(0, BAND, one, 0, unroll=16)


def by_bin(blocks):
    nodes, windows, _ = blocks[0].shape
    steps = len(blocks)
    shape = jax.ShapeDtypeStruct((BAND, nodes, LANES), jnp.bfloat16)
    vmem = pl.BlockSpec(memory_space=pltpu.VMEM)
    return pl.pallas_call(
        functools.partial(by_bin_kernel, steps=steps),
        out_shape=[shape, shape, jax.ShapeDtypeStruct((BAND, 2 * nodes, LANES), jnp.bfloat16)],
        in_specs=[pl.BlockSpec(memory_space=pl.ANY)] + [vmem] * (len(blocks) - 1),
        out_specs=[vmem] * 3,
        scratch_shapes=[
            pltpu.VMEM((2 * nodes * PITCH, LANES), jnp.float32),
            pltpu.VMEM((nodes, windows, LANES), jnp.bfloat16),
            pltpu.SemaphoreType.DMA,
        ],
        compiler_params=pltpu.CompilerParams(vmem_limit_bytes=8 * MIB),
        cost_estimate=pl.CostEstimate(flops=1 << 31, bytes_accessed=1 << 22, transcendentals=0),
        name="by_bin",
    )(*blocks)


def cross_kernel(*refs):
    halves = [refs[5 * h : 5 * h + 5] for h in range(HALVES)]
    select_ref, *outs, cross = refs[5 * HALVES :]
    nodes = halves[0][0].shape[1]
    slots = outs[0].shape[2]
    stations, count = 2 * nodes, 4 * nodes
    pitch = count + 8

    def one_bin(f, _):
        wide = lambda k: jnp.concatenate([half[k][f] for half in halves], 1)
        own = jnp.concatenate([wide(0), wide(1)], 0)
        both = jnp.concatenate([own, wide(2)], 0)
        partners = jnp.concatenate([own, wide(3), wide(4)] * 2, 0)
        cross[pl.ds(pl.multiple_of(f * pitch, 8), count), :] = lax.dot_general(
            both, partners, CONTRACT_LAST, preferred_element_type=jnp.float32
        )
        return 0

    lax.fori_loop(0, BAND, one_bin, 0, unroll=8)
    _, is_first = position(len(outs))
    own_at = jnp.where(is_first, 0, 1)
    left = lax.broadcasted_iota(jnp.int32, (2 * BAND, 2 * count), 1) < count
    tiles = (outs[: len(outs) // 2], own_at), (outs[len(outs) // 2 :], 1 - own_at)
    for shares, where in tiles:

        def one_node(node, _, shares=shares, where=where):
            index = where * nodes + node
            real = cross[pl.ds(index, BAND, stride=pitch), :]
            imag = cross[pl.ds(stations + index, BAND, stride=pitch), :]
            values = jnp.concatenate([real, imag], 0)
            high = values.astype(jnp.bfloat16).astype(jnp.float32)
            split = jnp.where(left, high, values - high).astype(jnp.bfloat16)
            picked = lax.dot_general(select_ref[index], split, CONTRACT_LAST, preferred_element_type=jnp.float32)
            for d in range(2 * len(shares)):
                shares[d // 2][d % 2, node] = picked[d * slots : (d + 1) * slots, :]
            return 0

        lax.fori_loop(0, nodes, one_node, 0, unroll=8)


def cross_products(halves, select, wins):
    nodes = halves[0][0].shape[1]
    block = jax.ShapeDtypeStruct((2, nodes, select.shape[1] // wins, LANES), jnp.float32)
    vmem = pl.BlockSpec(memory_space=pltpu.VMEM)
    operands = [x for half in halves for x in half]
    return pl.pallas_call(
        cross_kernel,
        out_shape=[block] * wins,
        in_specs=[vmem] * (len(operands) + 1),
        out_specs=[vmem] * wins,
        scratch_shapes=[pltpu.VMEM((BAND * (4 * nodes + 8), 8 * nodes), jnp.float32)],
        compiler_params=pltpu.CompilerParams(vmem_limit_bytes=12 * MIB),
        name="cross_products",
    )(*operands, select)


def inverse_kernel(high_ref, low_ref, *refs, far, wins):
    *refs, out_ref, both = refs
    blocks, before = refs[:wins], refs[wins:]
    _, nodes, slots, _ = blocks[0].shape
    rows, depth = nodes * slots, both.shape[1]
    me, _ = position(wins)

    @pl.when(pl.program_id(0) == 0)
    def _():
        for d, block in enumerate(blocks):
            columns = pl.ds(pl.multiple_of(((me ^ d) % wins) * LANES, LANES), LANES)
            values = block[0].reshape(rows, LANES)
            high = values.astype(jnp.bfloat16)
            both[0:rows, columns] = high
            both[rows : 2 * rows, columns] = (values - high.astype(jnp.float32)).astype(jnp.bfloat16)

    here = pl.ds(pl.multiple_of(((me // wins) ^ far) * depth, depth), depth)
    first = jnp.dot(both[...], high_ref[here, :], preferred_element_type=jnp.float32)
    second = jnp.dot(both[0:rows, :], low_ref[here, :], preferred_element_type=jnp.float32)
    total = (first[0:rows, :] + (first[rows : 2 * rows, :] + second)).reshape(out_ref.shape)
    for ref in before:
        total = total + ref[...]
    out_ref[...] = total


def inverse(blocks, high, low, far, before):
    _, nodes, slots, _ = blocks[0].shape
    wins = len(blocks)
    depth = high.shape[0] * LANES
    width = 256
    table = pl.BlockSpec((depth, width), lambda i: (0, i))
    lags = pl.BlockSpec((nodes, slots, width), lambda i: (0, 0, i))
    return pl.pallas_call(
        functools.partial(inverse_kernel, far=far, wins=wins),
        grid=(LAGS // width,),
        in_specs=[table, table]
        + [pl.BlockSpec((1, nodes, slots, LANES), lambda i, j=d % 2: (j, 0, 0, 0)) for d in range(wins)]
        + [lags] * len(before),
        out_specs=lags,
        out_shape=jax.ShapeDtypeStruct((nodes, slots, LAGS), jnp.float32),
        scratch_shapes=[pltpu.VMEM((2 * nodes * slots, wins * LANES), jnp.bfloat16)],
        compiler_params=pltpu.CompilerParams(vmem_limit_bytes=12 * MIB),
        cost_estimate=pl.CostEstimate(flops=1 << 31, bytes_accessed=1 << 22, transcendentals=0),
        name="inverse",
    )(high.reshape(depth, LAGS), low.reshape(depth, LAGS), *blocks, *before)


def per_device(traces, taps, neighbours, valid, *, pairs, wins):
    windows, nodes, samples = traces.shape
    parts = 2 * wins
    place = lax.axis_index("pairs")
    win = lax.axis_index("win")

    def hop(array, d):
        pairing = [
            (i, ((i // wins) ^ (d // wins)) * wins + ((i % wins) ^ (d % wins))) for i in range(pairs * wins)
        ]
        return lax.ppermute(array, ("pairs", "win"), pairing)

    def between_chips(blocks):
        return [hop(block, 2 * s) if s else block for s, block in enumerate(blocks)]

    def within_chip(moved):
        return [x for block in moved for x in (block, hop(block, 1))]

    rows, taps = traces.reshape(windows * nodes, samples), taps.reshape(1, TAPS)
    steps = tuple(range(wins))[::-1]
    partner_rows = hop(rows, 1)
    found = own_spectra(rows, taps, nodes, steps)
    found, neighbours, valid = lax.optimization_barrier((found, neighbours, valid))

    _, is_first = position(wins)
    tile, member = neighbours // nodes, neighbours % nodes
    inside = tile // 2 == place // 2
    leading = 1 - (place // 2) % 2
    block = jnp.where(inside, jnp.where(tile % 2 == leading, 0, 1), jnp.where(is_first, 2, 3))
    code = jnp.where(valid != 0, block * nodes + member, -1)
    other = lax.ppermute(code, "pairs", [(i, i ^ 1) for i in range(pairs)])
    codes = jnp.where(is_first, jnp.concatenate([code, other], 0), jnp.concatenate([other, code], 0))
    for bit in (1 << k for k in range((wins - 1).bit_length())):
        split = codes.reshape(2 * nodes, wins // (2 * bit), 2, -1)
        codes = jnp.where(win & bit != 0, split[:, :, ::-1], split)
    codes = codes.reshape(2 * nodes, -1)
    columns = jnp.arange(8 * nodes, dtype=jnp.int32) % (4 * nodes)
    select = (codes[:, :, None] == columns[None, None, :]).astype(jnp.bfloat16)

    factor = 1.0 / math.sqrt(BINS * windows * wins)
    high, low = make_lag_tables(parts, factor)

    swap_a = [(i, i ^ 2) for i in range(pairs) if (i ^ 2) < pairs]
    swap_b = [(i, j) for i in range(2, pairs) for j in [((i - 2) ^ 2) + 2] if j < pairs]
    halves = []
    for half in range(HALVES):
        if half:
            found = own_spectra(partner_rows, taps, nodes, steps)
        blocks = between_chips([found[steps.index(s)] for s in range(wins)])
        a, b, turned = by_bin(blocks)
        halves.append((a, b, turned, lax.ppermute(a, "pairs", swap_a), lax.ppermute(b, "pairs", swap_b)))
    stack = cross_products(halves, select, wins)
    blocks = within_chip(between_chips(stack))
    total = inverse(blocks[:wins], high, low, 0, [])
    return inverse(blocks[wins:], high, low, 1, [total])


def solution(mesh):
    placed = (P("win", "pairs", None), P(), P("pairs", None), P("pairs", None))
    body = functools.partial(per_device, pairs=mesh.shape["pairs"], wins=mesh.shape["win"])
    return jax.shard_map(
        body, mesh=mesh, in_specs=placed, out_specs=P("pairs", "win", None), check_vma=False
    )
```

```python
import functools
import math

import jax
import jax.numpy as jnp
import numpy as np
from jax import lax
from jax.experimental import pallas as pl
from jax.experimental.pallas import tpu as pltpu
from jax.sharding import PartitionSpec as P

SAMPLES = 4096
BINS = 512
BAND = 64
LOW_BIN = 64
LAGS = 1024
TAPS = 129
LANES = 2 * BAND
EPSILON = 1e-06
STEP = 64
CHUNK = 512
HALVES = 2
PITCH = LANES + 8
MIB = 1024 * 1024
CONTRACT_LAST = (((1,), (1,)), ((), ()))


def unit_circle(products):
    angles = (products % SAMPLES).astype(np.float64) * (2.0 * math.pi / SAMPLES)
    return np.cos(angles).astype(np.float32), (-np.sin(angles)).astype(np.float32)


def banded(first, second):
    rows = first.shape[0]
    parts = [a.reshape(rows, BINS // BAND, 1, BAND) for a in (first, second)]
    return np.concatenate(parts, 2).reshape(rows, 2 * BINS)


def forward_tables():
    bins = LOW_BIN + np.arange(BINS, dtype=np.int64)
    cos, msin = unit_circle(np.arange(TAPS, dtype=np.int64)[:, None] * bins[None, :])
    fine = banded(cos, msin)
    starts = np.arange(0, SAMPLES, STEP, dtype=np.int64)
    cos, msin = unit_circle(starts[:, None] * bins[None, :])
    return fine, banded(cos, cos), banded(-msin, msin)


def lag_tables(parts):
    lags = np.arange(LAGS, dtype=np.int64) - LAGS // 2
    cos, msin = unit_circle(np.arange(BAND, dtype=np.int64)[:, None] * lags[None, :])
    first = LOW_BIN + BAND * np.arange(parts, dtype=np.int64)
    cos0, msin0 = unit_circle(first[:, None] * lags[None, :])
    return cos, msin, cos0, msin0


def position(wins):
    place = lax.axis_index("pairs")
    me = (place % 2) * wins + lax.axis_index("win")
    return me, place % 2 != (place // 2) % 2


def spectra_kernel(x_hbm, taps_ref, fine_hbm, turn_c_hbm, turn_s_hbm, *refs, steps, wins):
    outs, refs = refs[: len(steps)], refs[len(steps) :]
    x_ref, fine_ref, turn_c_ref, turn_s_ref, *refs, sems = refs
    tables, totals, stages = refs[0:2], refs[2:4], refs[4:6]
    count = x_ref.shape[0]
    nodes, windows = outs[0].shape[0], outs[0].shape[1]
    width = 2 * LANES
    pitch = stages[0].shape[1] // windows
    pieces = SAMPLES // CHUNK
    me, _ = position(wins)
    copies = [
        pltpu.make_async_copy(source, target, sems.at[pieces + i])
        for i, (source, target) in enumerate(
            ((fine_hbm, fine_ref), (turn_c_hbm, turn_c_ref), (turn_s_hbm, turn_s_ref))
        )
    ]
    chunks = [
        pltpu.make_async_copy(
            x_hbm.at[:, pl.ds(i * CHUNK, CHUNK)], x_ref.at[:, pl.ds(i * CHUNK, CHUNK)], sems.at[i]
        )
        for i in range(pieces)
    ]
    for copy in copies + chunks:
        copy.start()

    def columns_of(i):
        return [pl.ds(pl.multiple_of((me ^ (2 * step)) * LANES, LANES), LANES) for step in steps[2 * i : 2 * i + 2]]

    def generate(i):
        for c, columns in enumerate(columns_of(i)):
            base = fine_ref[0:STEP, columns]
            swapped = pltpu.roll(base, BAND, 1)
            for j in range(SAMPLES // STEP):
                row = pl.ds(j, 1)
                turned = base * turn_c_ref[row, columns] + swapped * turn_s_ref[row, columns]
                tables[i % 2][j * STEP : (j + 1) * STEP, c * LANES : (c + 1) * LANES] = turned.astype(jnp.bfloat16)

    low = lax.broadcasted_iota(jnp.int32, (1, LANES), 1) < BAND
    responses = {}

    def respond(i):
        responses[i] = []
        for columns in columns_of(i):
            here = jnp.dot(
                taps_ref[:, 0:128],
                fine_ref[0:128, columns],
                precision=lax.Precision.HIGHEST,
                preferred_element_type=jnp.float32,
            )
            here = here + taps_ref[:, 128:129] * fine_ref[128:129, columns]
            other = pltpu.roll(jnp.broadcast_to(here, (8, LANES)), BAND, 1)[0:1, :]
            responses[i].append((jnp.where(low, here, other), jnp.where(low, -other, here)))

    row = lax.broadcasted_iota(jnp.int32, (width, width), 0)
    same_band = (row // LANES) == (lax.broadcasted_iota(jnp.int32, (width, width), 1) // LANES)
    summing = same_band.astype(jnp.bfloat16)

    def whiten(i):
        raw = jnp.concatenate([totals[i % 2][c] for c in range(2)], 1)
        square = raw * raw
        high = square.astype(jnp.bfloat16)
        rest = (square - high.astype(jnp.float32)).astype(jnp.bfloat16)
        sums = jnp.dot(jnp.concatenate([high, rest], 0), summing, preferred_element_type=jnp.float32)
        white = raw * lax.rsqrt((sums[0:count, :] + sums[count:, :]) * (1.0 / BAND) + EPSILON)
        for c, (same, cross) in enumerate(responses[i]):
            part = white[:, c * LANES : (c + 1) * LANES]
            turned = part * same + pltpu.roll(part, BAND, 1) * cross
            for window in range(windows):
                stages[i % 2][c, window * pitch : window * pitch + nodes, :] = turned[window * nodes : (window + 1) * nodes]

    def give(i):
        for c in range(2):
            for node in range(nodes):
                values = stages[i % 2][c, pl.ds(node, windows, stride=pitch), :]
                outs[2 * i + c][node] = values.astype(jnp.bfloat16)

    for copy in copies:
        copy.wait()
    generate(0)
    last = len(steps) // 2 - 1
    for copy in chunks:
        copy.wait()
    for i in range(len(steps) // 2):
        respond(i)
        product = jnp.dot(x_ref[...], tables[i % 2][...], preferred_element_type=jnp.float32)
        for c in range(2):
            totals[i % 2][c] = product[:, c * LANES : (c + 1) * LANES]
        if i < last:
            generate(i + 1)
        if i > 0:
            whiten(i - 1)
        if i > 1:
            give(i - 2)
    if last > 0:
        give(last - 1)
    whiten(last)
    give(last)


def own_spectra(rows, taps, nodes, steps):
    tables = [jnp.asarray(t) for t in forward_tables()]
    count = rows.shape[0]
    hbm = pl.BlockSpec(memory_space=pltpu.HBM)
    vmem = pl.BlockSpec(memory_space=pltpu.VMEM)
    shape = jax.ShapeDtypeStruct((nodes, count // nodes, LANES), jnp.bfloat16)
    return pl.pallas_call(
        functools.partial(spectra_kernel, steps=steps, wins=len(steps)),
        in_specs=[hbm, vmem, hbm, hbm, hbm],
        out_specs=[vmem] * len(steps),
        out_shape=[shape] * len(steps),
        scratch_shapes=[
            pltpu.VMEM(rows.shape, jnp.bfloat16),
            *[pltpu.VMEM(t.shape, jnp.float32) for t in tables],
            *[pltpu.VMEM((SAMPLES, 2 * LANES), jnp.bfloat16)] * 2,
            *[pltpu.VMEM((2, count, LANES), jnp.float32)] * 2,
            *[pltpu.VMEM((2, (nodes + 8) * (count // nodes), LANES), jnp.float32)] * 2,
            pltpu.SemaphoreType.DMA((SAMPLES // CHUNK + 3,)),
        ],
        compiler_params=pltpu.CompilerParams(vmem_limit_bytes=60 * MIB),
        cost_estimate=pl.CostEstimate(
            flops=2 * len(steps) * count * SAMPLES * LANES, bytes_accessed=2 * count * SAMPLES, transcendentals=0
        ),
        name="own_spectra",
    )(rows, taps, *tables)


def lag_table_kernel(cos_ref, msin_ref, cos0_ref, msin0_ref, high_ref, low_ref, *, factor):
    part = pl.program_id(0)
    c0 = cos0_ref[pl.ds(part, 1), :] * factor
    s0 = msin0_ref[pl.ds(part, 1), :] * factor
    cos, msin = cos_ref[...], msin_ref[...]
    for half, values in ((0, cos * c0 - msin * s0), (1, cos * s0 + msin * c0)):
        high = values.astype(jnp.bfloat16)
        rows = pl.ds(half * BAND, BAND)
        high_ref[0, rows, :] = high
        low_ref[0, rows, :] = (values - high.astype(jnp.float32)).astype(jnp.bfloat16)


def make_lag_tables(parts, factor):
    tables = [jnp.asarray(t) for t in lag_tables(parts)]
    shape = jax.ShapeDtypeStruct((parts, LANES, LAGS), jnp.bfloat16)
    block = pl.BlockSpec((1, LANES, LAGS), lambda i: (i, 0, 0))
    return pl.pallas_call(
        functools.partial(lag_table_kernel, factor=factor),
        grid=(parts,),
        in_specs=[pl.BlockSpec(t.shape, lambda i: (0, 0)) for t in tables],
        out_specs=[block, block],
        out_shape=[shape, shape],
        compiler_params=pltpu.CompilerParams(vmem_limit_bytes=6 * MIB),
        name="lag_tables",
    )(*tables)


def by_bin_kernel(*refs, steps):
    blocks, refs = refs[:steps], refs[steps:]
    first_ref, second_ref, turned_ref, turned, near, sem = refs
    nodes, windows = near.shape[0], near.shape[1]
    _, is_first = position(steps)
    own_at = jnp.where(is_first, 0, 1)
    copy = pltpu.make_async_copy(blocks[0], near, sem)
    copy.start()
    row = lax.broadcasted_iota(jnp.int32, (LANES, LANES), 0)
    unit = (row == lax.broadcasted_iota(jnp.int32, (LANES, LANES), 1)).astype(jnp.bfloat16)
    for tile in (1, 0):
        here = [near if s == 0 else blocks[s] for s in range(tile * steps // 2, (tile + 1) * steps // 2)]
        if tile == 0:
            copy.wait()

        def turn(node, _, here=here, tile=tile):
            values = jnp.concatenate([block[node] for block in here] * 2, 0)
            values = lax.dot_general(unit, values, CONTRACT_LAST, preferred_element_type=jnp.float32)
            turned[pl.ds(pl.multiple_of((tile * nodes + node) * PITCH, 8), LANES), :] = values
            return 0

        lax.fori_loop(0, nodes, turn, 0, unroll=16)
    left = lax.broadcasted_iota(jnp.int32, (nodes, LANES), 1) < LANES // 2
    for which, (out_ref, tile) in enumerate(((first_ref, own_at), (second_ref, 1 - own_at))):
        start = tile * (nodes * PITCH)

        def one(f, _, out_ref=out_ref, start=start, which=which):
            real = turned[pl.ds(start + f, nodes, stride=PITCH), :]
            imag = turned[pl.ds(start + BAND + f, nodes, stride=PITCH), :]
            out_ref[f] = jnp.where(left, real, imag).astype(jnp.bfloat16)
            turned_ref[f, which * nodes : (which + 1) * nodes, :] = jnp.where(left, imag, -real).astype(jnp.bfloat16)
            return 0

        lax.fori_loop(0, BAND, one, 0, unroll=16)


def by_bin(blocks):
    nodes, windows, _ = blocks[0].shape
    steps = len(blocks)
    shape = jax.ShapeDtypeStruct((BAND, nodes, LANES), jnp.bfloat16)
    vmem = pl.BlockSpec(memory_space=pltpu.VMEM)
    return pl.pallas_call(
        functools.partial(by_bin_kernel, steps=steps),
        out_shape=[shape, shape, jax.ShapeDtypeStruct((BAND, 2 * nodes, LANES), jnp.bfloat16)],
        in_specs=[pl.BlockSpec(memory_space=pl.ANY)] + [vmem] * (len(blocks) - 1),
        out_specs=[vmem] * 3,
        scratch_shapes=[
            pltpu.VMEM((2 * nodes * PITCH, LANES), jnp.float32),
            pltpu.VMEM((nodes, windows, LANES), jnp.bfloat16),
            pltpu.SemaphoreType.DMA,
        ],
        compiler_params=pltpu.CompilerParams(vmem_limit_bytes=8 * MIB),
        cost_estimate=pl.CostEstimate(flops=1 << 31, bytes_accessed=1 << 22, transcendentals=0),
        name="by_bin",
    )(*blocks)


def cross_kernel(*refs):
    halves = [refs[5 * h : 5 * h + 5] for h in range(HALVES)]
    select_ref, *outs, cross = refs[5 * HALVES :]
    nodes = halves[0][0].shape[1]
    slots = outs[0].shape[2]
    stations, count = 2 * nodes, 4 * nodes
    pitch = count + 8

    def one_bin(f, _):
        wide = lambda k: jnp.concatenate([half[k][f] for half in halves], 1)
        own = jnp.concatenate([wide(0), wide(1)], 0)
        both = jnp.concatenate([own, wide(2)], 0)
        partners = jnp.concatenate([own, wide(3), wide(4)] * 2, 0)
        cross[pl.ds(pl.multiple_of(f * pitch, 8), count), :] = lax.dot_general(
            both, partners, CONTRACT_LAST, preferred_element_type=jnp.float32
        )
        return 0

    lax.fori_loop(0, BAND, one_bin, 0, unroll=8)
    _, is_first = position(len(outs))
    own_at = jnp.where(is_first, 0, 1)
    left = lax.broadcasted_iota(jnp.int32, (2 * BAND, 2 * count), 1) < count
    tiles = (outs[: len(outs) // 2], own_at), (outs[len(outs) // 2 :], 1 - own_at)
    for shares, where in tiles:

        def one_node(node, _, shares=shares, where=where):
            index = where * nodes + node
            real = cross[pl.ds(index, BAND, stride=pitch), :]
            imag = cross[pl.ds(stations + index, BAND, stride=pitch), :]
            values = jnp.concatenate([real, imag], 0)
            high = values.astype(jnp.bfloat16).astype(jnp.float32)
            split = jnp.where(left, high, values - high).astype(jnp.bfloat16)
            picked = lax.dot_general(select_ref[index], split, CONTRACT_LAST, preferred_element_type=jnp.float32)
            for d in range(2 * len(shares)):
                shares[d // 2][d % 2, node] = picked[d * slots : (d + 1) * slots, :]
            return 0

        lax.fori_loop(0, nodes, one_node, 0, unroll=8)


def cross_products(halves, select, wins):
    nodes = halves[0][0].shape[1]
    block = jax.ShapeDtypeStruct((2, nodes, select.shape[1] // wins, LANES), jnp.float32)
    vmem = pl.BlockSpec(memory_space=pltpu.VMEM)
    operands = [x for half in halves for x in half]
    return pl.pallas_call(
        cross_kernel,
        out_shape=[block] * wins,
        in_specs=[vmem] * (len(operands) + 1),
        out_specs=[vmem] * wins,
        scratch_shapes=[pltpu.VMEM((BAND * (4 * nodes + 8), 8 * nodes), jnp.float32)],
        compiler_params=pltpu.CompilerParams(vmem_limit_bytes=12 * MIB),
        name="cross_products",
    )(*operands, select)


def inverse_kernel(high_ref, low_ref, *refs, far, wins):
    *refs, out_ref, both = refs
    blocks, before = refs[:wins], refs[wins:]
    _, nodes, slots, _ = blocks[0].shape
    rows, depth = nodes * slots, both.shape[1]
    me, _ = position(wins)

    @pl.when(pl.program_id(0) == 0)
    def _():
        for d, block in enumerate(blocks):
            columns = pl.ds(pl.multiple_of(((me ^ d) % wins) * LANES, LANES), LANES)
            values = block[0].reshape(rows, LANES)
            high = values.astype(jnp.bfloat16)
            both[0:rows, columns] = high
            both[rows : 2 * rows, columns] = (values - high.astype(jnp.float32)).astype(jnp.bfloat16)

    here = pl.ds(pl.multiple_of(((me // wins) ^ far) * depth, depth), depth)
    first = jnp.dot(both[...], high_ref[here, :], preferred_element_type=jnp.float32)
    second = jnp.dot(both[0:rows, :], low_ref[here, :], preferred_element_type=jnp.float32)
    total = (first[0:rows, :] + (first[rows : 2 * rows, :] + second)).reshape(out_ref.shape)
    for ref in before:
        total = total + ref[...]
    out_ref[...] = total


def inverse(blocks, high, low, far, before):
    _, nodes, slots, _ = blocks[0].shape
    wins = len(blocks)
    depth = high.shape[0] * LANES
    width = 256
    table = pl.BlockSpec((depth, width), lambda i: (0, i))
    lags = pl.BlockSpec((nodes, slots, width), lambda i: (0, 0, i))
    return pl.pallas_call(
        functools.partial(inverse_kernel, far=far, wins=wins),
        grid=(LAGS // width,),
        in_specs=[table, table]
        + [pl.BlockSpec((1, nodes, slots, LANES), lambda i, j=d % 2: (j, 0, 0, 0)) for d in range(wins)]
        + [lags] * len(before),
        out_specs=lags,
        out_shape=jax.ShapeDtypeStruct((nodes, slots, LAGS), jnp.float32),
        scratch_shapes=[pltpu.VMEM((2 * nodes * slots, wins * LANES), jnp.bfloat16)],
        compiler_params=pltpu.CompilerParams(vmem_limit_bytes=12 * MIB),
        cost_estimate=pl.CostEstimate(flops=1 << 31, bytes_accessed=1 << 22, transcendentals=0),
        name="inverse",
    )(high.reshape(depth, LAGS), low.reshape(depth, LAGS), *blocks, *before)


def per_device(traces, taps, neighbours, valid, *, pairs, wins):
    windows, nodes, samples = traces.shape
    parts = 2 * wins
    place = lax.axis_index("pairs")
    win = lax.axis_index("win")

    def hop(array, d):
        pairing = [
            (i, ((i // wins) ^ (d // wins)) * wins + ((i % wins) ^ (d % wins))) for i in range(pairs * wins)
        ]
        return lax.ppermute(array, ("pairs", "win"), pairing)

    def between_chips(blocks):
        return [hop(block, 2 * s) if s else block for s, block in enumerate(blocks)]

    def within_chip(moved):
        return [x for block in moved for x in (block, hop(block, 1))]

    rows, taps = traces.reshape(windows * nodes, samples), taps.reshape(1, TAPS)
    steps = tuple(range(wins))[::-1]
    partner_rows = hop(rows, 1)
    found = own_spectra(rows, taps, nodes, steps)
    found, neighbours, valid = lax.optimization_barrier((found, neighbours, valid))

    _, is_first = position(wins)
    tile, member = neighbours // nodes, neighbours % nodes
    inside = tile // 2 == place // 2
    leading = 1 - (place // 2) % 2
    block = jnp.where(inside, jnp.where(tile % 2 == leading, 0, 1), jnp.where(is_first, 2, 3))
    code = jnp.where(valid != 0, block * nodes + member, -1)
    other = lax.ppermute(code, "pairs", [(i, i ^ 1) for i in range(pairs)])
    codes = jnp.where(is_first, jnp.concatenate([code, other], 0), jnp.concatenate([other, code], 0))
    for bit in (1 << k for k in range((wins - 1).bit_length())):
        split = codes.reshape(2 * nodes, wins // (2 * bit), 2, -1)
        codes = jnp.where(win & bit != 0, split[:, :, ::-1], split)
    codes = codes.reshape(2 * nodes, -1)
    columns = jnp.arange(8 * nodes, dtype=jnp.int32) % (4 * nodes)
    select = (codes[:, :, None] == columns[None, None, :]).astype(jnp.bfloat16)

    factor = 1.0 / math.sqrt(BINS * windows * wins)
    high, low = make_lag_tables(parts, factor)

    swap_a = [(i, i ^ 2) for i in range(pairs) if (i ^ 2) < pairs]
    swap_b = [(i, j) for i in range(2, pairs) for j in [((i - 2) ^ 2) + 2] if j < pairs]
    halves = []
    for half in range(HALVES):
        if half:
            found = own_spectra(partner_rows, taps, nodes, steps)
        blocks = between_chips([found[steps.index(s)] for s in range(wins)])
        a, b, turned = by_bin(blocks)
        halves.append((a, b, turned, lax.ppermute(a, "pairs", swap_a), lax.ppermute(b, "pairs", swap_b)))
    stack = cross_products(halves, select, wins)
    moved = between_chips(stack)
    near, far = moved[: wins // 2], moved[wins // 2 :]
    near, high, low = lax.optimization_barrier((near, high, low))
    total = inverse(within_chip(near), high, low, 0, [])
    return inverse(within_chip(far), high, low, 1, [total])


def solution(mesh):
    placed = (P("win", "pairs", None), P(), P("pairs", None), P("pairs", None))
    body = functools.partial(per_device, pairs=mesh.shape["pairs"], wins=mesh.shape["win"])
    return jax.shard_map(
        body, mesh=mesh, in_specs=placed, out_specs=P("pairs", "win", None), check_vma=False
    )
```

```python
import functools
import math

import jax
import jax.numpy as jnp
import numpy as np
from jax import lax
from jax.experimental import pallas as pl
from jax.experimental.pallas import tpu as pltpu
from jax.sharding import PartitionSpec as P

SAMPLES = 4096
BINS = 512
BAND = 64
LOW_BIN = 64
LAGS = 1024
TAPS = 129
LANES = 2 * BAND
EPSILON = 1e-06
STEP = 64
CHUNK = 512
HALVES = 2
PITCH = LANES + 8
MIB = 1024 * 1024
CONTRACT_LAST = (((1,), (1,)), ((), ()))


def unit_circle(products):
    angles = (products % SAMPLES).astype(np.float64) * (2.0 * math.pi / SAMPLES)
    return np.cos(angles).astype(np.float32), (-np.sin(angles)).astype(np.float32)


def banded(first, second):
    rows = first.shape[0]
    parts = [a.reshape(rows, BINS // BAND, 1, BAND) for a in (first, second)]
    return np.concatenate(parts, 2).reshape(rows, 2 * BINS)


def forward_tables():
    bins = LOW_BIN + np.arange(BINS, dtype=np.int64)
    cos, msin = unit_circle(np.arange(TAPS, dtype=np.int64)[:, None] * bins[None, :])
    fine = banded(cos, msin)
    starts = np.arange(0, SAMPLES, STEP, dtype=np.int64)
    cos, msin = unit_circle(starts[:, None] * bins[None, :])
    return fine, banded(cos, cos), banded(-msin, msin)


def lag_tables(parts):
    lags = np.arange(LAGS, dtype=np.int64) - LAGS // 2
    cos, msin = unit_circle(np.arange(BAND, dtype=np.int64)[:, None] * lags[None, :])
    first = LOW_BIN + BAND * np.arange(parts, dtype=np.int64)
    cos0, msin0 = unit_circle(first[:, None] * lags[None, :])
    return cos, msin, cos0, msin0


def position(wins):
    place = lax.axis_index("pairs")
    me = (place % 2) * wins + lax.axis_index("win")
    return me, place % 2 != (place // 2) % 2


def spectra_kernel(x_hbm, taps_ref, fine_hbm, turn_c_hbm, turn_s_hbm, *refs, steps, wins):
    outs, refs = refs[: len(steps)], refs[len(steps) :]
    x_ref, fine_ref, turn_c_ref, turn_s_ref, *refs, sems = refs
    tables, totals, stages = refs[0:2], refs[2:4], refs[4:6]
    count = x_ref.shape[0]
    nodes, windows = outs[0].shape[0], outs[0].shape[1]
    width = 2 * LANES
    pitch = stages[0].shape[1] // windows
    pieces = SAMPLES // CHUNK
    me, _ = position(wins)
    copies = [
        pltpu.make_async_copy(source, target, sems.at[pieces + i])
        for i, (source, target) in enumerate(
            ((fine_hbm, fine_ref), (turn_c_hbm, turn_c_ref), (turn_s_hbm, turn_s_ref))
        )
    ]
    chunks = [
        pltpu.make_async_copy(
            x_hbm.at[:, pl.ds(i * CHUNK, CHUNK)], x_ref.at[:, pl.ds(i * CHUNK, CHUNK)], sems.at[i]
        )
        for i in range(pieces)
    ]
    for copy in copies + chunks:
        copy.start()

    def columns_of(i):
        return [pl.ds(pl.multiple_of((me ^ (2 * step)) * LANES, LANES), LANES) for step in steps[2 * i : 2 * i + 2]]

    def generate(i):
        for c, columns in enumerate(columns_of(i)):
            base = fine_ref[0:STEP, columns]
            swapped = pltpu.roll(base, BAND, 1)
            for j in range(SAMPLES // STEP):
                row = pl.ds(j, 1)
                turned = base * turn_c_ref[row, columns] + swapped * turn_s_ref[row, columns]
                tables[i % 2][j * STEP : (j + 1) * STEP, c * LANES : (c + 1) * LANES] = turned.astype(jnp.bfloat16)

    low = lax.broadcasted_iota(jnp.int32, (1, LANES), 1) < BAND
    responses = {}

    def respond(i):
        responses[i] = []
        for columns in columns_of(i):
            here = jnp.dot(
                taps_ref[:, 0:128],
                fine_ref[0:128, columns],
                precision=lax.Precision.HIGHEST,
                preferred_element_type=jnp.float32,
            )
            here = here + taps_ref[:, 128:129] * fine_ref[128:129, columns]
            other = pltpu.roll(jnp.broadcast_to(here, (8, LANES)), BAND, 1)[0:1, :]
            responses[i].append((jnp.where(low, here, other), jnp.where(low, -other, here)))

    row = lax.broadcasted_iota(jnp.int32, (width, width), 0)
    same_band = (row // LANES) == (lax.broadcasted_iota(jnp.int32, (width, width), 1) // LANES)
    summing = same_band.astype(jnp.bfloat16)

    def whiten(i):
        raw = jnp.concatenate([totals[i % 2][c] for c in range(2)], 1)
        square = raw * raw
        high = square.astype(jnp.bfloat16)
        rest = (square - high.astype(jnp.float32)).astype(jnp.bfloat16)
        sums = jnp.dot(jnp.concatenate([high, rest], 0), summing, preferred_element_type=jnp.float32)
        white = raw * lax.rsqrt((sums[0:count, :] + sums[count:, :]) * (1.0 / BAND) + EPSILON)
        for c, (same, cross) in enumerate(responses[i]):
            part = white[:, c * LANES : (c + 1) * LANES]
            turned = part * same + pltpu.roll(part, BAND, 1) * cross
            for window in range(windows):
                stages[i % 2][c, window * pitch : window * pitch + nodes, :] = turned[window * nodes : (window + 1) * nodes]

    def give(i):
        for c in range(2):
            for node in range(nodes):
                values = stages[i % 2][c, pl.ds(node, windows, stride=pitch), :]
                outs[2 * i + c][node] = values.astype(jnp.bfloat16)

    for copy in copies:
        copy.wait()
    generate(0)
    last = len(steps) // 2 - 1
    for copy in chunks:
        copy.wait()
    for i in range(len(steps) // 2):
        respond(i)
        product = jnp.dot(x_ref[...], tables[i % 2][...], preferred_element_type=jnp.float32)
        for c in range(2):
            totals[i % 2][c] = product[:, c * LANES : (c + 1) * LANES]
        if i < last:
            generate(i + 1)
        if i > 0:
            whiten(i - 1)
        if i > 1:
            give(i - 2)
    if last > 0:
        give(last - 1)
    whiten(last)
    give(last)


def own_spectra(rows, taps, nodes, steps):
    tables = [jnp.asarray(t) for t in forward_tables()]
    count = rows.shape[0]
    hbm = pl.BlockSpec(memory_space=pltpu.HBM)
    vmem = pl.BlockSpec(memory_space=pltpu.VMEM)
    shape = jax.ShapeDtypeStruct((nodes, count // nodes, LANES), jnp.bfloat16)
    return pl.pallas_call(
        functools.partial(spectra_kernel, steps=steps, wins=len(steps)),
        in_specs=[hbm, vmem, hbm, hbm, hbm],
        out_specs=[vmem] * len(steps),
        out_shape=[shape] * len(steps),
        scratch_shapes=[
            pltpu.VMEM(rows.shape, jnp.bfloat16),
            *[pltpu.VMEM(t.shape, jnp.float32) for t in tables],
            *[pltpu.VMEM((SAMPLES, 2 * LANES), jnp.bfloat16)] * 2,
            *[pltpu.VMEM((2, count, LANES), jnp.float32)] * 2,
            *[pltpu.VMEM((2, (nodes + 8) * (count // nodes), LANES), jnp.float32)] * 2,
            pltpu.SemaphoreType.DMA((SAMPLES // CHUNK + 3,)),
        ],
        compiler_params=pltpu.CompilerParams(vmem_limit_bytes=60 * MIB),
        cost_estimate=pl.CostEstimate(
            flops=2 * len(steps) * count * SAMPLES * LANES, bytes_accessed=2 * count * SAMPLES, transcendentals=0
        ),
        name="own_spectra",
    )(rows, taps, *tables)


def lag_table_kernel(cos_ref, msin_ref, cos0_ref, msin0_ref, high_ref, low_ref, *, factor):
    part = pl.program_id(0)
    c0 = cos0_ref[pl.ds(part, 1), :] * factor
    s0 = msin0_ref[pl.ds(part, 1), :] * factor
    cos, msin = cos_ref[...], msin_ref[...]
    for half, values in ((0, cos * c0 - msin * s0), (1, cos * s0 + msin * c0)):
        high = values.astype(jnp.bfloat16)
        rows = pl.ds(half * BAND, BAND)
        high_ref[0, rows, :] = high
        low_ref[0, rows, :] = (values - high.astype(jnp.float32)).astype(jnp.bfloat16)


def make_lag_tables(parts, factor):
    tables = [jnp.asarray(t) for t in lag_tables(parts)]
    shape = jax.ShapeDtypeStruct((parts, LANES, LAGS), jnp.bfloat16)
    block = pl.BlockSpec((1, LANES, LAGS), lambda i: (i, 0, 0))
    return pl.pallas_call(
        functools.partial(lag_table_kernel, factor=factor),
        grid=(parts,),
        in_specs=[pl.BlockSpec(t.shape, lambda i: (0, 0)) for t in tables],
        out_specs=[block, block],
        out_shape=[shape, shape],
        compiler_params=pltpu.CompilerParams(vmem_limit_bytes=6 * MIB),
        name="lag_tables",
    )(*tables)


def by_bin_kernel(*refs, steps):
    blocks, refs = refs[:steps], refs[steps:]
    first_ref, second_ref, turned_ref, turned, near, sem = refs
    nodes, windows = near.shape[0], near.shape[1]
    _, is_first = position(steps)
    own_at = jnp.where(is_first, 0, 1)
    copy = pltpu.make_async_copy(blocks[0], near, sem)
    copy.start()
    row = lax.broadcasted_iota(jnp.int32, (LANES, LANES), 0)
    unit = (row == lax.broadcasted_iota(jnp.int32, (LANES, LANES), 1)).astype(jnp.bfloat16)
    for tile in (1, 0):
        here = [near if s == 0 else blocks[s] for s in range(tile * steps // 2, (tile + 1) * steps // 2)]
        if tile == 0:
            copy.wait()

        def turn(node, _, here=here, tile=tile):
            values = jnp.concatenate([block[node] for block in here] * 2, 0)
            values = lax.dot_general(unit, values, CONTRACT_LAST, preferred_element_type=jnp.float32)
            turned[pl.ds(pl.multiple_of((tile * nodes + node) * PITCH, 8), LANES), :] = values
            return 0

        lax.fori_loop(0, nodes, turn, 0, unroll=16)
    left = lax.broadcasted_iota(jnp.int32, (nodes, LANES), 1) < LANES // 2
    for which, (out_ref, tile) in enumerate(((first_ref, own_at), (second_ref, 1 - own_at))):
        start = tile * (nodes * PITCH)

        def one(f, _, out_ref=out_ref, start=start, which=which):
            real = turned[pl.ds(start + f, nodes, stride=PITCH), :]
            imag = turned[pl.ds(start + BAND + f, nodes, stride=PITCH), :]
            out_ref[f] = jnp.where(left, real, imag).astype(jnp.bfloat16)
            turned_ref[f, which * nodes : (which + 1) * nodes, :] = jnp.where(left, imag, -real).astype(jnp.bfloat16)
            return 0

        lax.fori_loop(0, BAND, one, 0, unroll=16)


def by_bin(blocks):
    nodes, windows, _ = blocks[0].shape
    steps = len(blocks)
    shape = jax.ShapeDtypeStruct((BAND, nodes, LANES), jnp.bfloat16)
    vmem = pl.BlockSpec(memory_space=pltpu.VMEM)
    return pl.pallas_call(
        functools.partial(by_bin_kernel, steps=steps),
        out_shape=[shape, shape, jax.ShapeDtypeStruct((BAND, 2 * nodes, LANES), jnp.bfloat16)],
        in_specs=[pl.BlockSpec(memory_space=pl.ANY)] + [vmem] * (len(blocks) - 1),
        out_specs=[vmem] * 3,
        scratch_shapes=[
            pltpu.VMEM((2 * nodes * PITCH, LANES), jnp.float32),
            pltpu.VMEM((nodes, windows, LANES), jnp.bfloat16),
            pltpu.SemaphoreType.DMA,
        ],
        compiler_params=pltpu.CompilerParams(vmem_limit_bytes=8 * MIB),
        cost_estimate=pl.CostEstimate(flops=1 << 31, bytes_accessed=1 << 22, transcendentals=0),
        name="by_bin",
    )(*blocks)


def cross_kernel(*refs):
    halves = [refs[5 * h : 5 * h + 5] for h in range(HALVES)]
    select_ref, *outs, cross = refs[5 * HALVES :]
    nodes = halves[0][0].shape[1]
    slots = outs[0].shape[2]
    stations, count = 2 * nodes, 4 * nodes
    pitch = count + 8

    def one_bin(f, _):
        wide = lambda k: jnp.concatenate([half[k][f] for half in halves], 1)
        own = jnp.concatenate([wide(0), wide(1)], 0)
        both = jnp.concatenate([own, wide(2)], 0)
        partners = jnp.concatenate([own, wide(3), wide(4)] * 2, 0)
        cross[pl.ds(pl.multiple_of(f * pitch, 8), count), :] = lax.dot_general(
            both, partners, CONTRACT_LAST, preferred_element_type=jnp.float32
        )
        return 0

    lax.fori_loop(0, BAND, one_bin, 0, unroll=8)
    _, is_first = position(len(outs))
    own_at = jnp.where(is_first, 0, 1)
    left = lax.broadcasted_iota(jnp.int32, (2 * BAND, 2 * count), 1) < count
    tiles = (outs[: len(outs) // 2], own_at), (outs[len(outs) // 2 :], 1 - own_at)
    for shares, where in tiles:

        def one_node(node, _, shares=shares, where=where):
            index = where * nodes + node
            real = cross[pl.ds(index, BAND, stride=pitch), :]
            imag = cross[pl.ds(stations + index, BAND, stride=pitch), :]
            values = jnp.concatenate([real, imag], 0)
            high = values.astype(jnp.bfloat16).astype(jnp.float32)
            split = jnp.where(left, high, values - high).astype(jnp.bfloat16)
            picked = lax.dot_general(select_ref[index], split, CONTRACT_LAST, preferred_element_type=jnp.float32)
            for d in range(2 * len(shares)):
                shares[d // 2][d % 2, node] = picked[d * slots : (d + 1) * slots, :]
            return 0

        lax.fori_loop(0, nodes, one_node, 0, unroll=8)


def cross_products(halves, select, wins):
    nodes = halves[0][0].shape[1]
    block = jax.ShapeDtypeStruct((2, nodes, select.shape[1] // wins, LANES), jnp.float32)
    vmem = pl.BlockSpec(memory_space=pltpu.VMEM)
    operands = [x for half in halves for x in half]
    return pl.pallas_call(
        cross_kernel,
        out_shape=[block] * wins,
        in_specs=[vmem] * (len(operands) + 1),
        out_specs=[vmem] * wins,
        scratch_shapes=[pltpu.VMEM((BAND * (4 * nodes + 8), 8 * nodes), jnp.float32)],
        compiler_params=pltpu.CompilerParams(vmem_limit_bytes=12 * MIB),
        name="cross_products",
    )(*operands, select)


def inverse_kernel(high_ref, low_ref, *refs):
    *blocks, out_hbm, both, out_ref, sems = refs
    _, nodes, slots, _ = blocks[0].shape
    rows = nodes * slots
    me, _ = position(len(blocks) // 2)
    for d, block in enumerate(blocks):
        columns = pl.ds(pl.multiple_of((me ^ d) * LANES, LANES), LANES)
        values = block[d % 2].reshape(rows, LANES)
        high = values.astype(jnp.bfloat16)
        both[0:rows, columns] = high
        both[rows : 2 * rows, columns] = (values - high.astype(jnp.float32)).astype(jnp.bfloat16)
    width = out_ref.shape[3]
    copies = []
    for i in range(LAGS // width):
        here = slice(i * width, (i + 1) * width)
        first = jnp.dot(both[...], high_ref[:, here], preferred_element_type=jnp.float32)
        second = jnp.dot(both[0:rows, :], low_ref[:, here], preferred_element_type=jnp.float32)
        total = first[0:rows, :] + (first[rows : 2 * rows, :] + second)
        out_ref[i] = total.reshape(nodes, slots, width)
        copy = pltpu.make_async_copy(out_ref.at[i], out_hbm.at[:, :, pl.ds(i * width, width)], sems.at[i])
        copy.start()
        copies.append(copy)
    for copy in copies:
        copy.wait()


def inverse(blocks, high, low):
    _, nodes, slots, _ = blocks[0].shape
    depth = high.shape[0] * LANES
    width = 256
    vmem = pl.BlockSpec(memory_space=pltpu.VMEM)
    return pl.pallas_call(
        inverse_kernel,
        in_specs=[vmem] * (2 + len(blocks)),
        out_specs=pl.BlockSpec(memory_space=pl.ANY),
        out_shape=jax.ShapeDtypeStruct((nodes, slots, LAGS), jnp.float32),
        scratch_shapes=[
            pltpu.VMEM((2 * nodes * slots, depth), jnp.bfloat16),
            pltpu.VMEM((LAGS // width, nodes, slots, width), jnp.float32),
            pltpu.SemaphoreType.DMA((LAGS // width,)),
        ],
        compiler_params=pltpu.CompilerParams(vmem_limit_bytes=12 * MIB),
        name="inverse",
    )(high.reshape(depth, LAGS), low.reshape(depth, LAGS), *blocks)


def per_device(traces, taps, neighbours, valid, *, pairs, wins):
    windows, nodes, samples = traces.shape
    parts = 2 * wins
    place = lax.axis_index("pairs")
    win = lax.axis_index("win")

    def hop(array, d):
        pairing = [
            (i, ((i // wins) ^ (d // wins)) * wins + ((i % wins) ^ (d % wins))) for i in range(pairs * wins)
        ]
        return lax.ppermute(array, ("pairs", "win"), pairing)

    def between_chips(blocks):
        return [hop(block, 2 * s) if s else block for s, block in enumerate(blocks)]

    def within_chip(moved):
        return [x for block in moved for x in (block, hop(block, 1))]

    rows, taps = traces.reshape(windows * nodes, samples), taps.reshape(1, TAPS)
    steps = tuple(range(wins))[::-1]
    partner_rows = hop(rows, 1)
    found = own_spectra(rows, taps, nodes, steps)
    found, neighbours, valid = lax.optimization_barrier((found, neighbours, valid))

    _, is_first = position(wins)
    tile, member = neighbours // nodes, neighbours % nodes
    inside = tile // 2 == place // 2
    leading = 1 - (place // 2) % 2
    block = jnp.where(inside, jnp.where(tile % 2 == leading, 0, 1), jnp.where(is_first, 2, 3))
    code = jnp.where(valid != 0, block * nodes + member, -1)
    other = lax.ppermute(code, "pairs", [(i, i ^ 1) for i in range(pairs)])
    codes = jnp.where(is_first, jnp.concatenate([code, other], 0), jnp.concatenate([other, code], 0))
    for bit in (1 << k for k in range((wins - 1).bit_length())):
        split = codes.reshape(2 * nodes, wins // (2 * bit), 2, -1)
        codes = jnp.where(win & bit != 0, split[:, :, ::-1], split)
    codes = codes.reshape(2 * nodes, -1)
    columns = jnp.arange(8 * nodes, dtype=jnp.int32) % (4 * nodes)
    select = (codes[:, :, None] == columns[None, None, :]).astype(jnp.bfloat16)

    factor = 1.0 / math.sqrt(BINS * windows * wins)
    high, low = make_lag_tables(parts, factor)

    swap_a = [(i, i ^ 2) for i in range(pairs) if (i ^ 2) < pairs]
    swap_b = [(i, j) for i in range(2, pairs) for j in [((i - 2) ^ 2) + 2] if j < pairs]
    halves = []
    for half in range(HALVES):
        if half:
            found = own_spectra(partner_rows, taps, nodes, steps)
        blocks = between_chips([found[steps.index(s)] for s in range(wins)])
        a, b, turned = by_bin(blocks)
        halves.append((a, b, turned, lax.ppermute(a, "pairs", swap_a), lax.ppermute(b, "pairs", swap_b)))
    stack = cross_products(halves, select, wins)
    moved = between_chips(stack)
    moved[1], high, low = lax.optimization_barrier((moved[1], high, low))
    return inverse(within_chip(moved), high, low)


def solution(mesh):
    placed = (P("win", "pairs", None), P(), P("pairs", None), P("pairs", None))
    body = functools.partial(per_device, pairs=mesh.shape["pairs"], wins=mesh.shape["win"])
    return jax.shard_map(
        body, mesh=mesh, in_specs=placed, out_specs=P("pairs", "win", None), check_vma=False
    )
```

```python
import functools
import math

import jax
import jax.numpy as jnp
import numpy as np
from jax import lax
from jax.experimental import pallas as pl
from jax.experimental.pallas import tpu as pltpu
from jax.sharding import PartitionSpec as P

SAMPLES = 4096
BINS = 512
BAND = 64
LOW_BIN = 64
LAGS = 1024
TAPS = 129
LANES = 2 * BAND
EPSILON = 1e-06
STEP = 64
CHUNK = 512
HALVES = 2
PITCH = LANES + 8
MIB = 1024 * 1024
CONTRACT_LAST = (((1,), (1,)), ((), ()))


def unit_circle(products):
    angles = (products % SAMPLES).astype(np.float64) * (2.0 * math.pi / SAMPLES)
    return np.cos(angles).astype(np.float32), (-np.sin(angles)).astype(np.float32)


def banded(first, second):
    rows = first.shape[0]
    parts = [a.reshape(rows, BINS // BAND, 1, BAND) for a in (first, second)]
    return np.concatenate(parts, 2).reshape(rows, 2 * BINS)


def forward_tables():
    bins = LOW_BIN + np.arange(BINS, dtype=np.int64)
    cos, msin = unit_circle(np.arange(TAPS, dtype=np.int64)[:, None] * bins[None, :])
    fine = banded(cos, msin)
    starts = np.arange(0, SAMPLES, STEP, dtype=np.int64)
    cos, msin = unit_circle(starts[:, None] * bins[None, :])
    return fine, banded(cos, cos), banded(-msin, msin)


def lag_tables(parts):
    lags = np.arange(LAGS, dtype=np.int64) - LAGS // 2
    cos, msin = unit_circle(np.arange(BAND, dtype=np.int64)[:, None] * lags[None, :])
    first = LOW_BIN + BAND * np.arange(parts, dtype=np.int64)
    cos0, msin0 = unit_circle(first[:, None] * lags[None, :])
    return cos, msin, cos0, msin0


def position(wins):
    place = lax.axis_index("pairs")
    me = (place % 2) * wins + lax.axis_index("win")
    return me, place % 2 != (place // 2) % 2


def spectra_kernel(x_hbm, taps_ref, fine_hbm, turn_c_hbm, turn_s_hbm, *refs, steps, wins):
    outs, refs = refs[: len(steps)], refs[len(steps) :]
    x_ref, fine_ref, turn_c_ref, turn_s_ref, *refs, sems = refs
    tables, totals, stages = refs[0:2], refs[2:4], refs[4:6]
    count = x_ref.shape[0]
    nodes, windows = outs[0].shape[0], outs[0].shape[1]
    width = 2 * LANES
    pitch = stages[0].shape[1] // windows
    pieces = SAMPLES // CHUNK
    me, _ = position(wins)
    copies = [
        pltpu.make_async_copy(source, target, sems.at[pieces + i])
        for i, (source, target) in enumerate(
            ((fine_hbm, fine_ref), (turn_c_hbm, turn_c_ref), (turn_s_hbm, turn_s_ref))
        )
    ]
    chunks = [
        pltpu.make_async_copy(
            x_hbm.at[:, pl.ds(i * CHUNK, CHUNK)], x_ref.at[:, pl.ds(i * CHUNK, CHUNK)], sems.at[i]
        )
        for i in range(pieces)
    ]
    for copy in copies + chunks:
        copy.start()

    def columns_of(i):
        return [pl.ds(pl.multiple_of((me ^ (2 * step)) * LANES, LANES), LANES) for step in steps[2 * i : 2 * i + 2]]

    def generate(i):
        for c, columns in enumerate(columns_of(i)):
            base = fine_ref[0:STEP, columns]
            swapped = pltpu.roll(base, BAND, 1)
            for j in range(SAMPLES // STEP):
                row = pl.ds(j, 1)
                turned = base * turn_c_ref[row, columns] + swapped * turn_s_ref[row, columns]
                tables[i % 2][j * STEP : (j + 1) * STEP, c * LANES : (c + 1) * LANES] = turned.astype(jnp.bfloat16)

    low = lax.broadcasted_iota(jnp.int32, (1, LANES), 1) < BAND
    responses = {}

    def respond(i):
        responses[i] = []
        for columns in columns_of(i):
            here = jnp.dot(
                taps_ref[:, 0:128],
                fine_ref[0:128, columns],
                precision=lax.Precision.HIGHEST,
                preferred_element_type=jnp.float32,
            )
            here = here + taps_ref[:, 128:129] * fine_ref[128:129, columns]
            other = pltpu.roll(jnp.broadcast_to(here, (8, LANES)), BAND, 1)[0:1, :]
            responses[i].append((jnp.where(low, here, other), jnp.where(low, -other, here)))

    row = lax.broadcasted_iota(jnp.int32, (width, width), 0)
    same_band = (row // LANES) == (lax.broadcasted_iota(jnp.int32, (width, width), 1) // LANES)
    summing = same_band.astype(jnp.bfloat16)

    def whiten(i):
        raw = jnp.concatenate([totals[i % 2][c] for c in range(2)], 1)
        square = raw * raw
        high = square.astype(jnp.bfloat16)
        rest = (square - high.astype(jnp.float32)).astype(jnp.bfloat16)
        sums = jnp.dot(jnp.concatenate([high, rest], 0), summing, preferred_element_type=jnp.float32)
        white = raw * lax.rsqrt((sums[0:count, :] + sums[count:, :]) * (1.0 / BAND) + EPSILON)
        for c, (same, cross) in enumerate(responses[i]):
            part = white[:, c * LANES : (c + 1) * LANES]
            turned = part * same + pltpu.roll(part, BAND, 1) * cross
            for window in range(windows):
                stages[i % 2][c, window * pitch : window * pitch + nodes, :] = turned[window * nodes : (window + 1) * nodes]

    def give(i):
        for c in range(2):
            for node in range(nodes):
                values = stages[i % 2][c, pl.ds(node, windows, stride=pitch), :]
                outs[2 * i + c][node] = values.astype(jnp.bfloat16)

    for copy in copies:
        copy.wait()
    generate(0)
    last = len(steps) // 2 - 1
    for copy in chunks:
        copy.wait()
    for i in range(len(steps) // 2):
        respond(i)
        product = jnp.dot(x_ref[...], tables[i % 2][...], preferred_element_type=jnp.float32)
        for c in range(2):
            totals[i % 2][c] = product[:, c * LANES : (c + 1) * LANES]
        if i < last:
            generate(i + 1)
        if i > 0:
            whiten(i - 1)
        if i > 1:
            give(i - 2)
    if last > 0:
        give(last - 1)
    whiten(last)
    give(last)


def own_spectra(rows, taps, nodes, steps):
    tables = [jnp.asarray(t) for t in forward_tables()]
    count = rows.shape[0]
    hbm = pl.BlockSpec(memory_space=pltpu.HBM)
    vmem = pl.BlockSpec(memory_space=pltpu.VMEM)
    shape = jax.ShapeDtypeStruct((nodes, count // nodes, LANES), jnp.bfloat16)
    return pl.pallas_call(
        functools.partial(spectra_kernel, steps=steps, wins=len(steps)),
        in_specs=[hbm, vmem, hbm, hbm, hbm],
        out_specs=[vmem] * len(steps),
        out_shape=[shape] * len(steps),
        scratch_shapes=[
            pltpu.VMEM(rows.shape, jnp.bfloat16),
            *[pltpu.VMEM(t.shape, jnp.float32) for t in tables],
            *[pltpu.VMEM((SAMPLES, 2 * LANES), jnp.bfloat16)] * 2,
            *[pltpu.VMEM((2, count, LANES), jnp.float32)] * 2,
            *[pltpu.VMEM((2, (nodes + 8) * (count // nodes), LANES), jnp.float32)] * 2,
            pltpu.SemaphoreType.DMA((SAMPLES // CHUNK + 3,)),
        ],
        compiler_params=pltpu.CompilerParams(vmem_limit_bytes=60 * MIB),
        cost_estimate=pl.CostEstimate(
            flops=2 * len(steps) * count * SAMPLES * LANES, bytes_accessed=2 * count * SAMPLES, transcendentals=0
        ),
        name="own_spectra",
    )(rows, taps, *tables)


def lag_table_kernel(cos_ref, msin_ref, cos0_ref, msin0_ref, high_ref, low_ref, *, factor):
    part = pl.program_id(0)
    c0 = cos0_ref[pl.ds(part, 1), :] * factor
    s0 = msin0_ref[pl.ds(part, 1), :] * factor
    cos, msin = cos_ref[...], msin_ref[...]
    for half, values in ((0, cos * c0 - msin * s0), (1, cos * s0 + msin * c0)):
        high = values.astype(jnp.bfloat16)
        rows = pl.ds(half * BAND, BAND)
        high_ref[0, rows, :] = high
        low_ref[0, rows, :] = (values - high.astype(jnp.float32)).astype(jnp.bfloat16)


def make_lag_tables(parts, factor):
    tables = [jnp.asarray(t) for t in lag_tables(parts)]
    shape = jax.ShapeDtypeStruct((parts, LANES, LAGS), jnp.bfloat16)
    block = pl.BlockSpec((1, LANES, LAGS), lambda i: (i, 0, 0))
    return pl.pallas_call(
        functools.partial(lag_table_kernel, factor=factor),
        grid=(parts,),
        in_specs=[pl.BlockSpec(t.shape, lambda i: (0, 0)) for t in tables],
        out_specs=[block, block],
        out_shape=[shape, shape],
        compiler_params=pltpu.CompilerParams(vmem_limit_bytes=6 * MIB),
        name="lag_tables",
    )(*tables)


def by_bin_kernel(*refs, steps):
    blocks, refs = refs[:steps], refs[steps:]
    first_ref, second_ref, turned_ref, turned, near, sem = refs
    nodes, windows = near.shape[0], near.shape[1]
    _, is_first = position(steps)
    own_at = jnp.where(is_first, 0, 1)
    copy = pltpu.make_async_copy(blocks[0], near, sem)
    copy.start()
    row = lax.broadcasted_iota(jnp.int32, (LANES, LANES), 0)
    unit = (row == lax.broadcasted_iota(jnp.int32, (LANES, LANES), 1)).astype(jnp.bfloat16)
    for tile in (1, 0):
        here = [near if s == 0 else blocks[s] for s in range(tile * steps // 2, (tile + 1) * steps // 2)]
        if tile == 0:
            copy.wait()

        def turn(node, _, here=here, tile=tile):
            values = jnp.concatenate([block[node] for block in here] * 2, 0)
            values = lax.dot_general(unit, values, CONTRACT_LAST, preferred_element_type=jnp.float32)
            turned[pl.ds(pl.multiple_of((tile * nodes + node) * PITCH, 8), LANES), :] = values
            return 0

        lax.fori_loop(0, nodes, turn, 0, unroll=16)
    left = lax.broadcasted_iota(jnp.int32, (nodes, LANES), 1) < LANES // 2
    for which, (out_ref, tile) in enumerate(((first_ref, own_at), (second_ref, 1 - own_at))):
        start = tile * (nodes * PITCH)

        def one(f, _, out_ref=out_ref, start=start, which=which):
            real = turned[pl.ds(start + f, nodes, stride=PITCH), :]
            imag = turned[pl.ds(start + BAND + f, nodes, stride=PITCH), :]
            out_ref[f] = jnp.where(left, real, imag).astype(jnp.bfloat16)
            turned_ref[f, which * nodes : (which + 1) * nodes, :] = jnp.where(left, imag, -real).astype(jnp.bfloat16)
            return 0

        lax.fori_loop(0, BAND, one, 0, unroll=32)


def by_bin(blocks):
    nodes, windows, _ = blocks[0].shape
    steps = len(blocks)
    shape = jax.ShapeDtypeStruct((BAND, nodes, LANES), jnp.bfloat16)
    vmem = pl.BlockSpec(memory_space=pltpu.VMEM)
    return pl.pallas_call(
        functools.partial(by_bin_kernel, steps=steps),
        out_shape=[shape, shape, jax.ShapeDtypeStruct((BAND, 2 * nodes, LANES), jnp.bfloat16)],
        in_specs=[pl.BlockSpec(memory_space=pl.ANY)] + [vmem] * (len(blocks) - 1),
        out_specs=[vmem] * 3,
        scratch_shapes=[
            pltpu.VMEM((2 * nodes * PITCH, LANES), jnp.float32),
            pltpu.VMEM((nodes, windows, LANES), jnp.bfloat16),
            pltpu.SemaphoreType.DMA,
        ],
        compiler_params=pltpu.CompilerParams(vmem_limit_bytes=8 * MIB),
        cost_estimate=pl.CostEstimate(flops=1 << 31, bytes_accessed=1 << 22, transcendentals=0),
        name="by_bin",
    )(*blocks)


def cross_kernel(*refs):
    halves = [refs[5 * h : 5 * h + 5] for h in range(HALVES)]
    select_ref, *outs, cross = refs[5 * HALVES :]
    nodes = halves[0][0].shape[1]
    slots = outs[0].shape[2]
    stations, count = 2 * nodes, 4 * nodes
    pitch = count + 8

    def one_bin(f, _):
        wide = lambda k: jnp.concatenate([half[k][f] for half in halves], 1)
        own = jnp.concatenate([wide(0), wide(1)], 0)
        both = jnp.concatenate([own, wide(2)], 0)
        partners = jnp.concatenate([own, wide(3), wide(4)] * 2, 0)
        cross[pl.ds(pl.multiple_of(f * pitch, 8), count), :] = lax.dot_general(
            both, partners, CONTRACT_LAST, preferred_element_type=jnp.float32
        )
        return 0

    lax.fori_loop(0, BAND, one_bin, 0, unroll=32)
    _, is_first = position(len(outs))
    own_at = jnp.where(is_first, 0, 1)
    left = lax.broadcasted_iota(jnp.int32, (2 * BAND, 2 * count), 1) < count
    tiles = (outs[: len(outs) // 2], own_at), (outs[len(outs) // 2 :], 1 - own_at)
    for shares, where in tiles:

        def one_node(node, _, shares=shares, where=where):
            index = where * nodes + node
            real = cross[pl.ds(index, BAND, stride=pitch), :]
            imag = cross[pl.ds(stations + index, BAND, stride=pitch), :]
            values = jnp.concatenate([real, imag], 0)
            high = values.astype(jnp.bfloat16).astype(jnp.float32)
            split = jnp.where(left, high, values - high).astype(jnp.bfloat16)
            picked = lax.dot_general(select_ref[index], split, CONTRACT_LAST, preferred_element_type=jnp.float32)
            for d in range(2 * len(shares)):
                shares[d // 2][d % 2, node] = picked[d * slots : (d + 1) * slots, :]
            return 0

        lax.fori_loop(0, nodes, one_node, 0, unroll=16)


def cross_products(halves, select, wins):
    nodes = halves[0][0].shape[1]
    block = jax.ShapeDtypeStruct((2, nodes, select.shape[1] // wins, LANES), jnp.float32)
    vmem = pl.BlockSpec(memory_space=pltpu.VMEM)
    operands = [x for half in halves for x in half]
    return pl.pallas_call(
        cross_kernel,
        out_shape=[block] * wins,
        in_specs=[vmem] * (len(operands) + 1),
        out_specs=[vmem] * wins,
        scratch_shapes=[pltpu.VMEM((BAND * (4 * nodes + 8), 8 * nodes), jnp.float32)],
        compiler_params=pltpu.CompilerParams(vmem_limit_bytes=12 * MIB),
        name="cross_products",
    )(*operands, select)


def inverse_kernel(high_ref, low_ref, *refs):
    *blocks, out_hbm, both, out_ref, sems = refs
    _, nodes, slots, _ = blocks[0].shape
    rows = nodes * slots
    me, _ = position(len(blocks) // 2)
    for d, block in enumerate(blocks):
        columns = pl.ds(pl.multiple_of((me ^ d) * LANES, LANES), LANES)
        values = block[d % 2].reshape(rows, LANES)
        high = values.astype(jnp.bfloat16)
        both[0:rows, columns] = high
        both[rows : 2 * rows, columns] = (values - high.astype(jnp.float32)).astype(jnp.bfloat16)
    width = out_ref.shape[3]
    copies = []
    for i in range(LAGS // width):
        here = slice(i * width, (i + 1) * width)
        first = jnp.dot(both[...], high_ref[:, here], preferred_element_type=jnp.float32)
        second = jnp.dot(both[0:rows, :], low_ref[:, here], preferred_element_type=jnp.float32)
        total = first[0:rows, :] + (first[rows : 2 * rows, :] + second)
        out_ref[i] = total.reshape(nodes, slots, width)
        copy = pltpu.make_async_copy(out_ref.at[i], out_hbm.at[:, :, pl.ds(i * width, width)], sems.at[i])
        copy.start()
        copies.append(copy)
    for copy in copies:
        copy.wait()


def inverse(blocks, high, low):
    _, nodes, slots, _ = blocks[0].shape
    depth = high.shape[0] * LANES
    width = 256
    vmem = pl.BlockSpec(memory_space=pltpu.VMEM)
    return pl.pallas_call(
        inverse_kernel,
        in_specs=[vmem] * (2 + len(blocks)),
        out_specs=pl.BlockSpec(memory_space=pl.ANY),
        out_shape=jax.ShapeDtypeStruct((nodes, slots, LAGS), jnp.float32),
        scratch_shapes=[
            pltpu.VMEM((2 * nodes * slots, depth), jnp.bfloat16),
            pltpu.VMEM((LAGS // width, nodes, slots, width), jnp.float32),
            pltpu.SemaphoreType.DMA((LAGS // width,)),
        ],
        compiler_params=pltpu.CompilerParams(vmem_limit_bytes=12 * MIB),
        name="inverse",
    )(high.reshape(depth, LAGS), low.reshape(depth, LAGS), *blocks)


def per_device(traces, taps, neighbours, valid, *, pairs, wins):
    windows, nodes, samples = traces.shape
    parts = 2 * wins
    place = lax.axis_index("pairs")
    win = lax.axis_index("win")

    def hop(array, d):
        pairing = [
            (i, ((i // wins) ^ (d // wins)) * wins + ((i % wins) ^ (d % wins))) for i in range(pairs * wins)
        ]
        return lax.ppermute(array, ("pairs", "win"), pairing)

    def between_chips(blocks):
        return [hop(block, 2 * s) if s else block for s, block in enumerate(blocks)]

    def within_chip(moved):
        return [x for block in moved for x in (block, hop(block, 1))]

    rows, taps = traces.reshape(windows * nodes, samples), taps.reshape(1, TAPS)
    steps = tuple(range(wins))[::-1]
    partner_rows = hop(rows, 1)
    found = own_spectra(rows, taps, nodes, steps)
    found, neighbours, valid = lax.optimization_barrier((found, neighbours, valid))

    _, is_first = position(wins)
    tile, member = neighbours // nodes, neighbours % nodes
    inside = tile // 2 == place // 2
    leading = 1 - (place // 2) % 2
    block = jnp.where(inside, jnp.where(tile % 2 == leading, 0, 1), jnp.where(is_first, 2, 3))
    code = jnp.where(valid != 0, block * nodes + member, -1)
    other = lax.ppermute(code, "pairs", [(i, i ^ 1) for i in range(pairs)])
    codes = jnp.where(is_first, jnp.concatenate([code, other], 0), jnp.concatenate([other, code], 0))
    for bit in (1 << k for k in range((wins - 1).bit_length())):
        split = codes.reshape(2 * nodes, wins // (2 * bit), 2, -1)
        codes = jnp.where(win & bit != 0, split[:, :, ::-1], split)
    codes = codes.reshape(2 * nodes, -1)
    columns = jnp.arange(8 * nodes, dtype=jnp.int32) % (4 * nodes)
    select = (codes[:, :, None] == columns[None, None, :]).astype(jnp.bfloat16)

    factor = 1.0 / math.sqrt(BINS * windows * wins)
    high, low = make_lag_tables(parts, factor)

    swap_a = [(i, i ^ 2) for i in range(pairs) if (i ^ 2) < pairs]
    swap_b = [(i, j) for i in range(2, pairs) for j in [((i - 2) ^ 2) + 2] if j < pairs]
    halves = []
    for half in range(HALVES):
        if half:
            found = own_spectra(partner_rows, taps, nodes, steps)
        blocks = between_chips([found[steps.index(s)] for s in range(wins)])
        a, b, turned = by_bin(blocks)
        halves.append((a, b, turned, lax.ppermute(a, "pairs", swap_a), lax.ppermute(b, "pairs", swap_b)))
    stack = cross_products(halves, select, wins)
    moved = between_chips(stack)
    moved[1], high, low = lax.optimization_barrier((moved[1], high, low))
    return inverse(within_chip(moved), high, low)


def solution(mesh):
    placed = (P("win", "pairs", None), P(), P("pairs", None), P("pairs", None))
    body = functools.partial(per_device, pairs=mesh.shape["pairs"], wins=mesh.shape["win"])
    return jax.shard_map(
        body, mesh=mesh, in_specs=placed, out_specs=P("pairs", "win", None), check_vma=False
    )
```

```python
import functools
import math

import jax
import jax.numpy as jnp
import numpy as np
from jax import lax
from jax.experimental import pallas as pl
from jax.experimental.pallas import tpu as pltpu
from jax.sharding import PartitionSpec as P

SAMPLES = 4096
BINS = 512
BAND = 64
LOW_BIN = 64
LAGS = 1024
TAPS = 129
LANES = 2 * BAND
EPSILON = 1e-06
STEP = 64
CHUNK = 512
HALVES = 2
PITCH = LANES + 8
MIB = 1024 * 1024
CONTRACT_LAST = (((1,), (1,)), ((), ()))


def unit_circle(products):
    angles = (products % SAMPLES).astype(np.float64) * (2.0 * math.pi / SAMPLES)
    return np.cos(angles).astype(np.float32), (-np.sin(angles)).astype(np.float32)


def banded(first, second):
    rows = first.shape[0]
    parts = [a.reshape(rows, BINS // BAND, 1, BAND) for a in (first, second)]
    return np.concatenate(parts, 2).reshape(rows, 2 * BINS)


def forward_tables():
    bins = LOW_BIN + np.arange(BINS, dtype=np.int64)
    cos, msin = unit_circle(np.arange(TAPS, dtype=np.int64)[:, None] * bins[None, :])
    fine = banded(cos, msin)
    starts = np.arange(0, SAMPLES, STEP, dtype=np.int64)
    cos, msin = unit_circle(starts[:, None] * bins[None, :])
    return fine, banded(cos, cos), banded(-msin, msin)


def lag_tables(parts):
    lags = np.arange(LAGS, dtype=np.int64) - LAGS // 2
    cos, msin = unit_circle(np.arange(BAND, dtype=np.int64)[:, None] * lags[None, :])
    first = LOW_BIN + BAND * np.arange(parts, dtype=np.int64)
    cos0, msin0 = unit_circle(first[:, None] * lags[None, :])
    return cos, msin, cos0, msin0


def position(wins):
    place = lax.axis_index("pairs")
    me = (place % 2) * wins + lax.axis_index("win")
    return me, place % 2 != (place // 2) % 2


def spectra_kernel(x_hbm, taps_ref, fine_hbm, turn_c_hbm, turn_s_hbm, *refs, steps, wins):
    outs, refs = refs[: len(steps)], refs[len(steps) :]
    x_ref, fine_ref, turn_c_ref, turn_s_ref, *refs, sems = refs
    tables, totals, stages = refs[0:2], refs[2:4], refs[4:6]
    count = x_ref.shape[0]
    nodes, windows = outs[0].shape[0], outs[0].shape[1]
    width = 2 * LANES
    pitch = stages[0].shape[1] // windows
    pieces = SAMPLES // CHUNK
    me, _ = position(wins)
    copies = [
        pltpu.make_async_copy(source, target, sems.at[pieces + i])
        for i, (source, target) in enumerate(
            ((fine_hbm, fine_ref), (turn_c_hbm, turn_c_ref), (turn_s_hbm, turn_s_ref))
        )
    ]
    chunks = [
        pltpu.make_async_copy(
            x_hbm.at[:, pl.ds(i * CHUNK, CHUNK)], x_ref.at[:, pl.ds(i * CHUNK, CHUNK)], sems.at[i]
        )
        for i in range(pieces)
    ]
    for copy in copies + chunks:
        copy.start()

    def columns_of(i):
        return [pl.ds(pl.multiple_of((me ^ (2 * step)) * LANES, LANES), LANES) for step in steps[2 * i : 2 * i + 2]]

    def generate(i):
        for c, columns in enumerate(columns_of(i)):
            base = fine_ref[0:STEP, columns]
            swapped = pltpu.roll(base, BAND, 1)
            for j in range(SAMPLES // STEP):
                row = pl.ds(j, 1)
                turned = base * turn_c_ref[row, columns] + swapped * turn_s_ref[row, columns]
                tables[i % 2][j * STEP : (j + 1) * STEP, c * LANES : (c + 1) * LANES] = turned.astype(jnp.bfloat16)

    low = lax.broadcasted_iota(jnp.int32, (1, LANES), 1) < BAND
    responses = {}

    def respond(i):
        responses[i] = []
        for columns in columns_of(i):
            here = jnp.dot(
                taps_ref[:, 0:128],
                fine_ref[0:128, columns],
                precision=lax.Precision.HIGHEST,
                preferred_element_type=jnp.float32,
            )
            here = here + taps_ref[:, 128:129] * fine_ref[128:129, columns]
            other = pltpu.roll(jnp.broadcast_to(here, (8, LANES)), BAND, 1)[0:1, :]
            responses[i].append((jnp.where(low, here, other), jnp.where(low, -other, here)))

    row = lax.broadcasted_iota(jnp.int32, (width, width), 0)
    same_band = (row // LANES) == (lax.broadcasted_iota(jnp.int32, (width, width), 1) // LANES)
    summing = same_band.astype(jnp.bfloat16)

    def whiten(i):
        raw = jnp.concatenate([totals[i % 2][c] for c in range(2)], 1)
        square = raw * raw
        high = square.astype(jnp.bfloat16)
        rest = (square - high.astype(jnp.float32)).astype(jnp.bfloat16)
        sums = jnp.dot(jnp.concatenate([high, rest], 0), summing, preferred_element_type=jnp.float32)
        white = raw * lax.rsqrt((sums[0:count, :] + sums[count:, :]) * (1.0 / BAND) + EPSILON)
        for c, (same, cross) in enumerate(responses[i]):
            part = white[:, c * LANES : (c + 1) * LANES]
            turned = part * same + pltpu.roll(part, BAND, 1) * cross
            for window in range(windows):
                stages[i % 2][c, window * pitch : window * pitch + nodes, :] = turned[window * nodes : (window + 1) * nodes]

    def give(i):
        for c in range(2):
            for node in range(nodes):
                values = stages[i % 2][c, pl.ds(node, windows, stride=pitch), :]
                outs[2 * i + c][node] = values.astype(jnp.bfloat16)

    for copy in copies:
        copy.wait()
    generate(0)
    last = len(steps) // 2 - 1
    for copy in chunks:
        copy.wait()
    for i in range(len(steps) // 2):
        respond(i)
        product = jnp.dot(x_ref[...], tables[i % 2][...], preferred_element_type=jnp.float32)
        for c in range(2):
            totals[i % 2][c] = product[:, c * LANES : (c + 1) * LANES]
        if i < last:
            generate(i + 1)
        if i > 0:
            whiten(i - 1)
        if i > 1:
            give(i - 2)
    if last > 0:
        give(last - 1)
    whiten(last)
    give(last)


def own_spectra(rows, taps, nodes, steps):
    tables = [jnp.asarray(t) for t in forward_tables()]
    count = rows.shape[0]
    hbm = pl.BlockSpec(memory_space=pltpu.HBM)
    vmem = pl.BlockSpec(memory_space=pltpu.VMEM)
    shape = jax.ShapeDtypeStruct((nodes, count // nodes, LANES), jnp.bfloat16)
    return pl.pallas_call(
        functools.partial(spectra_kernel, steps=steps, wins=len(steps)),
        in_specs=[hbm, vmem, hbm, hbm, hbm],
        out_specs=[vmem] * len(steps),
        out_shape=[shape] * len(steps),
        scratch_shapes=[
            pltpu.VMEM(rows.shape, jnp.bfloat16),
            *[pltpu.VMEM(t.shape, jnp.float32) for t in tables],
            *[pltpu.VMEM((SAMPLES, 2 * LANES), jnp.bfloat16)] * 2,
            *[pltpu.VMEM((2, count, LANES), jnp.float32)] * 2,
            *[pltpu.VMEM((2, (nodes + 8) * (count // nodes), LANES), jnp.float32)] * 2,
            pltpu.SemaphoreType.DMA((SAMPLES // CHUNK + 3,)),
        ],
        compiler_params=pltpu.CompilerParams(vmem_limit_bytes=60 * MIB),
        cost_estimate=pl.CostEstimate(
            flops=2 * len(steps) * count * SAMPLES * LANES, bytes_accessed=2 * count * SAMPLES, transcendentals=0
        ),
        name="own_spectra",
    )(rows, taps, *tables)


def lag_table_kernel(cos_ref, msin_ref, cos0_ref, msin0_ref, high_ref, low_ref, *, factor):
    part = pl.program_id(0)
    c0 = cos0_ref[pl.ds(part, 1), :] * factor
    s0 = msin0_ref[pl.ds(part, 1), :] * factor
    cos, msin = cos_ref[...], msin_ref[...]
    for half, values in ((0, cos * c0 - msin * s0), (1, cos * s0 + msin * c0)):
        high = values.astype(jnp.bfloat16)
        rows = pl.ds(half * BAND, BAND)
        high_ref[0, rows, :] = high
        low_ref[0, rows, :] = (values - high.astype(jnp.float32)).astype(jnp.bfloat16)


def make_lag_tables(parts, factor):
    tables = [jnp.asarray(t) for t in lag_tables(parts)]
    shape = jax.ShapeDtypeStruct((parts, LANES, LAGS), jnp.bfloat16)
    block = pl.BlockSpec((1, LANES, LAGS), lambda i: (i, 0, 0))
    return pl.pallas_call(
        functools.partial(lag_table_kernel, factor=factor),
        grid=(parts,),
        in_specs=[pl.BlockSpec(t.shape, lambda i: (0, 0)) for t in tables],
        out_specs=[block, block],
        out_shape=[shape, shape],
        compiler_params=pltpu.CompilerParams(vmem_limit_bytes=6 * MIB),
        name="lag_tables",
    )(*tables)


def by_bin_kernel(*refs, steps):
    blocks, refs = refs[:steps], refs[steps:]
    first_ref, second_ref, turned_ref, turned, near, sem = refs
    nodes, windows = near.shape[0], near.shape[1]
    _, is_first = position(steps)
    own_at = jnp.where(is_first, 0, 1)
    copy = pltpu.make_async_copy(blocks[0], near, sem)
    copy.start()
    row = lax.broadcasted_iota(jnp.int32, (LANES, LANES), 0)
    unit = (row == lax.broadcasted_iota(jnp.int32, (LANES, LANES), 1)).astype(jnp.bfloat16)
    for tile in (1, 0):
        here = [near if s == 0 else blocks[s] for s in range(tile * steps // 2, (tile + 1) * steps // 2)]
        if tile == 0:
            copy.wait()

        def turn(node, _, here=here, tile=tile):
            values = jnp.concatenate([block[node] for block in here] * 2, 0)
            values = lax.dot_general(unit, values, CONTRACT_LAST, preferred_element_type=jnp.float32)
            turned[pl.ds(pl.multiple_of((tile * nodes + node) * PITCH, 8), LANES), :] = values
            return 0

        lax.fori_loop(0, nodes, turn, 0, unroll=16)
    left = lax.broadcasted_iota(jnp.int32, (nodes, LANES), 1) < LANES // 2
    for which, (out_ref, tile) in enumerate(((first_ref, own_at), (second_ref, 1 - own_at))):
        start = tile * (nodes * PITCH)

        def one(f, _, out_ref=out_ref, start=start, which=which):
            real = turned[pl.ds(start + f, nodes, stride=PITCH), :]
            imag = turned[pl.ds(start + BAND + f, nodes, stride=PITCH), :]
            out_ref[f] = jnp.where(left, real, imag).astype(jnp.bfloat16)
            turned_ref[f, which * nodes : (which + 1) * nodes, :] = jnp.where(left, imag, -real).astype(jnp.bfloat16)
            return 0

        lax.fori_loop(0, BAND, one, 0, unroll=64)


def by_bin(blocks):
    nodes, windows, _ = blocks[0].shape
    steps = len(blocks)
    shape = jax.ShapeDtypeStruct((BAND, nodes, LANES), jnp.bfloat16)
    vmem = pl.BlockSpec(memory_space=pltpu.VMEM)
    return pl.pallas_call(
        functools.partial(by_bin_kernel, steps=steps),
        out_shape=[shape, shape, jax.ShapeDtypeStruct((BAND, 2 * nodes, LANES), jnp.bfloat16)],
        in_specs=[pl.BlockSpec(memory_space=pl.ANY)] + [vmem] * (len(blocks) - 1),
        out_specs=[vmem] * 3,
        scratch_shapes=[
            pltpu.VMEM((2 * nodes * PITCH, LANES), jnp.float32),
            pltpu.VMEM((nodes, windows, LANES), jnp.bfloat16),
            pltpu.SemaphoreType.DMA,
        ],
        compiler_params=pltpu.CompilerParams(vmem_limit_bytes=8 * MIB),
        cost_estimate=pl.CostEstimate(flops=1 << 31, bytes_accessed=1 << 22, transcendentals=0),
        name="by_bin",
    )(*blocks)


def cross_kernel(*refs):
    halves = [refs[5 * h : 5 * h + 5] for h in range(HALVES)]
    halves[-1] = (*halves[-1][0:3], halves[-1][4], halves[-1][3])
    select_ref, *outs, cross = refs[5 * HALVES :]
    nodes = halves[0][0].shape[1]
    slots = outs[0].shape[2]
    stations, count = 2 * nodes, 4 * nodes
    pitch = count + 8

    def one_bin(f, _):
        wide = lambda k: jnp.concatenate([half[k][f] for half in halves], 1)
        own = jnp.concatenate([wide(0), wide(1)], 0)
        both = jnp.concatenate([own, wide(2)], 0)
        partners = jnp.concatenate([own, wide(3), wide(4)] * 2, 0)
        cross[pl.ds(pl.multiple_of(f * pitch, 8), count), :] = lax.dot_general(
            both, partners, CONTRACT_LAST, preferred_element_type=jnp.float32
        )
        return 0

    lax.fori_loop(0, BAND, one_bin, 0, unroll=64)
    _, is_first = position(len(outs))
    own_at = jnp.where(is_first, 0, 1)
    left = lax.broadcasted_iota(jnp.int32, (2 * BAND, 2 * count), 1) < count
    tiles = (outs[: len(outs) // 2], own_at), (outs[len(outs) // 2 :], 1 - own_at)
    for shares, where in tiles:

        def one_node(node, _, shares=shares, where=where):
            index = where * nodes + node
            real = cross[pl.ds(index, BAND, stride=pitch), :]
            imag = cross[pl.ds(stations + index, BAND, stride=pitch), :]
            values = jnp.concatenate([real, imag], 0)
            high = values.astype(jnp.bfloat16).astype(jnp.float32)
            split = jnp.where(left, high, values - high).astype(jnp.bfloat16)
            picked = lax.dot_general(select_ref[index], split, CONTRACT_LAST, preferred_element_type=jnp.float32)
            for d in range(2 * len(shares)):
                shares[d // 2][d % 2, node] = picked[d * slots : (d + 1) * slots, :]
            return 0

        lax.fori_loop(0, nodes, one_node, 0, unroll=16)


def cross_products(halves, select, wins):
    nodes = halves[0][0].shape[1]
    block = jax.ShapeDtypeStruct((2, nodes, select.shape[1] // wins, LANES), jnp.float32)
    vmem = pl.BlockSpec(memory_space=pltpu.VMEM)
    halves = [*halves[:-1], (*halves[-1][0:3], halves[-1][4], halves[-1][3])]
    operands = [x for half in halves for x in half]
    return pl.pallas_call(
        cross_kernel,
        out_shape=[block] * wins,
        in_specs=[vmem] * (len(operands) + 1),
        out_specs=[vmem] * wins,
        scratch_shapes=[pltpu.VMEM((BAND * (4 * nodes + 8), 8 * nodes), jnp.float32)],
        compiler_params=pltpu.CompilerParams(vmem_limit_bytes=12 * MIB),
        name="cross_products",
    )(*operands, select)


def inverse_kernel(high_ref, low_ref, *refs):
    *blocks, out_hbm, both, out_ref, sems = refs
    _, nodes, slots, _ = blocks[0].shape
    rows = nodes * slots
    me, _ = position(len(blocks) // 2)
    for d, block in enumerate(blocks):
        columns = pl.ds(pl.multiple_of((me ^ d) * LANES, LANES), LANES)
        values = block[d % 2].reshape(rows, LANES)
        high = values.astype(jnp.bfloat16)
        both[0:rows, columns] = high
        both[rows : 2 * rows, columns] = (values - high.astype(jnp.float32)).astype(jnp.bfloat16)
    width = out_ref.shape[3]
    copies = []
    for i in range(LAGS // width):
        here = slice(i * width, (i + 1) * width)
        first = jnp.dot(both[...], high_ref[:, here], preferred_element_type=jnp.float32)
        second = jnp.dot(both[0:rows, :], low_ref[:, here], preferred_element_type=jnp.float32)
        total = first[0:rows, :] + (first[rows : 2 * rows, :] + second)
        out_ref[i] = total.reshape(nodes, slots, width)
        copy = pltpu.make_async_copy(out_ref.at[i], out_hbm.at[:, :, pl.ds(i * width, width)], sems.at[i])
        copy.start()
        copies.append(copy)
    for copy in copies:
        copy.wait()


def inverse(blocks, high, low):
    _, nodes, slots, _ = blocks[0].shape
    depth = high.shape[0] * LANES
    width = 256
    vmem = pl.BlockSpec(memory_space=pltpu.VMEM)
    return pl.pallas_call(
        inverse_kernel,
        in_specs=[vmem] * (2 + len(blocks)),
        out_specs=pl.BlockSpec(memory_space=pl.ANY),
        out_shape=jax.ShapeDtypeStruct((nodes, slots, LAGS), jnp.float32),
        scratch_shapes=[
            pltpu.VMEM((2 * nodes * slots, depth), jnp.bfloat16),
            pltpu.VMEM((LAGS // width, nodes, slots, width), jnp.float32),
            pltpu.SemaphoreType.DMA((LAGS // width,)),
        ],
        compiler_params=pltpu.CompilerParams(vmem_limit_bytes=12 * MIB),
        name="inverse",
    )(high.reshape(depth, LAGS), low.reshape(depth, LAGS), *blocks)


def per_device(traces, taps, neighbours, valid, *, pairs, wins):
    windows, nodes, samples = traces.shape
    parts = 2 * wins
    place = lax.axis_index("pairs")
    win = lax.axis_index("win")

    def hop(array, d):
        pairing = [
            (i, ((i // wins) ^ (d // wins)) * wins + ((i % wins) ^ (d % wins))) for i in range(pairs * wins)
        ]
        return lax.ppermute(array, ("pairs", "win"), pairing)

    def between_chips(blocks):
        return [hop(block, 2 * s) if s else block for s, block in enumerate(blocks)]

    def within_chip(moved):
        return [x for block in moved for x in (block, hop(block, 1))]

    rows, taps = traces.reshape(windows * nodes, samples), taps.reshape(1, TAPS)
    steps = tuple(range(wins))[::-1]
    partner_rows = hop(rows, 1)
    found = own_spectra(rows, taps, nodes, steps)
    found, neighbours, valid = lax.optimization_barrier((found, neighbours, valid))

    _, is_first = position(wins)
    tile, member = neighbours // nodes, neighbours % nodes
    inside = tile // 2 == place // 2
    leading = 1 - (place // 2) % 2
    block = jnp.where(inside, jnp.where(tile % 2 == leading, 0, 1), jnp.where(is_first, 2, 3))
    code = jnp.where(valid != 0, block * nodes + member, -1)
    other = lax.ppermute(code, "pairs", [(i, i ^ 1) for i in range(pairs)])
    codes = jnp.where(is_first, jnp.concatenate([code, other], 0), jnp.concatenate([other, code], 0))
    for bit in (1 << k for k in range((wins - 1).bit_length())):
        split = codes.reshape(2 * nodes, wins // (2 * bit), 2, -1)
        codes = jnp.where(win & bit != 0, split[:, :, ::-1], split)
    codes = codes.reshape(2 * nodes, -1)
    columns = jnp.arange(8 * nodes, dtype=jnp.int32) % (4 * nodes)
    select = (codes[:, :, None] == columns[None, None, :]).astype(jnp.bfloat16)

    factor = 1.0 / math.sqrt(BINS * windows * wins)
    high, low = make_lag_tables(parts, factor)

    swap_a = [(i, i ^ 2) for i in range(pairs) if (i ^ 2) < pairs]
    swap_b = [(i, j) for i in range(2, pairs) for j in [((i - 2) ^ 2) + 2] if j < pairs]
    halves = []
    for half in range(HALVES):
        if half:
            found = own_spectra(partner_rows, taps, nodes, steps)
        blocks = between_chips([found[steps.index(s)] for s in range(wins)])
        a, b, turned = by_bin(blocks)
        halves.append((a, b, turned, lax.ppermute(a, "pairs", swap_a), lax.ppermute(b, "pairs", swap_b)))
    stack = cross_products(halves, select, wins)
    moved = between_chips(stack)
    moved[1], high, low = lax.optimization_barrier((moved[1], high, low))
    return inverse(within_chip(moved), high, low)


def solution(mesh):
    placed = (P("win", "pairs", None), P(), P("pairs", None), P("pairs", None))
    body = functools.partial(per_device, pairs=mesh.shape["pairs"], wins=mesh.shape["win"])
    return jax.shard_map(
        body, mesh=mesh, in_specs=placed, out_specs=P("pairs", "win", None), check_vma=False
    )
```

```python
import functools
import math

import jax
import jax.numpy as jnp
import numpy as np
from jax import lax
from jax.experimental import pallas as pl
from jax.experimental.pallas import tpu as pltpu
from jax.sharding import PartitionSpec as P

SAMPLES = 4096
BINS = 512
BAND = 64
LOW_BIN = 64
LAGS = 1024
TAPS = 129
LANES = 2 * BAND
EPSILON = 1e-06
STEP = 64
CHUNK = 512
HALVES = 2
PITCH = LANES + 8
MIB = 1024 * 1024
CONTRACT_LAST = (((1,), (1,)), ((), ()))


def unit_circle(products):
    angles = (products % SAMPLES).astype(np.float64) * (2.0 * math.pi / SAMPLES)
    return np.cos(angles).astype(np.float32), (-np.sin(angles)).astype(np.float32)


def banded(first, second):
    rows = first.shape[0]
    parts = [a.reshape(rows, BINS // BAND, 1, BAND) for a in (first, second)]
    return np.concatenate(parts, 2).reshape(rows, 2 * BINS)


def forward_tables():
    bins = LOW_BIN + np.arange(BINS, dtype=np.int64)
    cos, msin = unit_circle(np.arange(TAPS, dtype=np.int64)[:, None] * bins[None, :])
    fine = banded(cos, msin)
    starts = np.arange(0, SAMPLES, STEP, dtype=np.int64)
    cos, msin = unit_circle(starts[:, None] * bins[None, :])
    return fine, banded(cos, cos), banded(-msin, msin)


def lag_tables(parts):
    lags = np.arange(LAGS, dtype=np.int64) - LAGS // 2
    cos, msin = unit_circle(np.arange(BAND, dtype=np.int64)[:, None] * lags[None, :])
    first = LOW_BIN + BAND * np.arange(parts, dtype=np.int64)
    cos0, msin0 = unit_circle(first[:, None] * lags[None, :])
    return cos, msin, cos0, msin0


def position(wins):
    place = lax.axis_index("pairs")
    me = (place % 2) * wins + lax.axis_index("win")
    return me, place % 2 != (place // 2) % 2


def spectra_kernel(x_hbm, taps_ref, fine_hbm, turn_c_hbm, turn_s_hbm, *refs, steps, wins):
    outs, refs = refs[: len(steps)], refs[len(steps) :]
    x_ref, fine_ref, turn_c_ref, turn_s_ref, *refs, sems = refs
    tables, totals, stages = refs[0:2], refs[2:4], refs[4:6]
    count = x_ref.shape[0]
    nodes, windows = outs[0].shape[0], outs[0].shape[1]
    width = 2 * LANES
    pitch = stages[0].shape[1] // windows
    pieces = SAMPLES // CHUNK
    share = count // pieces
    me, _ = position(wins)
    copies = [
        pltpu.make_async_copy(source, target, sems.at[pieces + i])
        for i, (source, target) in enumerate(
            ((fine_hbm, fine_ref), (turn_c_hbm, turn_c_ref), (turn_s_hbm, turn_s_ref))
        )
    ]
    chunks = [
        pltpu.make_async_copy(
            x_hbm.at[pl.ds(i * share, share), :], x_ref.at[pl.ds(i * share, share), :], sems.at[i]
        )
        for i in range(pieces)
    ]
    for copy in copies + chunks:
        copy.start()

    def columns_of(i):
        return [pl.ds(pl.multiple_of((me ^ (2 * step)) * LANES, LANES), LANES) for step in steps[2 * i : 2 * i + 2]]

    def generate(i):
        for c, columns in enumerate(columns_of(i)):
            base = fine_ref[0:STEP, columns]
            swapped = pltpu.roll(base, BAND, 1)
            for j in range(SAMPLES // STEP):
                row = pl.ds(j, 1)
                turned = base * turn_c_ref[row, columns] + swapped * turn_s_ref[row, columns]
                tables[i % 2][j * STEP : (j + 1) * STEP, c * LANES : (c + 1) * LANES] = turned.astype(jnp.bfloat16)

    low = lax.broadcasted_iota(jnp.int32, (1, LANES), 1) < BAND
    responses = {}

    def respond(i):
        responses[i] = []
        for columns in columns_of(i):
            here = jnp.dot(
                taps_ref[:, 0:128],
                fine_ref[0:128, columns],
                precision=lax.Precision.HIGHEST,
                preferred_element_type=jnp.float32,
            )
            here = here + taps_ref[:, 128:129] * fine_ref[128:129, columns]
            other = pltpu.roll(jnp.broadcast_to(here, (8, LANES)), BAND, 1)[0:1, :]
            responses[i].append((jnp.where(low, here, other), jnp.where(low, -other, here)))

    row = lax.broadcasted_iota(jnp.int32, (width, width), 0)
    same_band = (row // LANES) == (lax.broadcasted_iota(jnp.int32, (width, width), 1) // LANES)
    summing = same_band.astype(jnp.bfloat16)

    def whiten(i):
        raw = jnp.concatenate([totals[i % 2][c] for c in range(2)], 1)
        square = raw * raw
        high = square.astype(jnp.bfloat16)
        rest = (square - high.astype(jnp.float32)).astype(jnp.bfloat16)
        sums = jnp.dot(jnp.concatenate([high, rest], 0), summing, preferred_element_type=jnp.float32)
        white = raw * lax.rsqrt((sums[0:count, :] + sums[count:, :]) * (1.0 / BAND) + EPSILON)
        for c, (same, cross) in enumerate(responses[i]):
            part = white[:, c * LANES : (c + 1) * LANES]
            turned = part * same + pltpu.roll(part, BAND, 1) * cross
            for window in range(windows):
                stages[i % 2][c, window * pitch : window * pitch + nodes, :] = turned[window * nodes : (window + 1) * nodes]

    def give(i):
        for c in range(2):
            for node in range(nodes):
                values = stages[i % 2][c, pl.ds(node, windows, stride=pitch), :]
                outs[2 * i + c][node] = values.astype(jnp.bfloat16)

    for copy in copies:
        copy.wait()
    generate(0)
    last = len(steps) // 2 - 1
    for copy in chunks:
        copy.wait()
    for i in range(len(steps) // 2):
        respond(i)
        product = jnp.dot(x_ref[...], tables[i % 2][...], preferred_element_type=jnp.float32)
        for c in range(2):
            totals[i % 2][c] = product[:, c * LANES : (c + 1) * LANES]
        if i < last:
            generate(i + 1)
        if i > 0:
            whiten(i - 1)
        if i > 1:
            give(i - 2)
    if last > 0:
        give(last - 1)
    whiten(last)
    give(last)


def own_spectra(rows, taps, nodes, steps):
    tables = [jnp.asarray(t) for t in forward_tables()]
    count = rows.shape[0]
    hbm = pl.BlockSpec(memory_space=pltpu.HBM)
    vmem = pl.BlockSpec(memory_space=pltpu.VMEM)
    shape = jax.ShapeDtypeStruct((nodes, count // nodes, LANES), jnp.bfloat16)
    return pl.pallas_call(
        functools.partial(spectra_kernel, steps=steps, wins=len(steps)),
        in_specs=[hbm, vmem, hbm, hbm, hbm],
        out_specs=[vmem] * len(steps),
        out_shape=[shape] * len(steps),
        scratch_shapes=[
            pltpu.VMEM(rows.shape, jnp.bfloat16),
            *[pltpu.VMEM(t.shape, jnp.float32) for t in tables],
            *[pltpu.VMEM((SAMPLES, 2 * LANES), jnp.bfloat16)] * 2,
            *[pltpu.VMEM((2, count, LANES), jnp.float32)] * 2,
            *[pltpu.VMEM((2, (nodes + 8) * (count // nodes), LANES), jnp.float32)] * 2,
            pltpu.SemaphoreType.DMA((SAMPLES // CHUNK + 3,)),
        ],
        compiler_params=pltpu.CompilerParams(vmem_limit_bytes=60 * MIB),
        cost_estimate=pl.CostEstimate(
            flops=2 * len(steps) * count * SAMPLES * LANES, bytes_accessed=2 * count * SAMPLES, transcendentals=0
        ),
        name="own_spectra",
    )(rows, taps, *tables)


def lag_table_kernel(cos_ref, msin_ref, cos0_ref, msin0_ref, high_ref, low_ref, *, factor):
    part = pl.program_id(0)
    c0 = cos0_ref[pl.ds(part, 1), :] * factor
    s0 = msin0_ref[pl.ds(part, 1), :] * factor
    cos, msin = cos_ref[...], msin_ref[...]
    for half, values in ((0, cos * c0 - msin * s0), (1, cos * s0 + msin * c0)):
        high = values.astype(jnp.bfloat16)
        rows = pl.ds(half * BAND, BAND)
        high_ref[0, rows, :] = high
        low_ref[0, rows, :] = (values - high.astype(jnp.float32)).astype(jnp.bfloat16)


def make_lag_tables(parts, factor):
    tables = [jnp.asarray(t) for t in lag_tables(parts)]
    shape = jax.ShapeDtypeStruct((parts, LANES, LAGS), jnp.bfloat16)
    block = pl.BlockSpec((1, LANES, LAGS), lambda i: (i, 0, 0))
    return pl.pallas_call(
        functools.partial(lag_table_kernel, factor=factor),
        grid=(parts,),
        in_specs=[pl.BlockSpec(t.shape, lambda i: (0, 0)) for t in tables],
        out_specs=[block, block],
        out_shape=[shape, shape],
        compiler_params=pltpu.CompilerParams(vmem_limit_bytes=6 * MIB),
        name="lag_tables",
    )(*tables)


def by_bin_kernel(*refs, steps):
    blocks, refs = refs[:steps], refs[steps:]
    first_ref, second_ref, turned_ref, turned, near, sem = refs
    nodes, windows = near.shape[0], near.shape[1]
    _, is_first = position(steps)
    own_at = jnp.where(is_first, 0, 1)
    copy = pltpu.make_async_copy(blocks[0], near, sem)
    copy.start()
    row = lax.broadcasted_iota(jnp.int32, (LANES, LANES), 0)
    unit = (row == lax.broadcasted_iota(jnp.int32, (LANES, LANES), 1)).astype(jnp.bfloat16)
    for tile in (1, 0):
        here = [near if s == 0 else blocks[s] for s in range(tile * steps // 2, (tile + 1) * steps // 2)]
        if tile == 0:
            copy.wait()

        def turn(node, _, here=here, tile=tile):
            values = jnp.concatenate([block[node] for block in here] * 2, 0)
            values = lax.dot_general(unit, values, CONTRACT_LAST, preferred_element_type=jnp.float32)
            turned[pl.ds(pl.multiple_of((tile * nodes + node) * PITCH, 8), LANES), :] = values
            return 0

        lax.fori_loop(0, nodes, turn, 0, unroll=16)
    left = lax.broadcasted_iota(jnp.int32, (nodes, LANES), 1) < LANES // 2
    for which, (out_ref, tile) in enumerate(((first_ref, own_at), (second_ref, 1 - own_at))):
        start = tile * (nodes * PITCH)

        def one(f, _, out_ref=out_ref, start=start, which=which):
            real = turned[pl.ds(start + f, nodes, stride=PITCH), :]
            imag = turned[pl.ds(start + BAND + f, nodes, stride=PITCH), :]
            out_ref[f] = jnp.where(left, real, imag).astype(jnp.bfloat16)
            turned_ref[f, which * nodes : (which + 1) * nodes, :] = jnp.where(left, imag, -real).astype(jnp.bfloat16)
            return 0

        lax.fori_loop(0, BAND, one, 0, unroll=64)


def by_bin(blocks):
    nodes, windows, _ = blocks[0].shape
    steps = len(blocks)
    shape = jax.ShapeDtypeStruct((BAND, nodes, LANES), jnp.bfloat16)
    vmem = pl.BlockSpec(memory_space=pltpu.VMEM)
    return pl.pallas_call(
        functools.partial(by_bin_kernel, steps=steps),
        out_shape=[shape, shape, jax.ShapeDtypeStruct((BAND, 2 * nodes, LANES), jnp.bfloat16)],
        in_specs=[pl.BlockSpec(memory_space=pl.ANY)] + [vmem] * (len(blocks) - 1),
        out_specs=[vmem] * 3,
        scratch_shapes=[
            pltpu.VMEM((2 * nodes * PITCH, LANES), jnp.float32),
            pltpu.VMEM((nodes, windows, LANES), jnp.bfloat16),
            pltpu.SemaphoreType.DMA,
        ],
        compiler_params=pltpu.CompilerParams(vmem_limit_bytes=8 * MIB),
        cost_estimate=pl.CostEstimate(flops=1 << 31, bytes_accessed=1 << 22, transcendentals=0),
        name="by_bin",
    )(*blocks)


def cross_kernel(*refs):
    halves = [refs[5 * h : 5 * h + 5] for h in range(HALVES)]
    select_ref, *outs, cross = refs[5 * HALVES :]
    nodes = halves[0][0].shape[1]
    slots = outs[0].shape[2]
    stations, count = 2 * nodes, 4 * nodes
    pitch = count + 8

    def one_bin(f, _):
        wide = lambda k: jnp.concatenate([half[k][f] for half in halves], 1)
        own = jnp.concatenate([wide(0), wide(1)], 0)
        both = jnp.concatenate([own, wide(2)], 0)
        partners = jnp.concatenate([own, wide(3), wide(4)] * 2, 0)
        cross[pl.ds(pl.multiple_of(f * pitch, 8), count), :] = lax.dot_general(
            both, partners, CONTRACT_LAST, preferred_element_type=jnp.float32
        )
        return 0

    lax.fori_loop(0, BAND, one_bin, 0, unroll=64)
    _, is_first = position(len(outs))
    own_at = jnp.where(is_first, 0, 1)
    left = lax.broadcasted_iota(jnp.int32, (2 * BAND, 2 * count), 1) < count
    tiles = (outs[: len(outs) // 2], own_at), (outs[len(outs) // 2 :], 1 - own_at)
    for shares, where in tiles:

        def one_node(node, _, shares=shares, where=where):
            index = where * nodes + node
            real = cross[pl.ds(index, BAND, stride=pitch), :]
            imag = cross[pl.ds(stations + index, BAND, stride=pitch), :]
            values = jnp.concatenate([real, imag], 0)
            high = values.astype(jnp.bfloat16).astype(jnp.float32)
            split = jnp.where(left, high, values - high).astype(jnp.bfloat16)
            picked = lax.dot_general(select_ref[index], split, CONTRACT_LAST, preferred_element_type=jnp.float32)
            for d in range(2 * len(shares)):
                shares[d // 2][d % 2, node] = picked[d * slots : (d + 1) * slots, :]
            return 0

        lax.fori_loop(0, nodes, one_node, 0, unroll=16)


def cross_products(halves, select, wins):
    nodes = halves[0][0].shape[1]
    block = jax.ShapeDtypeStruct((2, nodes, select.shape[1] // wins, LANES), jnp.float32)
    vmem = pl.BlockSpec(memory_space=pltpu.VMEM)
    operands = [x for half in halves for x in half]
    return pl.pallas_call(
        cross_kernel,
        out_shape=[block] * wins,
        in_specs=[vmem] * (len(operands) + 1),
        out_specs=[vmem] * wins,
        scratch_shapes=[pltpu.VMEM((BAND * (4 * nodes + 8), 8 * nodes), jnp.float32)],
        compiler_params=pltpu.CompilerParams(vmem_limit_bytes=12 * MIB),
        name="cross_products",
    )(*operands, select)


def inverse_kernel(high_ref, low_ref, *refs):
    *blocks, out_hbm, both, out_ref, sems = refs
    _, nodes, slots, _ = blocks[0].shape
    rows = nodes * slots
    me, _ = position(len(blocks) // 2)
    for d, block in enumerate(blocks):
        columns = pl.ds(pl.multiple_of((me ^ d) * LANES, LANES), LANES)
        values = block[d % 2].reshape(rows, LANES)
        high = values.astype(jnp.bfloat16)
        both[0:rows, columns] = high
        both[rows : 2 * rows, columns] = (values - high.astype(jnp.float32)).astype(jnp.bfloat16)
    width = out_ref.shape[3]
    copies = []
    for i in range(LAGS // width):
        here = slice(i * width, (i + 1) * width)
        first = jnp.dot(both[...], high_ref[:, here], preferred_element_type=jnp.float32)
        second = jnp.dot(both[0:rows, :], low_ref[:, here], preferred_element_type=jnp.float32)
        total = first[0:rows, :] + (first[rows : 2 * rows, :] + second)
        out_ref[i] = total.reshape(nodes, slots, width)
        copy = pltpu.make_async_copy(out_ref.at[i], out_hbm.at[:, :, pl.ds(i * width, width)], sems.at[i])
        copy.start()
        copies.append(copy)
    for copy in copies:
        copy.wait()


def inverse(blocks, high, low):
    _, nodes, slots, _ = blocks[0].shape
    depth = high.shape[0] * LANES
    width = 256
    vmem = pl.BlockSpec(memory_space=pltpu.VMEM)
    return pl.pallas_call(
        inverse_kernel,
        in_specs=[vmem] * (2 + len(blocks)),
        out_specs=pl.BlockSpec(memory_space=pl.ANY),
        out_shape=jax.ShapeDtypeStruct((nodes, slots, LAGS), jnp.float32),
        scratch_shapes=[
            pltpu.VMEM((2 * nodes * slots, depth), jnp.bfloat16),
            pltpu.VMEM((LAGS // width, nodes, slots, width), jnp.float32),
            pltpu.SemaphoreType.DMA((LAGS // width,)),
        ],
        compiler_params=pltpu.CompilerParams(vmem_limit_bytes=12 * MIB),
        name="inverse",
    )(high.reshape(depth, LAGS), low.reshape(depth, LAGS), *blocks)


def per_device(traces, taps, neighbours, valid, *, pairs, wins):
    windows, nodes, samples = traces.shape
    parts = 2 * wins
    place = lax.axis_index("pairs")
    win = lax.axis_index("win")

    def hop(array, d):
        pairing = [
            (i, ((i // wins) ^ (d // wins)) * wins + ((i % wins) ^ (d % wins))) for i in range(pairs * wins)
        ]
        return lax.ppermute(array, ("pairs", "win"), pairing)

    def between_chips(blocks):
        return [hop(block, 2 * s) if s else block for s, block in enumerate(blocks)]

    def within_chip(moved):
        return [x for block in moved for x in (block, hop(block, 1))]

    rows, taps = traces.reshape(windows * nodes, samples), taps.reshape(1, TAPS)
    steps = tuple(range(wins))[::-1]
    partner_rows = hop(rows, 1)
    found = own_spectra(rows, taps, nodes, steps)
    found, neighbours, valid = lax.optimization_barrier((found, neighbours, valid))

    _, is_first = position(wins)
    tile, member = neighbours // nodes, neighbours % nodes
    inside = tile // 2 == place // 2
    leading = 1 - (place // 2) % 2
    block = jnp.where(inside, jnp.where(tile % 2 == leading, 0, 1), jnp.where(is_first, 2, 3))
    code = jnp.where(valid != 0, block * nodes + member, -1)
    other = lax.ppermute(code, "pairs", [(i, i ^ 1) for i in range(pairs)])
    codes = jnp.where(is_first, jnp.concatenate([code, other], 0), jnp.concatenate([other, code], 0))
    for bit in (1 << k for k in range((wins - 1).bit_length())):
        split = codes.reshape(2 * nodes, wins // (2 * bit), 2, -1)
        codes = jnp.where(win & bit != 0, split[:, :, ::-1], split)
    codes = codes.reshape(2 * nodes, -1)
    columns = jnp.arange(8 * nodes, dtype=jnp.int32) % (4 * nodes)
    select = (codes[:, :, None] == columns[None, None, :]).astype(jnp.bfloat16)

    factor = 1.0 / math.sqrt(BINS * windows * wins)
    high, low = make_lag_tables(parts, factor)

    swap_a = [(i, i ^ 2) for i in range(pairs) if (i ^ 2) < pairs]
    swap_b = [(i, j) for i in range(2, pairs) for j in [((i - 2) ^ 2) + 2] if j < pairs]
    halves = []
    for half in range(HALVES):
        if half:
            found = own_spectra(partner_rows, taps, nodes, steps)
        blocks = between_chips([found[steps.index(s)] for s in range(wins)])
        a, b, turned = by_bin(blocks)
        halves.append((a, b, turned, lax.ppermute(a, "pairs", swap_a), lax.ppermute(b, "pairs", swap_b)))
    stack = cross_products(halves, select, wins)
    moved = between_chips(stack)
    moved[1], high, low = lax.optimization_barrier((moved[1], high, low))
    return inverse(within_chip(moved), high, low)


def solution(mesh):
    placed = (P("win", "pairs", None), P(), P("pairs", None), P("pairs", None))
    body = functools.partial(per_device, pairs=mesh.shape["pairs"], wins=mesh.shape["win"])
    return jax.shard_map(
        body, mesh=mesh, in_specs=placed, out_specs=P("pairs", "win", None), check_vma=False
    )
```

```python
import functools
import math

import jax
import jax.numpy as jnp
import numpy as np
from jax import lax
from jax.experimental import pallas as pl
from jax.experimental.pallas import tpu as pltpu
from jax.sharding import PartitionSpec as P

SAMPLES = 4096
BINS = 512
BAND = 64
LOW_BIN = 64
LAGS = 1024
TAPS = 129
LANES = 2 * BAND
EPSILON = 1e-06
STEP = 64
CHUNK = 512
HALVES = 2
PITCH = LANES + 8
MIB = 1024 * 1024
CONTRACT_LAST = (((1,), (1,)), ((), ()))


def unit_circle(products):
    angles = (products % SAMPLES).astype(np.float64) * (2.0 * math.pi / SAMPLES)
    return np.cos(angles).astype(np.float32), (-np.sin(angles)).astype(np.float32)


def banded(first, second):
    rows = first.shape[0]
    parts = [a.reshape(rows, BINS // BAND, 1, BAND) for a in (first, second)]
    return np.concatenate(parts, 2).reshape(rows, 2 * BINS)


def forward_tables():
    bins = LOW_BIN + np.arange(BINS, dtype=np.int64)
    cos, msin = unit_circle(np.arange(TAPS, dtype=np.int64)[:, None] * bins[None, :])
    fine = banded(cos, msin)
    starts = np.arange(0, SAMPLES, STEP, dtype=np.int64)
    cos, msin = unit_circle(starts[:, None] * bins[None, :])
    return fine, banded(cos, cos), banded(-msin, msin)


def lag_tables(parts):
    lags = np.arange(LAGS, dtype=np.int64) - LAGS // 2
    cos, msin = unit_circle(np.arange(BAND, dtype=np.int64)[:, None] * lags[None, :])
    first = LOW_BIN + BAND * np.arange(parts, dtype=np.int64)
    cos0, msin0 = unit_circle(first[:, None] * lags[None, :])
    return cos, msin, cos0, msin0


def position(wins):
    place = lax.axis_index("pairs")
    me = (place % 2) * wins + lax.axis_index("win")
    return me, place % 2 != (place // 2) % 2


def spectra_kernel(x_hbm, taps_ref, fine_hbm, turn_c_hbm, turn_s_hbm, *refs, steps, wins):
    outs, refs = refs[: len(steps)], refs[len(steps) :]
    x_ref, fine_ref, turn_c_ref, turn_s_ref, *refs, sems = refs
    tables, totals, stages = refs[0:2], refs[2:4], refs[4:6]
    count = x_ref.shape[0]
    nodes, windows = outs[0].shape[0], outs[0].shape[1]
    width = 2 * LANES
    pitch = stages[0].shape[1] // windows
    pieces = SAMPLES // CHUNK
    share = count // pieces
    me, _ = position(wins)
    copies = [
        pltpu.make_async_copy(source, target, sems.at[pieces + i])
        for i, (source, target) in enumerate(
            ((fine_hbm, fine_ref), (turn_c_hbm, turn_c_ref), (turn_s_hbm, turn_s_ref))
        )
    ]
    chunks = [
        pltpu.make_async_copy(
            x_hbm.at[pl.ds(i * share, share), :], x_ref.at[pl.ds(i * share, share), :], sems.at[i]
        )
        for i in range(pieces)
    ]
    for copy in copies + chunks:
        copy.start()

    def columns_of(i):
        return [pl.ds(pl.multiple_of((me ^ (2 * step)) * LANES, LANES), LANES) for step in steps[2 * i : 2 * i + 2]]

    def generate(i):
        for c, columns in enumerate(columns_of(i)):
            base = fine_ref[0:STEP, columns]
            swapped = pltpu.roll(base, BAND, 1)
            for j in range(SAMPLES // STEP):
                row = pl.ds(j, 1)
                turned = base * turn_c_ref[row, columns] + swapped * turn_s_ref[row, columns]
                tables[i % 2][j * STEP : (j + 1) * STEP, c * LANES : (c + 1) * LANES] = turned.astype(jnp.bfloat16)

    low = lax.broadcasted_iota(jnp.int32, (1, LANES), 1) < BAND
    responses = {}

    def respond(i):
        responses[i] = []
        for columns in columns_of(i):
            here = jnp.dot(
                taps_ref[:, 0:128],
                fine_ref[0:128, columns],
                precision=lax.Precision.HIGHEST,
                preferred_element_type=jnp.float32,
            )
            here = here + taps_ref[:, 128:129] * fine_ref[128:129, columns]
            other = pltpu.roll(jnp.broadcast_to(here, (8, LANES)), BAND, 1)[0:1, :]
            responses[i].append((jnp.where(low, here, other), jnp.where(low, -other, here)))

    row = lax.broadcasted_iota(jnp.int32, (width, width), 0)
    same_band = (row // LANES) == (lax.broadcasted_iota(jnp.int32, (width, width), 1) // LANES)
    summing = same_band.astype(jnp.bfloat16)

    def whiten(i):
        raw = jnp.concatenate([totals[i % 2][c] for c in range(2)], 1)
        square = raw * raw
        high = square.astype(jnp.bfloat16)
        rest = (square - high.astype(jnp.float32)).astype(jnp.bfloat16)
        sums = jnp.dot(jnp.concatenate([high, rest], 0), summing, preferred_element_type=jnp.float32)
        white = raw * lax.rsqrt((sums[0:count, :] + sums[count:, :]) * (1.0 / BAND) + EPSILON)
        for c, (same, cross) in enumerate(responses[i]):
            part = white[:, c * LANES : (c + 1) * LANES]
            turned = part * same + pltpu.roll(part, BAND, 1) * cross
            for window in range(windows):
                stages[i % 2][c, window * pitch : window * pitch + nodes, :] = turned[window * nodes : (window + 1) * nodes]

    def give(i):
        for c in range(2):
            for node in range(nodes):
                values = stages[i % 2][c, pl.ds(node, windows, stride=pitch), :]
                outs[2 * i + c][node] = values.astype(jnp.bfloat16)

    for copy in copies:
        copy.wait()
    generate(0)
    last = len(steps) // 2 - 1
    for copy in chunks:
        copy.wait()
    for i in range(len(steps) // 2):
        respond(i)
        product = jnp.dot(x_ref[...], tables[i % 2][...], preferred_element_type=jnp.float32)
        for c in range(2):
            totals[i % 2][c] = product[:, c * LANES : (c + 1) * LANES]
        if i < last:
            generate(i + 1)
        if i > 0:
            whiten(i - 1)
        if i > 1:
            give(i - 2)
    if last > 0:
        give(last - 1)
    whiten(last)
    give(last)


def own_spectra(rows, taps, nodes, steps):
    tables = [jnp.asarray(t) for t in forward_tables()]
    count = rows.shape[0]
    hbm = pl.BlockSpec(memory_space=pltpu.HBM)
    vmem = pl.BlockSpec(memory_space=pltpu.VMEM)
    shape = jax.ShapeDtypeStruct((nodes, count // nodes, LANES), jnp.bfloat16)
    return pl.pallas_call(
        functools.partial(spectra_kernel, steps=steps, wins=len(steps)),
        in_specs=[hbm, vmem, hbm, hbm, hbm],
        out_specs=[vmem] * len(steps),
        out_shape=[shape] * len(steps),
        scratch_shapes=[
            pltpu.VMEM(rows.shape, jnp.bfloat16),
            *[pltpu.VMEM(t.shape, jnp.float32) for t in tables],
            *[pltpu.VMEM((SAMPLES, 2 * LANES), jnp.bfloat16)] * 2,
            *[pltpu.VMEM((2, count, LANES), jnp.float32)] * 2,
            *[pltpu.VMEM((2, (nodes + 8) * (count // nodes), LANES), jnp.float32)] * 2,
            pltpu.SemaphoreType.DMA((SAMPLES // CHUNK + 3,)),
        ],
        compiler_params=pltpu.CompilerParams(vmem_limit_bytes=60 * MIB),
        cost_estimate=pl.CostEstimate(
            flops=2 * len(steps) * count * SAMPLES * LANES, bytes_accessed=2 * count * SAMPLES, transcendentals=0
        ),
        name="own_spectra",
    )(rows, taps, *tables)


def lag_table_kernel(cos_ref, msin_ref, cos0_ref, msin0_ref, high_ref, low_ref, *, factor):
    part = pl.program_id(0)
    c0 = cos0_ref[pl.ds(part, 1), :] * factor
    s0 = msin0_ref[pl.ds(part, 1), :] * factor
    cos, msin = cos_ref[...], msin_ref[...]
    for half, values in ((0, cos * c0 - msin * s0), (1, cos * s0 + msin * c0)):
        high = values.astype(jnp.bfloat16)
        rows = pl.ds(half * BAND, BAND)
        high_ref[0, rows, :] = high
        low_ref[0, rows, :] = (values - high.astype(jnp.float32)).astype(jnp.bfloat16)


def make_lag_tables(parts, factor):
    tables = [jnp.asarray(t) for t in lag_tables(parts)]
    shape = jax.ShapeDtypeStruct((parts, LANES, LAGS), jnp.bfloat16)
    block = pl.BlockSpec((1, LANES, LAGS), lambda i: (i, 0, 0))
    return pl.pallas_call(
        functools.partial(lag_table_kernel, factor=factor),
        grid=(parts,),
        in_specs=[pl.BlockSpec(t.shape, lambda i: (0, 0)) for t in tables],
        out_specs=[block, block],
        out_shape=[shape, shape],
        compiler_params=pltpu.CompilerParams(vmem_limit_bytes=6 * MIB),
        name="lag_tables",
    )(*tables)


def by_bin_kernel(*refs, steps):
    blocks, refs = refs[:steps], refs[steps:]
    first_ref, second_ref, turned_ref, turned, near, sem = refs
    nodes, windows = near.shape[0], near.shape[1]
    _, is_first = position(steps)
    own_at = jnp.where(is_first, 0, 1)
    copy = pltpu.make_async_copy(blocks[0], near, sem)
    copy.start()
    row = lax.broadcasted_iota(jnp.int32, (LANES, LANES), 0)
    unit = (row == lax.broadcasted_iota(jnp.int32, (LANES, LANES), 1)).astype(jnp.bfloat16)
    for tile in (1, 0):
        here = [near if s == 0 else blocks[s] for s in range(tile * steps // 2, (tile + 1) * steps // 2)]
        if tile == 0:
            copy.wait()

        def turn(node, _, here=here, tile=tile):
            values = jnp.concatenate([block[node] for block in here] * 2, 0)
            values = lax.dot_general(unit, values, CONTRACT_LAST, preferred_element_type=jnp.float32)
            turned[pl.ds(pl.multiple_of((tile * nodes + node) * PITCH, 8), LANES), :] = values
            return 0

        lax.fori_loop(0, nodes, turn, 0, unroll=16)
    left = lax.broadcasted_iota(jnp.int32, (nodes, LANES), 1) < LANES // 2
    for which, (out_ref, tile) in enumerate(((first_ref, own_at), (second_ref, 1 - own_at))):
        start = tile * (nodes * PITCH)

        def one(f, _, out_ref=out_ref, start=start, which=which):
            real = turned[pl.ds(start + f, nodes, stride=PITCH), :]
            imag = turned[pl.ds(start + BAND + f, nodes, stride=PITCH), :]
            out_ref[f] = jnp.where(left, real, imag).astype(jnp.bfloat16)
            turned_ref[f, which * nodes : (which + 1) * nodes, :] = jnp.where(left, imag, -real).astype(jnp.bfloat16)
            return 0

        lax.fori_loop(0, BAND, one, 0, unroll=64)


def by_bin(blocks):
    nodes, windows, _ = blocks[0].shape
    steps = len(blocks)
    shape = jax.ShapeDtypeStruct((BAND, nodes, LANES), jnp.bfloat16)
    vmem = pl.BlockSpec(memory_space=pltpu.VMEM)
    return pl.pallas_call(
        functools.partial(by_bin_kernel, steps=steps),
        out_shape=[shape, shape, jax.ShapeDtypeStruct((BAND, 2 * nodes, LANES), jnp.bfloat16)],
        in_specs=[pl.BlockSpec(memory_space=pl.ANY)] + [vmem] * (len(blocks) - 1),
        out_specs=[vmem] * 3,
        scratch_shapes=[
            pltpu.VMEM((2 * nodes * PITCH, LANES), jnp.float32),
            pltpu.VMEM((nodes, windows, LANES), jnp.bfloat16),
            pltpu.SemaphoreType.DMA,
        ],
        compiler_params=pltpu.CompilerParams(vmem_limit_bytes=8 * MIB),
        cost_estimate=pl.CostEstimate(flops=1 << 31, bytes_accessed=1 << 22, transcendentals=0),
        name="by_bin",
    )(*blocks)


def cross_kernel(*refs):
    halves = [refs[5 * h : 5 * h + 5] for h in range(HALVES)]
    select_ref, *outs, cross = refs[5 * HALVES :]
    nodes = halves[0][0].shape[1]
    slots = outs[0].shape[2]
    stations, count = 2 * nodes, 4 * nodes
    pitch = count + 8

    def one_bin(f, _):
        wide = lambda k: jnp.concatenate([half[k][f] for half in halves], 1)
        own = jnp.concatenate([wide(0), wide(1)], 0)
        both = jnp.concatenate([own, wide(2)], 0)
        partners = jnp.concatenate([own, wide(3), wide(4)] * 2, 0)
        cross[pl.ds(pl.multiple_of(f * pitch, 8), count), :] = lax.dot_general(
            both, partners, CONTRACT_LAST, preferred_element_type=jnp.float32
        )
        return 0

    lax.fori_loop(0, BAND, one_bin, 0, unroll=64)
    _, is_first = position(len(outs))
    own_at = jnp.where(is_first, 0, 1)
    left = lax.broadcasted_iota(jnp.int32, (2 * BAND, 2 * count), 1) < count
    tiles = (outs[: len(outs) // 2], own_at), (outs[len(outs) // 2 :], 1 - own_at)
    for shares, where in tiles:

        def one_node(node, _, shares=shares, where=where):
            index = where * nodes + node
            real = cross[pl.ds(index, BAND, stride=pitch), :]
            imag = cross[pl.ds(stations + index, BAND, stride=pitch), :]
            values = jnp.concatenate([real, imag], 0)
            high = values.astype(jnp.bfloat16).astype(jnp.float32)
            split = jnp.where(left, high, values - high).astype(jnp.bfloat16)
            picked = lax.dot_general(select_ref[index], split, CONTRACT_LAST, preferred_element_type=jnp.float32)
            for d in range(2 * len(shares)):
                shares[d // 2][d % 2, node] = picked[d * slots : (d + 1) * slots, :]
            return 0

        lax.fori_loop(0, nodes, one_node, 0, unroll=16)


def cross_products(halves, select, wins):
    nodes = halves[0][0].shape[1]
    block = jax.ShapeDtypeStruct((2, nodes, select.shape[1] // wins, LANES), jnp.float32)
    vmem = pl.BlockSpec(memory_space=pltpu.VMEM)
    operands = [x for half in halves for x in half]
    return pl.pallas_call(
        cross_kernel,
        out_shape=[block] * wins,
        in_specs=[vmem] * (len(operands) + 1),
        out_specs=[vmem] * wins,
        scratch_shapes=[pltpu.VMEM((BAND * (4 * nodes + 8), 8 * nodes), jnp.float32)],
        compiler_params=pltpu.CompilerParams(vmem_limit_bytes=12 * MIB),
        name="cross_products",
    )(*operands, select)


def inverse_kernel(high_ref, low_ref, *refs):
    *blocks, out_hbm, both, out_ref, sems = refs
    blocks = blocks[::-1]
    _, nodes, slots, _ = blocks[0].shape
    rows = nodes * slots
    me, _ = position(len(blocks) // 2)
    for d, block in enumerate(blocks):
        columns = pl.ds(pl.multiple_of((me ^ d) * LANES, LANES), LANES)
        values = block[d % 2].reshape(rows, LANES)
        high = values.astype(jnp.bfloat16)
        both[0:rows, columns] = high
        both[rows : 2 * rows, columns] = (values - high.astype(jnp.float32)).astype(jnp.bfloat16)
    width = out_ref.shape[3]
    copies = []
    for i in range(LAGS // width):
        here = slice(i * width, (i + 1) * width)
        first = jnp.dot(both[...], high_ref[:, here], preferred_element_type=jnp.float32)
        second = jnp.dot(both[0:rows, :], low_ref[:, here], preferred_element_type=jnp.float32)
        total = first[0:rows, :] + (first[rows : 2 * rows, :] + second)
        out_ref[i] = total.reshape(nodes, slots, width)
        copy = pltpu.make_async_copy(out_ref.at[i], out_hbm.at[:, :, pl.ds(i * width, width)], sems.at[i])
        copy.start()
        copies.append(copy)
    for copy in copies:
        copy.wait()


def inverse(blocks, high, low):
    _, nodes, slots, _ = blocks[0].shape
    depth = high.shape[0] * LANES
    width = 256
    vmem = pl.BlockSpec(memory_space=pltpu.VMEM)
    return pl.pallas_call(
        inverse_kernel,
        in_specs=[vmem] * (2 + len(blocks)),
        out_specs=pl.BlockSpec(memory_space=pl.ANY),
        out_shape=jax.ShapeDtypeStruct((nodes, slots, LAGS), jnp.float32),
        scratch_shapes=[
            pltpu.VMEM((2 * nodes * slots, depth), jnp.bfloat16),
            pltpu.VMEM((LAGS // width, nodes, slots, width), jnp.float32),
            pltpu.SemaphoreType.DMA((LAGS // width,)),
        ],
        compiler_params=pltpu.CompilerParams(vmem_limit_bytes=12 * MIB),
        name="inverse",
    )(high.reshape(depth, LAGS), low.reshape(depth, LAGS), *blocks)


def per_device(traces, taps, neighbours, valid, *, pairs, wins):
    windows, nodes, samples = traces.shape
    parts = 2 * wins
    place = lax.axis_index("pairs")
    win = lax.axis_index("win")

    def hop(array, d):
        pairing = [
            (i, ((i // wins) ^ (d // wins)) * wins + ((i % wins) ^ (d % wins))) for i in range(pairs * wins)
        ]
        return lax.ppermute(array, ("pairs", "win"), pairing)

    def between_chips(blocks):
        return [hop(block, 2 * s) if s else block for s, block in enumerate(blocks)]

    def within_chip(moved):
        return [x for block in moved for x in (block, hop(block, 1))]

    rows, taps = traces.reshape(windows * nodes, samples), taps.reshape(1, TAPS)
    steps = tuple(range(wins))[::-1]
    partner_rows = hop(rows, 1)
    found = own_spectra(rows, taps, nodes, steps)
    found, neighbours, valid = lax.optimization_barrier((found, neighbours, valid))

    _, is_first = position(wins)
    tile, member = neighbours // nodes, neighbours % nodes
    inside = tile // 2 == place // 2
    leading = 1 - (place // 2) % 2
    block = jnp.where(inside, jnp.where(tile % 2 == leading, 0, 1), jnp.where(is_first, 2, 3))
    code = jnp.where(valid != 0, block * nodes + member, -1)
    other = lax.ppermute(code, "pairs", [(i, i ^ 1) for i in range(pairs)])
    codes = jnp.where(is_first, jnp.concatenate([code, other], 0), jnp.concatenate([other, code], 0))
    for bit in (1 << k for k in range((wins - 1).bit_length())):
        split = codes.reshape(2 * nodes, wins // (2 * bit), 2, -1)
        codes = jnp.where(win & bit != 0, split[:, :, ::-1], split)
    codes = codes.reshape(2 * nodes, -1)
    columns = jnp.arange(8 * nodes, dtype=jnp.int32) % (4 * nodes)
    select = (codes[:, :, None] == columns[None, None, :]).astype(jnp.bfloat16)

    factor = 1.0 / math.sqrt(BINS * windows * wins)
    high, low = make_lag_tables(parts, factor)

    swap_a = [(i, i ^ 2) for i in range(pairs) if (i ^ 2) < pairs]
    swap_b = [(i, j) for i in range(2, pairs) for j in [((i - 2) ^ 2) + 2] if j < pairs]
    halves = []
    for half in range(HALVES):
        if half:
            found = own_spectra(partner_rows, taps, nodes, steps)
        blocks = between_chips([found[steps.index(s)] for s in range(wins)])
        a, b, turned = by_bin(blocks)
        halves.append((a, b, turned, lax.ppermute(a, "pairs", swap_a), lax.ppermute(b, "pairs", swap_b)))
    stack = cross_products(halves, select, wins)
    moved = between_chips(stack)
    moved[-1], high, low = lax.optimization_barrier((moved[-1], high, low))
    return inverse(within_chip(moved)[::-1], high, low)


def solution(mesh):
    placed = (P("win", "pairs", None), P(), P("pairs", None), P("pairs", None))
    body = functools.partial(per_device, pairs=mesh.shape["pairs"], wins=mesh.shape["win"])
    return jax.shard_map(
        body, mesh=mesh, in_specs=placed, out_specs=P("pairs", "win", None), check_vma=False
    )
```
